32 devices in a mesh: grp: 2 (over y), seq: 4 (over z), head: 2 (over x), clip: 2 (over core).
Axes of the slice: x: 2, y: 2, z: 4, core: 2. Of those that a mesh axis runs over, the one named last changes fastest.
Arguments:
- query_states: bfloat16 [4, 2048, 1536], P(('grp', 'clip'), 'seq', 'head'), parts along dimension 0, may hold values from -64 to 64
- key_states: bfloat16 [4, 2048, 1536], P(('grp', 'clip'), 'seq', 'head'), parts along dimension 0, may hold values from -4 to 4
- value_states: bfloat16 [4, 2048, 1536], P(('grp', 'clip'), 'seq', 'head'), parts along dimension 0, may hold values from -5 to 5
- output_grad: bfloat16 [4, 2048, 3072], P(('grp', 'clip'), 'seq', 'head'), parts along dimension 0, may hold values from -48 to 48
- w_out: bfloat16 [1536, 3072], P('head'), may hold values from -0.15625 to 0.15625
- key_list: int32 [4, 8, 8], P(('grp', 'clip')), parts along dimension 0, may hold values from 0 to 7, as said below
- key_count: int32 [4, 8], P(('grp', 'clip')), parts along dimension 0, may hold values from 1 to 8, as said below
Outputs:
- query_grad: bfloat16 [4, 2048, 1536], P(('grp', 'clip'), 'seq', 'head'), parts along dimension 0
- key_grad: bfloat16 [4, 2048, 1536], P(('grp', 'clip'), 'seq', 'head'), parts along dimension 0
- value_grad: bfloat16 [4, 2048, 1536], P(('grp', 'clip'), 'seq', 'head'), parts along dimension 0
- grad_features: float32 [4, 12, 3], P(('grp', 'clip'), 'head'), parts along dimension 0
The draws below stay inside these ranges and needn't reach their ends.
There are 2 independent parts, one for each index of `grp`. The reference program is written for one: setup_inputs(seed, part) draws one part's arguments, and reference() takes and returns one part's arrays. A program takes and returns all parts, laid end to end along the dimension named above; an argument that names none is the same for every part. Nothing has to cross between parts.
Inputs may be any that keep to these rules, and one draw needn't show every extreme that they name: Tile i lies in frame block i // 4 at place i % 4. For each clip and query tile i the first key_count entries of key_list are distinct key tiles in ascending order, among them i itself, each at a place within 2 of i's place, in i's frame block or in the other one; the remaining entries equal i. `key_count`: in every draw some query tile lists 8 key tiles.
All inputs are finite; a program needn't handle non-finite values.
Results may differ from the reference program's by a relative error of at most 0.035.
Values may be sent and summed in bfloat16 or wider, within the bound.
No kernel may reach another device: no remote copies, remote signals or barrier semaphores. Data moves between devices by JAX's collectives and lax.ppermute only.
A program may use at most 128 MiB of HBM per device.

```python
import jax
import jax.numpy as jnp
from jax import lax

D = 3072
HEADS = 12
HD = 128
TILE = 256
RADIUS = 2
CLIPS = 2
TILES_DEV = 2
TILES = 8
SPATIAL = 4
TOKENS = 2048
KMAX = 8
N_SEQ = 4


def window_tables(key):
    full_clip = jax.random.randint(jax.random.fold_in(key, 11), (), 0, CLIPS)
    place_radius = jax.random.randint(jax.random.fold_in(key, 12), (CLIPS,), 1, RADIUS + 1)
    time_radius = jax.random.randint(jax.random.fold_in(key, 13), (CLIPS,), 0, 2)
    is_full = jnp.arange(CLIPS) == full_clip
    place_radius = jnp.where(is_full, RADIUS, place_radius)
    time_radius = jnp.where(is_full, 1, time_radius)
    width = min(2 * RADIUS + 1, SPATIAL)
    tile_ids = jnp.arange(TILES)
    tile_frame = tile_ids // SPATIAL
    tile_place = tile_ids % SPATIAL
    slot_ids = jnp.arange(KMAX)
    slot_frame = slot_ids // width
    slot_step = slot_ids % width
    window_start = jnp.clip(tile_place - RADIUS, 0, SPATIAL - width)
    cand_place = window_start[:, None] + slot_step[None, :]
    candidate = slot_frame[None, :] * SPATIAL + cand_place
    same_frame = slot_frame[None, :] == tile_frame[:, None]
    all_lists = []
    all_counts = []
    for clip_idx in range(CLIPS):
        near_place = jnp.abs(cand_place - tile_place[:, None]) <= place_radius[clip_idx]
        near_time = same_frame | (time_radius[clip_idx] == 1)
        valid = near_place & near_time
        order_key = jnp.where(valid, 0, KMAX) + slot_ids[None, :]
        order = jnp.argsort(order_key, axis=1, stable=True)
        sorted_cand = jnp.take_along_axis(candidate, order, axis=1)
        sorted_valid = jnp.take_along_axis(valid, order, axis=1)
        all_lists.append(jnp.where(sorted_valid, sorted_cand, tile_ids[:, None]).astype(jnp.int32))
        all_counts.append(jnp.sum(valid.astype(jnp.int32), axis=1).astype(jnp.int32))
    return (jnp.stack(all_lists), jnp.stack(all_counts))


def draw_key_list(key, part):
    return window_tables(key)[0]


def draw_key_count(key, part):
    return window_tables(key)[1]


def drawn_pair(key):
    shape = (CLIPS, TOKENS, HEADS * HD)
    keys_out = jax.random.truncated_normal(jax.random.fold_in(key, 21), -4.0, 4.0, shape, jnp.float32)
    queries = jax.random.truncated_normal(jax.random.fold_in(key, 22), -4.0, 4.0, shape, jnp.float32)
    return (queries, keys_out)


def draw_query_states(key, part):
    return drawn_pair(key)[0].astype(jnp.bfloat16)


def draw_key_states(key, part):
    return drawn_pair(key)[1].astype(jnp.bfloat16)


def draw_output_grad(key, part):
    shape = (CLIPS, TOKENS, D)
    position = jnp.arange(TOKENS).astype(jnp.float32) / TOKENS
    col_scale = jnp.exp(jax.random.uniform(jax.random.fold_in(key, 33), (D,), jnp.float32, jnp.log(0.5), jnp.log(2.0)))
    noise = jax.random.truncated_normal(jax.random.fold_in(key, 31), -4.0, 4.0, shape, jnp.float32)
    rise = jnp.exp(jnp.log(3.0) * (position - 0.5))
    row_scale = jnp.exp(jax.random.uniform(jax.random.fold_in(key, 34), (CLIPS, TOKENS), jnp.float32, jnp.log(0.3), jnp.log(3.0)))
    return (noise * (rise[None, :] * row_scale)[:, :, None] * col_scale[None, None, :]).astype(jnp.bfloat16)


def levels(key, shape, cuts, smallest, top_value):
    def one(dim, blocks):
        draws = jax.random.uniform(jax.random.fold_in(jax.random.fold_in(key, 6), dim), (blocks,), jnp.float32, smallest / len(cuts), top_value / len(cuts))
        return jnp.repeat(jnp.exp(draws), shape[dim] // blocks).reshape((-1,) + (1,) * (len(shape) - dim - 1))

    factor_of = one(*cuts[0])
    for cut in cuts[1:]:
        factor_of = factor_of * one(*cut)
    return factor_of


def scatter_about(key, extent, spread, bound, shards=(), kind=jnp.bfloat16):
    entries = spread * jax.random.normal(key, extent, jnp.float32)
    if shards:
        entries = entries * levels(key, extent, shards, -0.22, 0.18)
    return jnp.clip(entries, -bound, bound).astype(kind)


def setup_inputs(seed: int = 0, part: int = 0) -> dict:
    arg_keys = jax.random.split(jax.random.key(seed), 8)
    own_keys = jax.random.split(jax.random.fold_in(arg_keys[7], part), 8)
    query_states = draw_query_states(jax.random.fold_in(jax.random.fold_in(arg_keys[7], part), 71), part)
    key_states = draw_key_states(jax.random.fold_in(jax.random.fold_in(arg_keys[7], part), 71), part)
    value_states = scatter_about(own_keys[2], (CLIPS, TOKENS, HEADS * HD), 1.0, 5.0, ((0, 2), (1, 4), (2, 2)))
    output_grad = draw_output_grad(jax.random.fold_in(jax.random.fold_in(arg_keys[7], part), 71), part)
    w_out = scatter_about(arg_keys[4], (HEADS * HD, D), (HEADS * HD) ** -0.5, 0.15625, ((0, 2),))
    key_list = draw_key_list(jax.random.fold_in(jax.random.fold_in(arg_keys[7], part), 71), part)
    key_count = draw_key_count(jax.random.fold_in(jax.random.fold_in(arg_keys[7], part), 71), part)
    return {"query_states": query_states, "key_states": key_states, "value_states": value_states, "output_grad": output_grad, "w_out": w_out, "key_list": key_list, "key_count": key_count}


def rounded(values):
    return lax.optimization_barrier(values.astype(jnp.bfloat16)).astype(jnp.float32)


def tile_terms(query_tile, key_tiles, value_tiles, grad_tile, tile_list, tile_count):
    score_scale = HD ** -0.5
    key_rows = key_tiles[tile_list].reshape(KMAX * TILE, HEADS, HD).astype(jnp.float32)
    value_rows = value_tiles[tile_list].reshape(KMAX * TILE, HEADS, HD).astype(jnp.float32)
    query_rows = query_tile.astype(jnp.float32)
    grad_rows = grad_tile.astype(jnp.float32)
    allowed = (jnp.arange(KMAX * TILE) // TILE) < tile_count
    scores = jnp.einsum("qhe,khe->hqk", query_rows, key_rows) * score_scale
    scores = jnp.where(allowed[None, None, :], scores, -jnp.inf)
    row_max = jnp.max(scores, axis=-1, keepdims=True)
    log_norm = row_max + jnp.log(jnp.sum(jnp.exp(scores - row_max), axis=-1, keepdims=True))
    weights = jnp.exp(scores - log_norm)
    weights_b = rounded(weights)
    attn_out = rounded(jnp.einsum("hqk,khe->qhe", weights_b, value_rows))
    row_delta = jnp.sum(grad_rows * attn_out, axis=-1)
    dprob = jnp.einsum("qhe,khe->hqk", grad_rows, value_rows)
    dscore = rounded(weights * (dprob - jnp.transpose(row_delta)[:, :, None]))
    query_full = score_scale * jnp.einsum("hqk,khe->qhe", dscore, key_rows)
    key_terms = score_scale * jnp.einsum("hqk,qhe->khe", dscore, query_rows)
    value_terms = jnp.einsum("hqk,qhe->khe", weights_b, grad_rows)
    return query_full, key_terms.reshape(KMAX, TILE, HEADS, HD), value_terms.reshape(KMAX, TILE, HEADS, HD)


def clip_grads(queries, keys_in, values_in, grads, lists, counts):
    key_tiles = keys_in.reshape(TILES, TILE, HEADS, HD)
    value_tiles = values_in.reshape(TILES, TILE, HEADS, HD)
    query_blocks = queries.reshape(N_SEQ, TILES_DEV, TILE, HEADS, HD)
    grad_blocks = grads.reshape(N_SEQ, TILES_DEV, TILE, HEADS, HD)
    list_blocks = lists.reshape(N_SEQ, TILES_DEV, KMAX)
    count_blocks = counts.reshape(N_SEQ, TILES_DEV)

    def block_step(carried, inputs):
        key_acc, value_acc = carried
        query_block, grad_block, list_block, count_block = inputs
        query_full, key_terms, value_terms = jax.vmap(tile_terms, in_axes=(0, None, None, 0, 0, 0))(
            query_block, key_tiles, value_tiles, grad_block, list_block, count_block)
        live_slot = (jnp.arange(KMAX)[None, :] < count_block[:, None]).astype(jnp.float32)[:, :, None, None, None]
        flat_list = list_block.reshape(-1)
        zero_tiles = jnp.zeros((TILES, TILE, HEADS, HD), jnp.float32)
        key_part = zero_tiles.at[flat_list].add((key_terms * live_slot).reshape(-1, TILE, HEADS, HD))
        value_part = zero_tiles.at[flat_list].add((value_terms * live_slot).reshape(-1, TILE, HEADS, HD))
        return (key_acc + rounded(key_part), value_acc + rounded(value_part)), query_full

    start_acc = jnp.zeros((TILES, TILE, HEADS, HD), jnp.float32)
    (key_full, value_full), query_full = lax.scan(
        block_step, (start_acc, start_acc), (query_blocks, grad_blocks, list_blocks, count_blocks))
    return (query_full.reshape(TOKENS, HEADS, HD), key_full.reshape(TOKENS, HEADS, HD),
            value_full.reshape(TOKENS, HEADS, HD))


def reference(query_states, key_states, value_states, output_grad, w_out, key_list, key_count):
    query_outs = []
    key_outs = []
    value_outs = []
    feature_outs = []
    for clip_idx in range(CLIPS):
        grad_out = jnp.dot(output_grad[clip_idx], jnp.transpose(w_out), preferred_element_type=jnp.float32)
        grad_out = grad_out.astype(jnp.bfloat16).reshape(TOKENS, HEADS, HD)
        query_full, key_full, value_full = clip_grads(
            query_states[clip_idx].reshape(TOKENS, HEADS, HD), key_states[clip_idx].reshape(TOKENS, HEADS, HD),
            value_states[clip_idx].reshape(TOKENS, HEADS, HD), grad_out, key_list[clip_idx], key_count[clip_idx])
        features = jnp.stack([jnp.log(jnp.mean(grads_full * grads_full, axis=(0, 2)) + 1e-6)
                              for grads_full in (query_full, key_full, value_full)], axis=-1)
        query_outs.append(query_full.reshape(TOKENS, HEADS * HD).astype(jnp.bfloat16))
        key_outs.append(key_full.reshape(TOKENS, HEADS * HD).astype(jnp.bfloat16))
        value_outs.append(value_full.reshape(TOKENS, HEADS * HD).astype(jnp.bfloat16))
        feature_outs.append(features)
    return (jnp.stack(query_outs), jnp.stack(key_outs), jnp.stack(value_outs), jnp.stack(feature_outs))
```

```python
import functools
import math

import jax
import jax.numpy as jnp
from jax import lax
from jax.experimental import pallas as pl
from jax.experimental.pallas import tpu as pltpu
from jax.sharding import PartitionSpec as P

HD = 128
TILE = 256
STAT_ROWS = 16
SMEM = pl.BlockSpec(memory_space=pltpu.SMEM)
VMEM = pl.BlockSpec(memory_space=pltpu.VMEM)
ANY = pl.BlockSpec(memory_space=pl.ANY)
NT = (((1,), (1,)), ((), ()))
NN = (((1,), (0,)), ((), ()))


def mm(lhs, rhs, dims):
    return lax.dot_general(lhs, rhs, dims, preferred_element_type=jnp.float32)


def pack_kernel(heads_ref, q_ref, k_ref, v_ref, *outs):
    for slot, out in enumerate(outs):
        cols = pl.ds(pl.multiple_of(heads_ref[slot] * HD, HD), HD)
        out[0] = q_ref[:, cols]
        out[1] = k_ref[:, cols]
        out[2] = v_ref[:, cols]


def pack(heads, query, key, value):
    rows = query.shape[0]
    slots = heads.shape[0]
    return pl.pallas_call(
        pack_kernel,
        out_shape=[jax.ShapeDtypeStruct((3, rows, HD), query.dtype)] * slots,
        in_specs=[SMEM, VMEM, VMEM, VMEM],
        out_specs=[VMEM] * slots,
        cost_estimate=pl.CostEstimate(
            flops=0, transcendentals=0, bytes_accessed=6 * (query.size + slots * rows * HD)
        ),
        name="pack_heads",
    )(heads, query, key, value)


def project_kernel(has_acc, slots, heads_ref, src_ref, *refs):
    refs = list(refs)
    grad_ref, w_even, w_odd = refs[:3]
    weights = jnp.concatenate([w_even[...], w_odd[...]], axis=0)
    total = mm(grad_ref[...], weights, NT)
    if has_acc:
        total = total + refs[3][0]
        outs = refs[4:]
        for slot in range(slots):
            @pl.when(pl.program_id(0) == slot // 2)
            def _():
                half = slot % 2
                outs[slot][...] = total[:, half * HD : (half + 1) * HD].astype(jnp.bfloat16)
    else:
        refs[3][0] = total


def project(heads, src, grads, w_out, acc, last):
    rows, feats = grads.shape
    slots = heads.shape[0]
    steps = slots // 2
    in_specs = [
        pl.BlockSpec((rows, feats), lambda s, heads, src: (0, 0)),
        pl.BlockSpec((HD, feats), lambda s, heads, src: (heads[2 * s], src[0])),
        pl.BlockSpec((HD, feats), lambda s, heads, src: (heads[2 * s + 1], src[0])),
    ]
    args = [grads, w_out, w_out]
    acc_spec = pl.BlockSpec((1, rows, 2 * HD), lambda s, heads, src: (s, 0, 0))
    if acc is not None:
        in_specs.append(acc_spec)
        args.append(acc)
    if last:
        out_shape = [jax.ShapeDtypeStruct((rows, HD), jnp.bfloat16)] * slots
        out_specs = [pl.BlockSpec((rows, HD), lambda s, heads, src: (0, 0))] * slots
    else:
        out_shape = jax.ShapeDtypeStruct((steps, rows, 2 * HD), jnp.float32)
        out_specs = acc_spec
    return pl.pallas_call(
        functools.partial(project_kernel, last, slots),
        out_shape=out_shape,
        grid_spec=pltpu.PrefetchScalarGridSpec(
            num_scalar_prefetch=2, grid=(steps,), in_specs=in_specs, out_specs=out_specs
        ),
        cost_estimate=pl.CostEstimate(
            flops=2 * rows * feats * slots * HD,
            transcendentals=0,
            bytes_accessed=2 * (grads.size + slots * HD * feats) + 6 * slots * rows * HD,
        ),
        name="project_last" if last else "project_own",
    )(heads, src, *args)


def attend_kernel(parts, tiles_dev, me_ref, mask_ref, *refs):
    tiles = parts * tiles_dev
    qkv_refs = refs[:parts]
    grad_refs = refs[parts : 2 * parts]
    outs = refs[2 * parts : 3 * parts]
    q_s, k_s, v_s, g_s, kt_s, dk_s, dv_s, dq_s, e_s, dp_s, dqt_s, m_s, l_s, d_s = refs[3 * parts :]
    score_scale = HD ** (-0.5)
    expo = score_scale * math.log2(math.e)
    me = me_ref[0]
    for part in range(parts):
        for sub in range(tiles_dev):
            tile = part * tiles_dev + sub
            span = slice(sub * TILE, (sub + 1) * TILE)
            q_s[tile] = qkv_refs[part][0, span, :]
            key = qkv_refs[part][1, span, :]
            k_s[tile] = key
            kt_s[tile] = key.T
            v_s[tile] = qkv_refs[part][2, span, :]
            g_s[tile] = grad_refs[part][span, :]
    dk_s[...] = jnp.zeros_like(dk_s)
    dv_s[...] = jnp.zeros_like(dv_s)

    def place(tile):
        part = lax.div(tile, tiles_dev)
        return lax.rem(me - part + parts, parts) * tiles_dev + lax.rem(tile, tiles_dev)

    key_place = [
        lax.rem(me - tile // tiles_dev + parts, parts) * tiles_dev + tile % tiles_dev
        for tile in range(tiles)
    ]

    def query_step(qi, query_sq):
        own = place(qi)
        query = q_s[qi]
        grad = g_s[qi]
        m_s[...] = jnp.full_like(m_s, -jnp.inf)
        l_s[...] = jnp.zeros_like(l_s)
        d_s[...] = jnp.zeros_like(d_s)
        dqt_s[...] = jnp.zeros_like(dqt_s)
        for ki in range(tiles):
            @pl.when(mask_ref[own, key_place[ki]] != 0)
            def _(ki=ki):
                scores = mm(k_s[ki], query, NT)
                dprob = mm(v_s[ki], grad, NT)
                top = jnp.max(scores, axis=0, keepdims=True)
                weight = jnp.exp2((scores - top) * expo)
                m_s[ki : ki + 1, :] = top
                l_s[ki : ki + 1, :] = jnp.sum(weight, axis=0, keepdims=True)
                d_s[ki : ki + 1, :] = jnp.sum(weight * dprob, axis=0, keepdims=True)
                e_s[ki] = weight
                dp_s[ki] = dprob

        tops = m_s[...]
        factor = jnp.exp2((tops - jnp.max(tops, axis=0, keepdims=True)) * expo)
        norm = jnp.sum(l_s[...] * factor, axis=0, keepdims=True)
        delta = jnp.sum(d_s[...] * factor, axis=0, keepdims=True) / norm
        m_s[...] = factor / norm
        for ki in range(tiles):
            @pl.when(mask_ref[own, key_place[ki]] != 0)
            def _(ki=ki):
                weight = e_s[ki] * m_s[ki : ki + 1, :]
                dscore = (weight * (dp_s[ki] - delta)).astype(jnp.bfloat16)
                dv_s[ki] += mm(weight.astype(jnp.bfloat16), grad, NN)
                dk_s[ki] += mm(dscore, query, NN)
                dqt_s[...] += mm(kt_s[ki], dscore, NN)

        query_full = dqt_s[...].T * score_scale
        dq_s[qi] = query_full.astype(jnp.bfloat16)
        return query_sq + jnp.sum(query_full * query_full, axis=0, keepdims=True)

    query_sq = lax.fori_loop(0, tiles, query_step, jnp.zeros((1, HD), jnp.float32))
    key_sq = jnp.zeros((1, HD), jnp.float32)
    value_sq = jnp.zeros((1, HD), jnp.float32)
    rows = tiles_dev * TILE
    for part in range(parts):
        for sub in range(tiles_dev):
            tile = part * tiles_dev + sub
            key_full = dk_s[tile] * score_scale
            value_full = dv_s[tile]
            key_sq = key_sq + jnp.sum(key_full * key_full, axis=0, keepdims=True)
            value_sq = value_sq + jnp.sum(value_full * value_full, axis=0, keepdims=True)
            low = sub * TILE
            outs[part][low : low + TILE, :] = dq_s[tile]
            outs[part][rows + low : rows + low + TILE, :] = key_full.astype(jnp.bfloat16)
            outs[part][2 * rows + low : 2 * rows + low + TILE, :] = value_full.astype(jnp.bfloat16)
    row = lax.broadcasted_iota(jnp.int32, (STAT_ROWS, HD), 0)
    total = jnp.where(
        row < 3,
        jnp.sum(query_sq, axis=1, keepdims=True),
        jnp.where(
            row < 6,
            jnp.sum(key_sq, axis=1, keepdims=True),
            jnp.sum(value_sq, axis=1, keepdims=True),
        ),
    )
    high = total.astype(jnp.bfloat16).astype(jnp.float32)
    mid = (total - high).astype(jnp.bfloat16).astype(jnp.float32)
    low = total - high - mid
    piece = lax.rem(row, 3)
    stats = jnp.where(piece == 0, high, jnp.where(piece == 1, mid, low)).astype(jnp.bfloat16)
    for part in range(parts):
        outs[part][3 * rows :, :] = stats


def attend(me, mask, qkv, grads):
    parts = len(qkv)
    rows = qkv[0].shape[1]
    tiles_dev = rows // TILE
    tiles = parts * tiles_dev
    bf16, f32 = jnp.bfloat16, jnp.float32
    pairs = tiles * tiles
    return pl.pallas_call(
        functools.partial(attend_kernel, parts, tiles_dev),
        out_shape=[jax.ShapeDtypeStruct((3 * rows + STAT_ROWS, HD), bf16)] * parts,
        in_specs=[SMEM, SMEM] + [VMEM] * (2 * parts),
        out_specs=[VMEM] * parts,
        scratch_shapes=[
            pltpu.VMEM((tiles, TILE, HD), bf16),
            pltpu.VMEM((tiles, TILE, HD), bf16),
            pltpu.VMEM((tiles, TILE, HD), bf16),
            pltpu.VMEM((tiles, TILE, HD), bf16),
            pltpu.VMEM((tiles, HD, TILE), bf16),
            pltpu.VMEM((tiles, TILE, HD), f32),
            pltpu.VMEM((tiles, TILE, HD), f32),
            pltpu.VMEM((tiles, TILE, HD), bf16),
            pltpu.VMEM((tiles, TILE, TILE), f32),
            pltpu.VMEM((tiles, TILE, TILE), f32),
            pltpu.VMEM((HD, TILE), f32),
            pltpu.VMEM((tiles, TILE), f32),
            pltpu.VMEM((tiles, TILE), f32),
            pltpu.VMEM((tiles, TILE), f32),
        ],
        cost_estimate=pl.CostEstimate(
            flops=pairs * 10 * TILE * TILE * HD,
            transcendentals=pairs * TILE * TILE,
            bytes_accessed=2 * 7 * parts * rows * HD,
        ),
        name="attend_head",
    )(me, mask, *qkv, *grads)


def unpack_kernel(parts, rows, count, fresh, heads_ref, live_ref, *refs):
    blocks = refs[:parts]
    rest = refs[parts:]
    feats = None
    if not fresh:
        feats = rest[3][...]
        rest = rest[4:]
    outs = rest[:3]
    feat_out = rest[3]
    sems = rest[4]
    if fresh:
        feats = jnp.zeros(feat_out.shape, jnp.float32)

    def copies(slot):
        cols = pl.ds(pl.multiple_of(heads_ref[slot] * HD, HD), HD)
        return [
            pltpu.make_async_copy(
                blocks[slot].at[pl.ds(j * rows, rows), :], outs[j].at[:, cols], sems.at[slot, j]
            )
            for j in range(3)
        ]

    for slot in range(parts):
        @pl.when(live_ref[slot] != 0)
        def _():
            for copy in copies(slot):
                copy.start()

    row = lax.broadcasted_iota(jnp.int32, feat_out.shape, 0)
    col = lax.broadcasted_iota(jnp.int32, feat_out.shape, 1)
    for slot in range(parts):
        stats = blocks[slot][3 * rows :, :].astype(jnp.float32)
        here = (row == heads_ref[slot]) & (live_ref[slot] != 0)
        for j in range(3):
            total = stats[3 * j : 3 * j + 1, :3] + stats[3 * j + 1 : 3 * j + 2, :3]
            total = total + stats[3 * j + 2 : 3 * j + 3, :3]
            feats = jnp.where(here & (col == j), jnp.log(total / count + 1e-06), feats)
    feat_out[...] = feats
    for slot in range(parts):
        @pl.when(live_ref[slot] != 0)
        def _():
            for copy in copies(slot):
                copy.wait()


def unpack(heads, live, blocks, before, head_count, count):
    parts = len(blocks)
    rows = (blocks[0].shape[0] - STAT_ROWS) // 3
    fresh = before is None
    kept = [] if fresh else list(before)
    big = jax.ShapeDtypeStruct((rows, head_count * HD), jnp.bfloat16)
    return pl.pallas_call(
        functools.partial(unpack_kernel, parts, rows, count, fresh),
        out_shape=[big, big, big, jax.ShapeDtypeStruct((head_count, 3), jnp.float32)],
        in_specs=[SMEM, SMEM] + [VMEM] * parts + ([] if fresh else [ANY, ANY, ANY, VMEM]),
        out_specs=[ANY, ANY, ANY, VMEM],
        scratch_shapes=[pltpu.SemaphoreType.DMA((parts, 3))],
        input_output_aliases={} if fresh else {2 + parts + j: j for j in range(3)},
        cost_estimate=pl.CostEstimate(
            flops=0, transcendentals=0, bytes_accessed=12 * parts * rows * HD
        ),
        name="unpack_heads",
    )(heads, live, *blocks, *kept)


def shift(arr, axis, step, size, targets):
    pairs = [(s, (s + step) % size) for s in range(size) if (s + step) % size in targets]
    return lax.ppermute(arr, axis, pairs)


def shift_back(arr, axis, step, size, sources):
    return lax.ppermute(arr, axis, [(s, (s - step) % size) for s in sources])


def allowed_tiles(key_list, key_count):
    tiles, slots = key_list.shape
    live = jnp.arange(slots)[None, :] < key_count[:, None]
    hit = (key_list[:, :, None] == jnp.arange(tiles)[None, None, :]) & live[:, :, None]
    return jnp.any(hit, axis=1).astype(jnp.int32)


def by_heads(query_states, key_states, value_states, output_grad, w_out, key_list, key_count):
    parts = lax.axis_size("seq")
    me = lax.axis_index("seq")
    sides = lax.axis_size("head")
    side = lax.axis_index("head")
    rows, width = query_states.shape[1:]
    head_count = width // HD
    full, extra = divmod(head_count, parts)
    low = (parts - extra) // 2
    rounds = [(k * parts, 0, parts) for k in range(full)]
    if extra:
        rounds.append((full * parts, low, extra))
    dest = lax.rem(me + jnp.arange(parts, dtype=jnp.int32), parts)
    heads, lives, targets = [], [], []
    for base, first, size in rounds:
        heads.append(base + jnp.clip(dest - first, 0, size - 1).astype(jnp.int32))
        lives.append(((dest >= first) & (dest < first + size)).astype(jnp.int32))
        targets.append(list(range(first, first + size)))
    me_arr = me.astype(jnp.int32).reshape(1)
    mask = allowed_tiles(key_list[0], key_count[0])
    other = [
        lax.ppermute(output_grad[0], "head", [(s, (s + i) % sides) for s in range(sides)])
        for i in range(1, sides)
    ]
    qkv = []
    for head, target in zip(heads, targets):
        slots = pack(head, query_states[0], key_states[0], value_states[0])
        qkv.append(
            [slots[0]] + [shift(slots[i], "seq", i, parts, target) for i in range(1, parts)]
        )
    all_heads = jnp.concatenate(heads)
    acc = project(all_heads, side.astype(jnp.int32).reshape(1), output_grad[0], w_out, None, False)
    for i in range(1, sides):
        src = lax.rem(side - i + sides, sides).astype(jnp.int32).reshape(1)
        acc = project(all_heads, src, other[i - 1], w_out, acc, i == sides - 1)
    before = None
    for k, (head, live, target) in enumerate(zip(heads, lives, targets)):
        slots = acc[k * parts : (k + 1) * parts]
        grads = [slots[0]] + [shift(slots[i], "seq", i, parts, target) for i in range(1, parts)]
        done = attend(me_arr, mask * live[0], qkv[k], grads)
        back = [done[0]] + [
            shift_back(done[i], "seq", i, parts, target) for i in range(1, parts)
        ]
        before = unpack(head, live, back, before, head_count, parts * rows * HD)
    return tuple(arr[None] for arr in before)


def attend_gathered(query_tiles, key_buf, value_buf, grad_tiles, buf_slots, counts):
    score_scale = HD ** (-0.5)
    tile_count, tile_rows, feat_width = query_tiles.shape
    slot_count = buf_slots.shape[1]
    key_span = slot_count * tile_rows
    buf_tiles = key_buf.shape[0]
    key_sel = key_buf[buf_slots].reshape(tile_count, key_span, feat_width)
    value_sel = value_buf[buf_slots].reshape(tile_count, key_span, feat_width)
    allowed = jnp.arange(key_span)[None, :] // tile_rows < counts[:, None]

    def head_step(head_idx, carried):
        query_acc, key_acc, value_acc = carried
        col_start = head_idx * HD
        query_head = lax.dynamic_slice_in_dim(query_tiles, col_start, HD, 2)
        key_head = lax.dynamic_slice_in_dim(key_sel, col_start, HD, 2)
        value_head = lax.dynamic_slice_in_dim(value_sel, col_start, HD, 2)
        grad_head = lax.dynamic_slice_in_dim(grad_tiles, col_start, HD, 2)
        scores = (
            jnp.einsum("iqe,ike->iqk", query_head, key_head, preferred_element_type=jnp.float32)
            * score_scale
        )
        scores = jnp.where(allowed[:, None, :], scores, -jnp.inf)
        row_max = jnp.max(scores, axis=-1, keepdims=True)
        log_norm = row_max + jnp.log(jnp.sum(jnp.exp(scores - row_max), axis=-1, keepdims=True))
        weights = jnp.exp(scores - log_norm)
        weights_b = weights.astype(jnp.bfloat16)
        attn_out = jnp.einsum(
            "iqk,ike->iqe", weights_b, value_head, preferred_element_type=jnp.float32
        ).astype(jnp.bfloat16)
        row_delta = jnp.sum(
            grad_head.astype(jnp.float32) * attn_out.astype(jnp.float32), axis=-1, keepdims=True
        )
        dprob = jnp.einsum(
            "iqe,ike->iqk", grad_head, value_head, preferred_element_type=jnp.float32
        )
        dscore = (weights * (dprob - row_delta)).astype(jnp.bfloat16)
        query_head_grad = score_scale * jnp.einsum(
            "iqk,ike->iqe", dscore, key_head, preferred_element_type=jnp.float32
        )
        key_head_grad = score_scale * jnp.einsum(
            "iqk,iqe->ike", dscore, query_head, preferred_element_type=jnp.float32
        )
        value_head_grad = jnp.einsum(
            "iqk,iqe->ike", weights_b, grad_head, preferred_element_type=jnp.float32
        )
        query_acc = lax.dynamic_update_slice_in_dim(query_acc, query_head_grad, col_start, 2)
        key_acc = lax.dynamic_update_slice_in_dim(key_acc, key_head_grad, col_start, 2)
        value_acc = lax.dynamic_update_slice_in_dim(value_acc, value_head_grad, col_start, 2)
        return (query_acc, key_acc, value_acc)

    start_state = (
        jnp.zeros((tile_count, tile_rows, feat_width), jnp.float32),
        jnp.zeros((tile_count, key_span, feat_width), jnp.float32),
        jnp.zeros((tile_count, key_span, feat_width), jnp.float32),
    )
    query_full, key_sel_grad, value_sel_grad = lax.fori_loop(
        0, feat_width // HD, head_step, start_state
    )
    live_slot = jnp.arange(slot_count)[None, :] < counts[:, None]
    routing = (
        (buf_slots[:, :, None] == jnp.arange(buf_tiles)[None, None, :]) & live_slot[:, :, None]
    ).astype(jnp.float32)
    key_grad_buf = jnp.einsum(
        "imb,imr->br",
        routing,
        key_sel_grad.reshape(tile_count, slot_count, tile_rows * feat_width),
        precision=lax.Precision.HIGHEST,
    )
    value_grad_buf = jnp.einsum(
        "imb,imr->br",
        routing,
        value_sel_grad.reshape(tile_count, slot_count, tile_rows * feat_width),
        precision=lax.Precision.HIGHEST,
    )
    return (
        query_full,
        key_grad_buf.reshape(buf_tiles, tile_rows, feat_width),
        value_grad_buf.reshape(buf_tiles, tile_rows, feat_width),
    )


def head_squares(grads_full, head_count):
    rows = grads_full.reshape(-1, head_count, HD)
    return jnp.sum(rows * rows, axis=(0, 2))


def by_gather(query_states, key_states, value_states, output_grad, w_out, key_list, key_count):
    seq_count = lax.axis_size("seq")
    seq_index = lax.axis_index("seq")
    tok_rows = query_states.shape[1]
    feat_width = query_states.shape[2]
    head_count = feat_width // HD
    tile_count = tok_rows // TILE
    first_tile = seq_index * tile_count
    own_lists = lax.dynamic_slice_in_dim(key_list[0], first_tile, tile_count, 0)
    own_counts = lax.dynamic_slice_in_dim(key_count[0], first_tile, tile_count, 0)
    grad_out = lax.dot_general(
        lax.all_gather(output_grad, "head", axis=2, tiled=True)[0],
        w_out,
        (((1,), (1,)), ((), ())),
        preferred_element_type=jnp.float32,
    ).astype(jnp.bfloat16)
    query_tiles = query_states[0].reshape(tile_count, TILE, feat_width)
    grad_tiles = grad_out.reshape(tile_count, TILE, feat_width)
    key_whole, value_whole = (
        lax.all_gather(key_states, "seq", axis=1, tiled=True),
        lax.all_gather(value_states, "seq", axis=1, tiled=True),
    )
    key_buf = key_whole[0].reshape(-1, TILE, feat_width)
    value_buf = value_whole[0].reshape(-1, TILE, feat_width)
    query_full, key_grad_buf, value_grad_buf = attend_gathered(
        query_tiles, key_buf, value_buf, grad_tiles, own_lists, own_counts
    )
    buf_rows = key_grad_buf.shape[0] * TILE
    key_sum, value_sum = (
        lax.psum_scatter(
            key_grad_buf.reshape(1, buf_rows, feat_width).astype(jnp.bfloat16),
            "seq",
            scatter_dimension=1,
            tiled=True,
        ).astype(jnp.float32),
        lax.psum_scatter(
            value_grad_buf.reshape(1, buf_rows, feat_width).astype(jnp.bfloat16),
            "seq",
            scatter_dimension=1,
            tiled=True,
        ).astype(jnp.float32),
    )
    key_full = key_sum[0]
    value_full = value_sum[0]
    query_rows = query_full.reshape(tok_rows, feat_width)
    local_sums = jnp.stack(
        [
            head_squares(query_rows, head_count),
            head_squares(key_full, head_count),
            head_squares(value_full, head_count),
        ],
        axis=-1,
    )
    total_sums = lax.psum(local_sums, "seq")
    grad_features = jnp.log(total_sums / (seq_count * tok_rows * HD) + 1e-06)
    return (
        query_rows.astype(jnp.bfloat16)[None],
        key_full.astype(jnp.bfloat16)[None],
        value_full.astype(jnp.bfloat16)[None],
        grad_features[None],
    )


def per_device(*args):
    parts, sides = lax.axis_size("seq"), lax.axis_size("head")
    head_count = args[0].shape[2] // HD
    if head_count >= parts > 1 and parts % 2 == 0 and sides > 1:
        return by_heads(*args)
    return by_gather(*args)


def solution(mesh):
    in_specs = (
        P(("grp", "clip"), "seq", "head"),
        P(("grp", "clip"), "seq", "head"),
        P(("grp", "clip"), "seq", "head"),
        P(("grp", "clip"), "seq", "head"),
        P("head", None),
        P(("grp", "clip"), None, None),
        P(("grp", "clip"), None),
    )
    out_specs = (
        P(("grp", "clip"), "seq", "head"),
        P(("grp", "clip"), "seq", "head"),
        P(("grp", "clip"), "seq", "head"),
        P(("grp", "clip"), "head", None),
    )
    return jax.shard_map(
        per_device, mesh=mesh, in_specs=in_specs, out_specs=out_specs, check_vma=False
    )
```

```python
import functools
import math

import jax
import jax.numpy as jnp
from jax import lax
from jax.experimental import pallas as pl
from jax.experimental.pallas import tpu as pltpu
from jax.sharding import PartitionSpec as P

HD = 128
TILE = 256
STAT_ROWS = 16
SMEM = pl.BlockSpec(memory_space=pltpu.SMEM)
VMEM = pl.BlockSpec(memory_space=pltpu.VMEM)
ANY = pl.BlockSpec(memory_space=pl.ANY)
NT = (((1,), (1,)), ((), ()))
NN = (((1,), (0,)), ((), ()))
TN = (((0,), (0,)), ((), ()))


def mm(lhs, rhs, dims):
    return lax.dot_general(lhs, rhs, dims, preferred_element_type=jnp.float32)


def pack_kernel(heads_ref, q_ref, k_ref, v_ref, *outs):
    for slot, out in enumerate(outs):
        cols = pl.ds(pl.multiple_of(heads_ref[slot] * HD, HD), HD)
        out[0] = q_ref[:, cols]
        out[1] = k_ref[:, cols]
        out[2] = v_ref[:, cols]


def pack(heads, query, key, value):
    rows = query.shape[0]
    slots = heads.shape[0]
    return pl.pallas_call(
        pack_kernel,
        out_shape=[jax.ShapeDtypeStruct((3, rows, HD), query.dtype)] * slots,
        in_specs=[SMEM, VMEM, VMEM, VMEM],
        out_specs=[VMEM] * slots,
        cost_estimate=pl.CostEstimate(
            flops=0, transcendentals=0, bytes_accessed=6 * (query.size + slots * rows * HD)
        ),
        name="pack_heads",
    )(heads, query, key, value)


def project_kernel(last, heads_ref, src_ref, grad_ref, w_ref, *refs):
    total = mm(grad_ref[...], w_ref[...], NT)
    if not refs[1:]:
        refs[0][0] = total
        return
    total = total + refs[0][0]
    if not last:
        refs[1][0] = total
        return
    outs, held = refs[1:-1], refs[-1]
    step = pl.program_id(0)
    for half in range(2):
        held[2 * step + half] = total[:, half * HD : (half + 1) * HD].astype(jnp.bfloat16)

    @pl.when(step == pl.num_programs(0) - 1)
    def _():
        for slot, out in enumerate(outs):
            out[...] = held[heads_ref[slot]]


def project(heads, src, grads, w_out, acc, last):
    rows, feats = grads.shape
    slots = heads.shape[0]
    width = w_out.shape[0]
    steps = width // (2 * HD)
    in_specs = [
        pl.BlockSpec((rows, feats), lambda s, heads, src: (0, 0)),
        pl.BlockSpec((2 * HD, feats), lambda s, heads, src: (s, src[0])),
    ]
    args = [grads, w_out]
    acc_spec = pl.BlockSpec((1, rows, 2 * HD), lambda s, heads, src: (s, 0, 0))
    if acc is not None:
        in_specs.append(acc_spec)
        args.append(acc)
    scratch = []
    if last:
        out_shape = [jax.ShapeDtypeStruct((rows, HD), jnp.bfloat16)] * slots
        out_specs = [pl.BlockSpec((rows, HD), lambda s, heads, src: (0, 0))] * slots
        scratch = [pltpu.VMEM((width // HD, rows, HD), jnp.bfloat16)]
    else:
        out_shape = jax.ShapeDtypeStruct((steps, rows, 2 * HD), jnp.float32)
        out_specs = acc_spec
    return pl.pallas_call(
        functools.partial(project_kernel, last),
        out_shape=out_shape,
        grid_spec=pltpu.PrefetchScalarGridSpec(
            num_scalar_prefetch=2,
            grid=(steps,),
            in_specs=in_specs,
            out_specs=out_specs,
            scratch_shapes=scratch,
        ),
        cost_estimate=pl.CostEstimate(
            flops=2 * rows * feats * width,
            transcendentals=0,
            bytes_accessed=2 * (grads.size + width * feats) + 6 * rows * width,
        ),
        name="project_last" if last else "project_own",
    )(heads, src, *args)


def attend_kernel(parts, tiles_dev, me_ref, mask_ref, *refs):
    tiles = parts * tiles_dev
    rows = tiles_dev * TILE
    qkv_refs = refs[:parts]
    grad_refs = refs[parts : 2 * parts]
    outs = refs[2 * parts : 3 * parts]
    q_s, k_s, v_s, g_s, dk_s, dv_s, dq_s, e_s, dp_s, ds_s, m_s, l_s, d_s, sems = refs[
        3 * parts :
    ]
    score_scale = HD ** (-0.5)
    expo = score_scale * math.log2(math.e)
    me = me_ref[0]
    copies = []
    for part in range(parts):
        span = pl.ds(part * rows, rows)
        sources = [qkv_refs[part].at[0], qkv_refs[part].at[1], qkv_refs[part].at[2]]
        sources.append(grad_refs[part])
        for j, (source, held) in enumerate(zip(sources, (q_s, k_s, v_s, g_s))):
            copies.append(pltpu.make_async_copy(source, held.at[span], sems.at[part, j]))
    for copy in copies:
        copy.start()
    for copy in copies:
        copy.wait()
    dk_s[...] = jnp.zeros_like(dk_s)
    dv_s[...] = jnp.zeros_like(dv_s)

    def home(part):
        return lax.rem(me - part + parts, parts) * tiles_dev

    def query_step(part, query_sq):
        own = home(part)
        span = pl.ds(pl.multiple_of(part * rows, rows), rows)
        query = q_s[span, :]
        grad = g_s[span, :]
        for ki in range(tiles):
            place = home(ki // tiles_dev) + ki % tiles_dev
            scores = mm(k_s[ki * TILE : (ki + 1) * TILE, :], query, NT)
            dprob = mm(v_s[ki * TILE : (ki + 1) * TILE, :], grad, NT)
            top = jnp.max(scores, axis=0, keepdims=True)
            weight = jnp.exp2((scores - top) * expo)
            for sub in range(tiles_dev):
                cols = slice(sub * TILE, (sub + 1) * TILE)
                live = mask_ref[own + sub, place] != 0
                m_s[ki : ki + 1, cols] = jnp.where(live, top[:, cols], -jnp.inf)
            l_s[ki : ki + 1, :] = jnp.sum(weight, axis=0, keepdims=True)
            d_s[ki : ki + 1, :] = jnp.sum(weight * dprob, axis=0, keepdims=True)
            e_s[ki] = weight
            dp_s[ki] = dprob

        tops = m_s[...]
        factor = jnp.exp2((tops - jnp.max(tops, axis=0, keepdims=True)) * expo)
        norm = jnp.sum(l_s[...] * factor, axis=0, keepdims=True)
        delta = jnp.sum(d_s[...] * factor, axis=0, keepdims=True) / norm
        m_s[...] = factor / norm
        for ki in range(tiles):
            weight = e_s[ki] * m_s[ki : ki + 1, :]
            dscore = (weight * (dp_s[ki] - delta)).astype(jnp.bfloat16)
            dv_s[ki] += mm(weight.astype(jnp.bfloat16), grad, NN)
            dk_s[ki] += mm(dscore, query, NN)
            ds_s[ki * TILE : (ki + 1) * TILE, :] = dscore

        query_full = mm(ds_s[...], k_s[...], TN) * score_scale
        dq_s[part] = query_full.astype(jnp.bfloat16)
        return query_sq + jnp.sum(query_full * query_full, axis=0, keepdims=True)

    query_sq = lax.fori_loop(0, parts * me_ref[1], query_step, jnp.zeros((1, HD), jnp.float32))
    key_sq = jnp.zeros((1, HD), jnp.float32)
    value_sq = jnp.zeros((1, HD), jnp.float32)
    for part in range(parts):
        for sub in range(tiles_dev):
            tile = part * tiles_dev + sub
            key_full = dk_s[tile] * score_scale
            value_full = dv_s[tile]
            key_sq = key_sq + jnp.sum(key_full * key_full, axis=0, keepdims=True)
            value_sq = value_sq + jnp.sum(value_full * value_full, axis=0, keepdims=True)
            low = sub * TILE
            outs[part][low : low + TILE, :] = dq_s[part, low : low + TILE, :]
            outs[part][rows + low : rows + low + TILE, :] = key_full.astype(jnp.bfloat16)
            outs[part][2 * rows + low : 2 * rows + low + TILE, :] = value_full.astype(jnp.bfloat16)
    row = lax.broadcasted_iota(jnp.int32, (STAT_ROWS, HD), 0)
    total = jnp.where(
        row < 3,
        jnp.sum(query_sq, axis=1, keepdims=True),
        jnp.where(
            row < 6,
            jnp.sum(key_sq, axis=1, keepdims=True),
            jnp.sum(value_sq, axis=1, keepdims=True),
        ),
    )
    high = total.astype(jnp.bfloat16).astype(jnp.float32)
    mid = (total - high).astype(jnp.bfloat16).astype(jnp.float32)
    low = total - high - mid
    piece = lax.rem(row, 3)
    stats = jnp.where(piece == 0, high, jnp.where(piece == 1, mid, low)).astype(jnp.bfloat16)
    for part in range(parts):
        outs[part][3 * rows :, :] = stats


def attend(me, mask, qkv, grads):
    parts = len(qkv)
    rows = qkv[0].shape[1]
    tiles_dev = rows // TILE
    tiles = parts * tiles_dev
    bf16, f32 = jnp.bfloat16, jnp.float32
    pairs = tiles * tiles
    return pl.pallas_call(
        functools.partial(attend_kernel, parts, tiles_dev),
        out_shape=[jax.ShapeDtypeStruct((3 * rows + STAT_ROWS, HD), bf16)] * parts,
        in_specs=[SMEM, SMEM] + [ANY] * (2 * parts),
        out_specs=[VMEM] * parts,
        scratch_shapes=[
            pltpu.VMEM((parts * rows, HD), bf16),
            pltpu.VMEM((parts * rows, HD), bf16),
            pltpu.VMEM((parts * rows, HD), bf16),
            pltpu.VMEM((parts * rows, HD), bf16),
            pltpu.VMEM((tiles, TILE, HD), f32),
            pltpu.VMEM((tiles, TILE, HD), f32),
            pltpu.VMEM((parts, rows, HD), bf16),
            pltpu.VMEM((tiles, TILE, rows), f32),
            pltpu.VMEM((tiles, TILE, rows), f32),
            pltpu.VMEM((tiles * TILE, rows), bf16),
            pltpu.VMEM((tiles, rows), f32),
            pltpu.VMEM((tiles, rows), f32),
            pltpu.VMEM((tiles, rows), f32),
            pltpu.SemaphoreType.DMA((parts, 4)),
        ],
        cost_estimate=pl.CostEstimate(
            flops=pairs * 10 * TILE * TILE * HD,
            transcendentals=pairs * TILE * TILE,
            bytes_accessed=2 * 7 * parts * rows * HD,
        ),
        name="attend_head",
    )(me, mask, *qkv, *grads)


def unpack_kernel(parts, rows, count, fresh, heads_ref, live_ref, *refs):
    blocks = refs[:parts]
    rest = refs[parts:]
    feats = None
    if not fresh:
        feats = rest[3][...]
        rest = rest[4:]
    outs = rest[:3]
    feat_out = rest[3]
    sems = rest[4]
    if fresh:
        feats = jnp.zeros(feat_out.shape, jnp.float32)

    def copies(slot):
        cols = pl.ds(pl.multiple_of(heads_ref[slot] * HD, HD), HD)
        return [
            pltpu.make_async_copy(
                blocks[slot].at[pl.ds(j * rows, rows), :], outs[j].at[:, cols], sems.at[slot, j]
            )
            for j in range(3)
        ]

    for slot in range(parts):
        @pl.when(live_ref[slot] != 0)
        def _():
            for copy in copies(slot):
                copy.start()

    row = lax.broadcasted_iota(jnp.int32, feat_out.shape, 0)
    col = lax.broadcasted_iota(jnp.int32, feat_out.shape, 1)
    for slot in range(parts):
        stats = blocks[slot][3 * rows :, :].astype(jnp.float32)
        here = (row == heads_ref[slot]) & (live_ref[slot] != 0)
        for j in range(3):
            total = stats[3 * j : 3 * j + 1, :3] + stats[3 * j + 1 : 3 * j + 2, :3]
            total = total + stats[3 * j + 2 : 3 * j + 3, :3]
            feats = jnp.where(here & (col == j), jnp.log(total / count + 1e-06), feats)
    feat_out[...] = feats
    for slot in range(parts):
        @pl.when(live_ref[slot] != 0)
        def _():
            for copy in copies(slot):
                copy.wait()


def unpack(heads, live, blocks, before, head_count, count):
    parts = len(blocks)
    rows = (blocks[0].shape[0] - STAT_ROWS) // 3
    fresh = before is None
    kept = [] if fresh else list(before)
    big = jax.ShapeDtypeStruct((rows, head_count * HD), jnp.bfloat16)
    return pl.pallas_call(
        functools.partial(unpack_kernel, parts, rows, count, fresh),
        out_shape=[big, big, big, jax.ShapeDtypeStruct((head_count, 3), jnp.float32)],
        in_specs=[SMEM, SMEM] + [VMEM] * parts + ([] if fresh else [ANY, ANY, ANY, VMEM]),
        out_specs=[ANY, ANY, ANY, VMEM],
        scratch_shapes=[pltpu.SemaphoreType.DMA((parts, 3))],
        input_output_aliases={} if fresh else {2 + parts + j: j for j in range(3)},
        cost_estimate=pl.CostEstimate(
            flops=0, transcendentals=0, bytes_accessed=12 * parts * rows * HD
        ),
        name="unpack_heads",
    )(heads, live, *blocks, *kept)


def shift(arr, axis, step, size, targets):
    pairs = [(s, (s + step) % size) for s in range(size) if (s + step) % size in targets]
    return lax.ppermute(arr, axis, pairs)


def shift_back(arr, axis, step, size, sources):
    return lax.ppermute(arr, axis, [(s, (s - step) % size) for s in sources])


def allowed_tiles(key_list, key_count):
    tiles, slots = key_list.shape
    live = jnp.arange(slots)[None, :] < key_count[:, None]
    hit = (key_list[:, :, None] == jnp.arange(tiles)[None, None, :]) & live[:, :, None]
    return jnp.any(hit, axis=1).astype(jnp.int32)


def by_heads(query_states, key_states, value_states, output_grad, w_out, key_list, key_count):
    parts = lax.axis_size("seq")
    me = lax.axis_index("seq")
    sides = lax.axis_size("head")
    side = lax.axis_index("head")
    rows, width = query_states.shape[1:]
    head_count = width // HD
    full, extra = divmod(head_count, parts)
    low = (parts - extra) // 2
    rounds = [(k * parts, 0, parts) for k in range(full)]
    if extra:
        rounds.append((full * parts, low, extra))
    dest = lax.rem(me + jnp.arange(parts, dtype=jnp.int32), parts)
    heads, lives, targets = [], [], []
    for base, first, size in rounds:
        heads.append(base + jnp.clip(dest - first, 0, size - 1).astype(jnp.int32))
        lives.append(((dest >= first) & (dest < first + size)).astype(jnp.int32))
        targets.append(list(range(first, first + size)))
    mask = allowed_tiles(key_list[0], key_count[0])
    other = [
        lax.ppermute(output_grad[0], "head", [(s, (s + i) % sides) for s in range(sides)])
        for i in range(1, sides)
    ]
    qkv = []
    for head, target in zip(heads, targets):
        slots = pack(head, query_states[0], key_states[0], value_states[0])
        qkv.append(
            [slots[0]] + [shift(slots[i], "seq", i, parts, target) for i in range(1, parts)]
        )
    all_heads = jnp.concatenate(heads)
    acc = project(all_heads, side.astype(jnp.int32).reshape(1), output_grad[0], w_out, None, False)
    for i in range(1, sides):
        src = lax.rem(side - i + sides, sides).astype(jnp.int32).reshape(1)
        acc = project(all_heads, src, other[i - 1], w_out, acc, i == sides - 1)
    before = None
    for k, (head, live, target) in enumerate(zip(heads, lives, targets)):
        slots = acc[k * parts : (k + 1) * parts]
        grads = [slots[0]] + [shift(slots[i], "seq", i, parts, target) for i in range(1, parts)]
        done = attend(jnp.stack([me.astype(jnp.int32), live[0]]), mask, qkv[k], grads)
        back = [done[0]] + [
            shift_back(done[i], "seq", i, parts, target) for i in range(1, parts)
        ]
        before = unpack(head, live, back, before, head_count, parts * rows * HD)
    return tuple(arr[None] for arr in before)


def attend_gathered(query_tiles, key_buf, value_buf, grad_tiles, buf_slots, counts):
    score_scale = HD ** (-0.5)
    tile_count, tile_rows, feat_width = query_tiles.shape
    slot_count = buf_slots.shape[1]
    key_span = slot_count * tile_rows
    buf_tiles = key_buf.shape[0]
    key_sel = key_buf[buf_slots].reshape(tile_count, key_span, feat_width)
    value_sel = value_buf[buf_slots].reshape(tile_count, key_span, feat_width)
    allowed = jnp.arange(key_span)[None, :] // tile_rows < counts[:, None]

    def head_step(head_idx, carried):
        query_acc, key_acc, value_acc = carried
        col_start = head_idx * HD
        query_head = lax.dynamic_slice_in_dim(query_tiles, col_start, HD, 2)
        key_head = lax.dynamic_slice_in_dim(key_sel, col_start, HD, 2)
        value_head = lax.dynamic_slice_in_dim(value_sel, col_start, HD, 2)
        grad_head = lax.dynamic_slice_in_dim(grad_tiles, col_start, HD, 2)
        scores = (
            jnp.einsum("iqe,ike->iqk", query_head, key_head, preferred_element_type=jnp.float32)
            * score_scale
        )
        scores = jnp.where(allowed[:, None, :], scores, -jnp.inf)
        row_max = jnp.max(scores, axis=-1, keepdims=True)
        log_norm = row_max + jnp.log(jnp.sum(jnp.exp(scores - row_max), axis=-1, keepdims=True))
        weights = jnp.exp(scores - log_norm)
        weights_b = weights.astype(jnp.bfloat16)
        attn_out = jnp.einsum(
            "iqk,ike->iqe", weights_b, value_head, preferred_element_type=jnp.float32
        ).astype(jnp.bfloat16)
        row_delta = jnp.sum(
            grad_head.astype(jnp.float32) * attn_out.astype(jnp.float32), axis=-1, keepdims=True
        )
        dprob = jnp.einsum(
            "iqe,ike->iqk", grad_head, value_head, preferred_element_type=jnp.float32
        )
        dscore = (weights * (dprob - row_delta)).astype(jnp.bfloat16)
        query_head_grad = score_scale * jnp.einsum(
            "iqk,ike->iqe", dscore, key_head, preferred_element_type=jnp.float32
        )
        key_head_grad = score_scale * jnp.einsum(
            "iqk,iqe->ike", dscore, query_head, preferred_element_type=jnp.float32
        )
        value_head_grad = jnp.einsum(
            "iqk,iqe->ike", weights_b, grad_head, preferred_element_type=jnp.float32
        )
        query_acc = lax.dynamic_update_slice_in_dim(query_acc, query_head_grad, col_start, 2)
        key_acc = lax.dynamic_update_slice_in_dim(key_acc, key_head_grad, col_start, 2)
        value_acc = lax.dynamic_update_slice_in_dim(value_acc, value_head_grad, col_start, 2)
        return (query_acc, key_acc, value_acc)

    start_state = (
        jnp.zeros((tile_count, tile_rows, feat_width), jnp.float32),
        jnp.zeros((tile_count, key_span, feat_width), jnp.float32),
        jnp.zeros((tile_count, key_span, feat_width), jnp.float32),
    )
    query_full, key_sel_grad, value_sel_grad = lax.fori_loop(
        0, feat_width // HD, head_step, start_state
    )
    live_slot = jnp.arange(slot_count)[None, :] < counts[:, None]
    routing = (
        (buf_slots[:, :, None] == jnp.arange(buf_tiles)[None, None, :]) & live_slot[:, :, None]
    ).astype(jnp.float32)
    key_grad_buf = jnp.einsum(
        "imb,imr->br",
        routing,
        key_sel_grad.reshape(tile_count, slot_count, tile_rows * feat_width),
        precision=lax.Precision.HIGHEST,
    )
    value_grad_buf = jnp.einsum(
        "imb,imr->br",
        routing,
        value_sel_grad.reshape(tile_count, slot_count, tile_rows * feat_width),
        precision=lax.Precision.HIGHEST,
    )
    return (
        query_full,
        key_grad_buf.reshape(buf_tiles, tile_rows, feat_width),
        value_grad_buf.reshape(buf_tiles, tile_rows, feat_width),
    )


def head_squares(grads_full, head_count):
    rows = grads_full.reshape(-1, head_count, HD)
    return jnp.sum(rows * rows, axis=(0, 2))


def by_gather(query_states, key_states, value_states, output_grad, w_out, key_list, key_count):
    seq_count = lax.axis_size("seq")
    seq_index = lax.axis_index("seq")
    tok_rows = query_states.shape[1]
    feat_width = query_states.shape[2]
    head_count = feat_width // HD
    tile_count = tok_rows // TILE
    first_tile = seq_index * tile_count
    own_lists = lax.dynamic_slice_in_dim(key_list[0], first_tile, tile_count, 0)
    own_counts = lax.dynamic_slice_in_dim(key_count[0], first_tile, tile_count, 0)
    grad_out = lax.dot_general(
        lax.all_gather(output_grad, "head", axis=2, tiled=True)[0],
        w_out,
        (((1,), (1,)), ((), ())),
        preferred_element_type=jnp.float32,
    ).astype(jnp.bfloat16)
    query_tiles = query_states[0].reshape(tile_count, TILE, feat_width)
    grad_tiles = grad_out.reshape(tile_count, TILE, feat_width)
    key_whole, value_whole = (
        lax.all_gather(key_states, "seq", axis=1, tiled=True),
        lax.all_gather(value_states, "seq", axis=1, tiled=True),
    )
    key_buf = key_whole[0].reshape(-1, TILE, feat_width)
    value_buf = value_whole[0].reshape(-1, TILE, feat_width)
    query_full, key_grad_buf, value_grad_buf = attend_gathered(
        query_tiles, key_buf, value_buf, grad_tiles, own_lists, own_counts
    )
    buf_rows = key_grad_buf.shape[0] * TILE
    key_sum, value_sum = (
        lax.psum_scatter(
            key_grad_buf.reshape(1, buf_rows, feat_width).astype(jnp.bfloat16),
            "seq",
            scatter_dimension=1,
            tiled=True,
        ).astype(jnp.float32),
        lax.psum_scatter(
            value_grad_buf.reshape(1, buf_rows, feat_width).astype(jnp.bfloat16),
            "seq",
            scatter_dimension=1,
            tiled=True,
        ).astype(jnp.float32),
    )
    key_full = key_sum[0]
    value_full = value_sum[0]
    query_rows = query_full.reshape(tok_rows, feat_width)
    local_sums = jnp.stack(
        [
            head_squares(query_rows, head_count),
            head_squares(key_full, head_count),
            head_squares(value_full, head_count),
        ],
        axis=-1,
    )
    total_sums = lax.psum(local_sums, "seq")
    grad_features = jnp.log(total_sums / (seq_count * tok_rows * HD) + 1e-06)
    return (
        query_rows.astype(jnp.bfloat16)[None],
        key_full.astype(jnp.bfloat16)[None],
        value_full.astype(jnp.bfloat16)[None],
        grad_features[None],
    )


def per_device(*args):
    parts, sides = lax.axis_size("seq"), lax.axis_size("head")
    head_count = args[0].shape[2] // HD
    if head_count >= parts > 1 and head_count % 2 == 0 and sides > 1:
        return by_heads(*args)
    return by_gather(*args)


def solution(mesh):
    in_specs = (
        P(("grp", "clip"), "seq", "head"),
        P(("grp", "clip"), "seq", "head"),
        P(("grp", "clip"), "seq", "head"),
        P(("grp", "clip"), "seq", "head"),
        P("head", None),
        P(("grp", "clip"), None, None),
        P(("grp", "clip"), None),
    )
    out_specs = (
        P(("grp", "clip"), "seq", "head"),
        P(("grp", "clip"), "seq", "head"),
        P(("grp", "clip"), "seq", "head"),
        P(("grp", "clip"), "head", None),
    )
    return jax.shard_map(
        per_device, mesh=mesh, in_specs=in_specs, out_specs=out_specs, check_vma=False
    )
```

```python
import functools
import math

import jax
import jax.numpy as jnp
from jax import lax
from jax.experimental import pallas as pl
from jax.experimental.pallas import tpu as pltpu
from jax.sharding import PartitionSpec as P

HD = 128
TILE = 256
STAT_ROWS = 16
SMALL_GRANT = 12 << 20
ATTEND_GRANT = 24 << 20
SMEM = pl.BlockSpec(memory_space=pltpu.SMEM)
VMEM = pl.BlockSpec(memory_space=pltpu.VMEM)
ANY = pl.BlockSpec(memory_space=pl.ANY)
NT = (((1,), (1,)), ((), ()))
NN = (((1,), (0,)), ((), ()))
TN = (((0,), (0,)), ((), ()))


def mm(lhs, rhs, dims):
    return lax.dot_general(lhs, rhs, dims, preferred_element_type=jnp.float32)


def pack_kernel(slots, heads_ref, q_ref, k_ref, v_ref, *refs):
    outs = refs[len(refs) - slots :]
    chunks = len(refs) // slots - 1
    for slot, out in enumerate(outs):
        cols = pl.ds(pl.multiple_of(heads_ref[slot] * HD, HD), HD)
        out[0] = q_ref[:, cols]
        out[1] = k_ref[:, cols]
        out[2] = v_ref[:, cols]
        for chunk in range(chunks):
            out[3, chunk * TILE : (chunk + 1) * TILE, :] = refs[chunk * slots + slot][...]


def pack(heads, query, key, value, grads):
    rows = query.shape[0]
    slots = heads.shape[0]
    kinds = 4 if grads else 3
    return pl.pallas_call(
        functools.partial(pack_kernel, slots),
        out_shape=[jax.ShapeDtypeStruct((kinds, rows, HD), query.dtype)] * slots,
        in_specs=[SMEM, VMEM, VMEM, VMEM] + [VMEM] * len(grads),
        out_specs=[VMEM] * slots,
        compiler_params=pltpu.CompilerParams(vmem_limit_bytes=SMALL_GRANT),
        cost_estimate=pl.CostEstimate(
            flops=0, transcendentals=0, bytes_accessed=6 * (query.size + slots * rows * HD)
        ),
        name="pack_heads",
    )(heads, query, key, value, *grads)


def project_own_kernel(src_ref, grad_ref, w_ref, out):
    out[0] = mm(grad_ref[...], w_ref[...], NT)


def project_own(src, grads, w_out):
    rows, feats = grads.shape
    width = w_out.shape[0]
    steps = width // (2 * HD)
    return pl.pallas_call(
        project_own_kernel,
        out_shape=jax.ShapeDtypeStruct((steps, rows, 2 * HD), jnp.float32),
        grid_spec=pltpu.PrefetchScalarGridSpec(
            num_scalar_prefetch=1,
            grid=(steps,),
            in_specs=[
                pl.BlockSpec((rows, feats), lambda s, src: (0, 0)),
                pl.BlockSpec((2 * HD, feats), lambda s, src: (s, src[0])),
            ],
            out_specs=pl.BlockSpec((1, rows, 2 * HD), lambda s, src: (s, 0, 0)),
        ),
        compiler_params=pltpu.CompilerParams(vmem_limit_bytes=SMALL_GRANT),
        cost_estimate=pl.CostEstimate(
            flops=2 * rows * feats * width,
            transcendentals=0,
            bytes_accessed=2 * (grads.size + width * feats) + 4 * rows * width,
        ),
        name="project_own",
    )(src, grads, w_out)


def project_rest_kernel(heads_ref, src_ref, grad_ref, w_ref, acc_ref, *refs):
    outs, held = refs[:-1], refs[-1]
    total = mm(grad_ref[...], w_ref[...], NT) + acc_ref[0]
    step = pl.program_id(0)
    for half in range(2):
        held[2 * step + half] = total[:, half * HD : (half + 1) * HD].astype(jnp.bfloat16)

    @pl.when(step == pl.num_programs(0) - 1)
    def _():
        for slot, out in enumerate(outs):
            out[...] = held[heads_ref[slot]]


def project_rest(heads, src, grads, w_out, acc, chunk):
    rows, feats = grads.shape
    slots = heads.shape[0]
    width = w_out.shape[0]
    steps = width // (2 * HD)
    return pl.pallas_call(
        project_rest_kernel,
        out_shape=[jax.ShapeDtypeStruct((rows, HD), jnp.bfloat16)] * slots,
        grid_spec=pltpu.PrefetchScalarGridSpec(
            num_scalar_prefetch=2,
            grid=(steps,),
            in_specs=[
                pl.BlockSpec((rows, feats), lambda s, heads, src: (0, 0)),
                pl.BlockSpec((2 * HD, feats), lambda s, heads, src: (s, src[0])),
                pl.BlockSpec((1, rows, 2 * HD), lambda s, heads, src: (s, chunk, 0)),
            ],
            out_specs=[pl.BlockSpec((rows, HD), lambda s, heads, src: (0, 0))] * slots,
            scratch_shapes=[pltpu.VMEM((width // HD, rows, HD), jnp.bfloat16)],
        ),
        compiler_params=pltpu.CompilerParams(vmem_limit_bytes=SMALL_GRANT),
        cost_estimate=pl.CostEstimate(
            flops=2 * rows * feats * width,
            transcendentals=0,
            bytes_accessed=2 * (grads.size + width * feats) + 6 * rows * width,
        ),
        name="project_rest",
    )(heads, src, grads, w_out, acc)


def attend_kernel(parts, tiles_dev, me_ref, mask_ref, *refs):
    @pl.when(me_ref[1] != 0)
    def _():
        attend_body(parts, tiles_dev, me_ref, mask_ref, *refs)


def attend_body(parts, tiles_dev, me_ref, mask_ref, *refs):
    tiles = parts * tiles_dev
    rows = tiles_dev * TILE
    blocks = refs[:parts]
    chunks = refs[parts : len(refs) - parts - 14]
    outs = refs[len(refs) - parts - 14 : len(refs) - 14]
    q_s, k_s, v_s, g_s, dk_s, dv_s, dq_s, e_s, dp_s, ds_s, m_s, l_s, d_s, sems = refs[-14:]
    score_scale = HD ** (-0.5)
    expo = score_scale * math.log2(math.e)
    me = me_ref[0]
    copies = []
    for part in range(parts):
        span = pl.ds(part * rows, rows)
        pairs = [(blocks[part].at[j], held.at[span]) for j, held in enumerate((q_s, k_s, v_s))]
        if chunks:
            for sub in range(tiles_dev):
                span = pl.ds(part * rows + sub * TILE, TILE)
                pairs.append((chunks[sub * parts + part], g_s.at[span]))
        else:
            pairs.append((blocks[part].at[3], g_s.at[span]))
        for j, (source, held) in enumerate(pairs):
            copies.append(pltpu.make_async_copy(source, held, sems.at[part, j]))
    for copy in copies:
        copy.start()
    for copy in copies:
        copy.wait()
    dk_s[...] = jnp.zeros_like(dk_s)
    dv_s[...] = jnp.zeros_like(dv_s)

    def home(part):
        return lax.rem(me - part + parts, parts) * tiles_dev

    def query_step(part, query_sq):
        own = home(part)
        span = pl.ds(pl.multiple_of(part * rows, rows), rows)
        query = q_s[span, :]
        grad = g_s[span, :]
        for ki in range(tiles):
            place = home(ki // tiles_dev) + ki % tiles_dev
            scores = mm(k_s[ki * TILE : (ki + 1) * TILE, :], query, NT)
            dprob = mm(v_s[ki * TILE : (ki + 1) * TILE, :], grad, NT)
            top = jnp.max(scores, axis=0, keepdims=True)
            weight = jnp.exp2((scores - top) * expo)
            for sub in range(tiles_dev):
                cols = slice(sub * TILE, (sub + 1) * TILE)
                live = mask_ref[own + sub, place] != 0
                m_s[ki : ki + 1, cols] = jnp.where(live, top[:, cols], -jnp.inf)
            l_s[ki : ki + 1, :] = jnp.sum(weight, axis=0, keepdims=True)
            d_s[ki : ki + 1, :] = jnp.sum(weight * dprob, axis=0, keepdims=True)
            e_s[ki] = weight
            dp_s[ki] = dprob

        tops = m_s[...]
        factor = jnp.exp2((tops - jnp.max(tops, axis=0, keepdims=True)) * expo)
        norm = jnp.sum(l_s[...] * factor, axis=0, keepdims=True)
        delta = jnp.sum(d_s[...] * factor, axis=0, keepdims=True) / norm
        m_s[...] = factor / norm
        for ki in range(tiles):
            weight = e_s[ki] * m_s[ki : ki + 1, :]
            dscore = (weight * (dp_s[ki] - delta)).astype(jnp.bfloat16)
            dv_s[ki] += mm(weight.astype(jnp.bfloat16), grad, NN)
            dk_s[ki] += mm(dscore, query, NN)
            ds_s[ki * TILE : (ki + 1) * TILE, :] = dscore

        query_full = mm(ds_s[...], k_s[...], TN) * score_scale
        dq_s[part] = query_full.astype(jnp.bfloat16)
        return query_sq + jnp.sum(query_full * query_full, axis=0, keepdims=True)

    query_sq = lax.fori_loop(0, parts, query_step, jnp.zeros((1, HD), jnp.float32))
    key_sq = jnp.zeros((1, HD), jnp.float32)
    value_sq = jnp.zeros((1, HD), jnp.float32)
    for part in range(parts):
        for sub in range(tiles_dev):
            tile = part * tiles_dev + sub
            key_full = dk_s[tile] * score_scale
            value_full = dv_s[tile]
            key_sq = key_sq + jnp.sum(key_full * key_full, axis=0, keepdims=True)
            value_sq = value_sq + jnp.sum(value_full * value_full, axis=0, keepdims=True)
            low = sub * TILE
            outs[part][low : low + TILE, :] = dq_s[part, low : low + TILE, :]
            outs[part][rows + low : rows + low + TILE, :] = key_full.astype(jnp.bfloat16)
            outs[part][2 * rows + low : 2 * rows + low + TILE, :] = value_full.astype(jnp.bfloat16)
    row = lax.broadcasted_iota(jnp.int32, (STAT_ROWS, HD), 0)
    total = jnp.where(
        row < 3,
        jnp.sum(query_sq, axis=1, keepdims=True),
        jnp.where(
            row < 6,
            jnp.sum(key_sq, axis=1, keepdims=True),
            jnp.sum(value_sq, axis=1, keepdims=True),
        ),
    )
    high = total.astype(jnp.bfloat16).astype(jnp.float32)
    mid = (total - high).astype(jnp.bfloat16).astype(jnp.float32)
    low = total - high - mid
    piece = lax.rem(row, 3)
    stats = jnp.where(piece == 0, high, jnp.where(piece == 1, mid, low)).astype(jnp.bfloat16)
    for part in range(parts):
        outs[part][3 * rows :, :] = stats


def attend(me, mask, blocks, chunks):
    parts = len(blocks)
    rows = blocks[0].shape[1]
    tiles_dev = rows // TILE
    tiles = parts * tiles_dev
    bf16, f32 = jnp.bfloat16, jnp.float32
    pairs = tiles * tiles
    return pl.pallas_call(
        functools.partial(attend_kernel, parts, tiles_dev),
        out_shape=[jax.ShapeDtypeStruct((3 * rows + STAT_ROWS, HD), bf16)] * parts,
        in_specs=[SMEM, SMEM] + [ANY] * (parts + len(chunks)),
        out_specs=[VMEM] * parts,
        scratch_shapes=[
            pltpu.VMEM((parts * rows, HD), bf16),
            pltpu.VMEM((parts * rows, HD), bf16),
            pltpu.VMEM((parts * rows, HD), bf16),
            pltpu.VMEM((parts * rows, HD), bf16),
            pltpu.VMEM((tiles, TILE, HD), f32),
            pltpu.VMEM((tiles, TILE, HD), f32),
            pltpu.VMEM((parts, rows, HD), bf16),
            pltpu.VMEM((tiles, TILE, rows), f32),
            pltpu.VMEM((tiles, TILE, rows), f32),
            pltpu.VMEM((tiles * TILE, rows), bf16),
            pltpu.VMEM((tiles, rows), f32),
            pltpu.VMEM((tiles, rows), f32),
            pltpu.VMEM((tiles, rows), f32),
            pltpu.SemaphoreType.DMA((parts, 3 + tiles_dev)),
        ],
        cost_estimate=pl.CostEstimate(
            flops=pairs * 10 * TILE * TILE * HD,
            transcendentals=pairs * TILE * TILE,
            bytes_accessed=2 * 7 * parts * rows * HD,
        ),
        compiler_params=pltpu.CompilerParams(vmem_limit_bytes=ATTEND_GRANT),
        name="attend_head",
    )(me, mask, *blocks, *chunks)


def unpack_kernel(parts, rows, count, fresh, heads_ref, live_ref, *refs):
    blocks = refs[:parts]
    rest = refs[parts:]
    feats = None
    if not fresh:
        feats = rest[3][...]
        rest = rest[4:]
    outs = rest[:3]
    feat_out = rest[3]
    sems = rest[4]
    if fresh:
        feats = jnp.zeros(feat_out.shape, jnp.float32)

    def copies(slot):
        cols = pl.ds(pl.multiple_of(heads_ref[slot] * HD, HD), HD)
        return [
            pltpu.make_async_copy(
                blocks[slot].at[pl.ds(j * rows, rows), :], outs[j].at[:, cols], sems.at[slot, j]
            )
            for j in range(3)
        ]

    for slot in range(parts):
        @pl.when(live_ref[slot] != 0)
        def _():
            for copy in copies(slot):
                copy.start()

    row = lax.broadcasted_iota(jnp.int32, feat_out.shape, 2)
    col = lax.broadcasted_iota(jnp.int32, feat_out.shape, 0)
    for slot in range(parts):
        stats = blocks[slot][3 * rows :, :].astype(jnp.float32)
        here = (row == heads_ref[slot]) & (live_ref[slot] != 0)
        for j in range(3):
            total = stats[3 * j : 3 * j + 1, :] + stats[3 * j + 1 : 3 * j + 2, :]
            total = total + stats[3 * j + 2 : 3 * j + 3, :]
            value = jnp.log(total / count + 1e-06)[:, : feat_out.shape[2]]
            feats = jnp.where(here & (col == j), value[None], feats)
    feat_out[...] = feats
    for slot in range(parts):
        @pl.when(live_ref[slot] != 0)
        def _():
            for copy in copies(slot):
                copy.wait()


def unpack(heads, live, blocks, before, head_count, count):
    parts = len(blocks)
    rows = (blocks[0].shape[0] - STAT_ROWS) // 3
    fresh = before is None
    kept = [] if fresh else list(before)
    big = jax.ShapeDtypeStruct((rows, head_count * HD), jnp.bfloat16)
    return pl.pallas_call(
        functools.partial(unpack_kernel, parts, rows, count, fresh),
        out_shape=[big, big, big, jax.ShapeDtypeStruct((3, 1, head_count), jnp.float32)],
        in_specs=[SMEM, SMEM] + [VMEM] * parts + ([] if fresh else [ANY, ANY, ANY, VMEM]),
        out_specs=[ANY, ANY, ANY, VMEM],
        scratch_shapes=[pltpu.SemaphoreType.DMA((parts, 3))],
        input_output_aliases={} if fresh else {2 + parts + j: j for j in range(3)},
        compiler_params=pltpu.CompilerParams(vmem_limit_bytes=SMALL_GRANT),
        cost_estimate=pl.CostEstimate(
            flops=0, transcendentals=0, bytes_accessed=12 * parts * rows * HD
        ),
        name="unpack_heads",
    )(heads, live, *blocks, *kept)


def shift(arr, axis, step, size, targets):
    pairs = [(s, (s + step) % size) for s in range(size) if (s + step) % size in targets]
    return lax.ppermute(arr, axis, pairs)


def shift_back(arr, axis, step, size, sources):
    return lax.ppermute(arr, axis, [(s, (s - step) % size) for s in sources])


def allowed_tiles(key_list, key_count):
    tiles, slots = key_list.shape
    live = jnp.arange(slots)[None, :] < key_count[:, None]
    hit = (key_list[:, :, None] == jnp.arange(tiles)[None, None, :]) & live[:, :, None]
    return jnp.any(hit, axis=1).astype(jnp.int32)


def by_heads(query_states, key_states, value_states, output_grad, w_out, key_list, key_count):
    parts = lax.axis_size("seq")
    me = lax.axis_index("seq")
    side = lax.axis_index("head")
    rows, width = query_states.shape[1:]
    head_count = width // HD
    full, extra = divmod(head_count, parts)
    low = (parts - extra) // 2
    rounds = [(k * parts, 0, parts) for k in range(full)]
    if extra:
        rounds.append((full * parts, low, extra))
    dest = lax.rem(me + jnp.arange(parts, dtype=jnp.int32), parts)
    heads, lives, targets = [], [], []
    for base, first, size in rounds:
        heads.append(base + jnp.clip(dest - first, 0, size - 1).astype(jnp.int32))
        lives.append(((dest >= first) & (dest < first + size)).astype(jnp.int32))
        targets.append(list(range(first, first + size)))
    mask = allowed_tiles(key_list[0], key_count[0])
    all_heads = jnp.concatenate(heads)
    chunk_count = rows // TILE
    tensors = (query_states[0], key_states[0], value_states[0])
    other = []
    for chunk in range(chunk_count):
        own = output_grad[0, chunk * TILE : (chunk + 1) * TILE]
        if other:
            own, _ = lax.optimization_barrier((own, other[-1]))
        other.append(lax.ppermute(own, "head", [(0, 1), (1, 0)]))
    side = side.astype(jnp.int32).reshape(1)
    slots = pack(heads[0], *tensors, [])
    blocks = [slots[0]] + [shift(slots[i], "seq", i, parts, targets[0]) for i in range(1, parts)]
    acc = project_own(side, output_grad[0], w_out)
    projected = [
        project_rest(all_heads, 1 - side, other[chunk], w_out, acc, chunk)
        for chunk in range(chunk_count)
    ]
    chunks = []
    for slots in projected:
        chunks += [slots[0]]
        chunks += [shift(slots[i], "seq", i, parts, targets[0]) for i in range(1, parts)]
    before = None
    for k in range(len(rounds)):
        me_live = jnp.stack([me.astype(jnp.int32), lives[k][0]])
        ready = (blocks, chunks)
        done = attend(me_live, mask, blocks, chunks)
        if k + 1 < len(rounds):
            grads = [slot for slots in projected for slot in slots[(k + 1) * parts : (k + 2) * parts]]
            slots = pack(heads[k + 1], *tensors, grads)
            slots, _ = lax.optimization_barrier((slots, ready))
            blocks = [slots[0]] + [
                shift(slots[i], "seq", i, parts, targets[k + 1]) for i in range(1, parts)
            ]
            chunks = []
        back = [done[0]] + [
            shift_back(done[i], "seq", i, parts, targets[k]) for i in range(1, parts)
        ]
        before = unpack(heads[k], lives[k], back, before, head_count, parts * rows * HD)
    query_grad, key_grad, value_grad, feats = before
    return query_grad[None], key_grad[None], value_grad[None], feats.transpose(1, 2, 0)


def attend_gathered(query_tiles, key_buf, value_buf, grad_tiles, buf_slots, counts):
    score_scale = HD ** (-0.5)
    tile_count, tile_rows, feat_width = query_tiles.shape
    slot_count = buf_slots.shape[1]
    key_span = slot_count * tile_rows
    buf_tiles = key_buf.shape[0]
    key_sel = key_buf[buf_slots].reshape(tile_count, key_span, feat_width)
    value_sel = value_buf[buf_slots].reshape(tile_count, key_span, feat_width)
    allowed = jnp.arange(key_span)[None, :] // tile_rows < counts[:, None]

    def head_step(head_idx, carried):
        query_acc, key_acc, value_acc = carried
        col_start = head_idx * HD
        query_head = lax.dynamic_slice_in_dim(query_tiles, col_start, HD, 2)
        key_head = lax.dynamic_slice_in_dim(key_sel, col_start, HD, 2)
        value_head = lax.dynamic_slice_in_dim(value_sel, col_start, HD, 2)
        grad_head = lax.dynamic_slice_in_dim(grad_tiles, col_start, HD, 2)
        scores = (
            jnp.einsum("iqe,ike->iqk", query_head, key_head, preferred_element_type=jnp.float32)
            * score_scale
        )
        scores = jnp.where(allowed[:, None, :], scores, -jnp.inf)
        row_max = jnp.max(scores, axis=-1, keepdims=True)
        log_norm = row_max + jnp.log(jnp.sum(jnp.exp(scores - row_max), axis=-1, keepdims=True))
        weights = jnp.exp(scores - log_norm)
        weights_b = weights.astype(jnp.bfloat16)
        attn_out = jnp.einsum(
            "iqk,ike->iqe", weights_b, value_head, preferred_element_type=jnp.float32
        ).astype(jnp.bfloat16)
        row_delta = jnp.sum(
            grad_head.astype(jnp.float32) * attn_out.astype(jnp.float32), axis=-1, keepdims=True
        )
        dprob = jnp.einsum(
            "iqe,ike->iqk", grad_head, value_head, preferred_element_type=jnp.float32
        )
        dscore = (weights * (dprob - row_delta)).astype(jnp.bfloat16)
        query_head_grad = score_scale * jnp.einsum(
            "iqk,ike->iqe", dscore, key_head, preferred_element_type=jnp.float32
        )
        key_head_grad = score_scale * jnp.einsum(
            "iqk,iqe->ike", dscore, query_head, preferred_element_type=jnp.float32
        )
        value_head_grad = jnp.einsum(
            "iqk,iqe->ike", weights_b, grad_head, preferred_element_type=jnp.float32
        )
        query_acc = lax.dynamic_update_slice_in_dim(query_acc, query_head_grad, col_start, 2)
        key_acc = lax.dynamic_update_slice_in_dim(key_acc, key_head_grad, col_start, 2)
        value_acc = lax.dynamic_update_slice_in_dim(value_acc, value_head_grad, col_start, 2)
        return (query_acc, key_acc, value_acc)

    start_state = (
        jnp.zeros((tile_count, tile_rows, feat_width), jnp.float32),
        jnp.zeros((tile_count, key_span, feat_width), jnp.float32),
        jnp.zeros((tile_count, key_span, feat_width), jnp.float32),
    )
    query_full, key_sel_grad, value_sel_grad = lax.fori_loop(
        0, feat_width // HD, head_step, start_state
    )
    live_slot = jnp.arange(slot_count)[None, :] < counts[:, None]
    routing = (
        (buf_slots[:, :, None] == jnp.arange(buf_tiles)[None, None, :]) & live_slot[:, :, None]
    ).astype(jnp.float32)
    key_grad_buf = jnp.einsum(
        "imb,imr->br",
        routing,
        key_sel_grad.reshape(tile_count, slot_count, tile_rows * feat_width),
        precision=lax.Precision.HIGHEST,
    )
    value_grad_buf = jnp.einsum(
        "imb,imr->br",
        routing,
        value_sel_grad.reshape(tile_count, slot_count, tile_rows * feat_width),
        precision=lax.Precision.HIGHEST,
    )
    return (
        query_full,
        key_grad_buf.reshape(buf_tiles, tile_rows, feat_width),
        value_grad_buf.reshape(buf_tiles, tile_rows, feat_width),
    )


def head_squares(grads_full, head_count):
    rows = grads_full.reshape(-1, head_count, HD)
    return jnp.sum(rows * rows, axis=(0, 2))


def by_gather(query_states, key_states, value_states, output_grad, w_out, key_list, key_count):
    seq_count = lax.axis_size("seq")
    seq_index = lax.axis_index("seq")
    tok_rows = query_states.shape[1]
    feat_width = query_states.shape[2]
    head_count = feat_width // HD
    tile_count = tok_rows // TILE
    first_tile = seq_index * tile_count
    own_lists = lax.dynamic_slice_in_dim(key_list[0], first_tile, tile_count, 0)
    own_counts = lax.dynamic_slice_in_dim(key_count[0], first_tile, tile_count, 0)
    grad_out = lax.dot_general(
        lax.all_gather(output_grad, "head", axis=2, tiled=True)[0],
        w_out,
        (((1,), (1,)), ((), ())),
        preferred_element_type=jnp.float32,
    ).astype(jnp.bfloat16)
    query_tiles = query_states[0].reshape(tile_count, TILE, feat_width)
    grad_tiles = grad_out.reshape(tile_count, TILE, feat_width)
    key_whole, value_whole = (
        lax.all_gather(key_states, "seq", axis=1, tiled=True),
        lax.all_gather(value_states, "seq", axis=1, tiled=True),
    )
    key_buf = key_whole[0].reshape(-1, TILE, feat_width)
    value_buf = value_whole[0].reshape(-1, TILE, feat_width)
    query_full, key_grad_buf, value_grad_buf = attend_gathered(
        query_tiles, key_buf, value_buf, grad_tiles, own_lists, own_counts
    )
    buf_rows = key_grad_buf.shape[0] * TILE
    key_sum, value_sum = (
        lax.psum_scatter(
            key_grad_buf.reshape(1, buf_rows, feat_width).astype(jnp.bfloat16),
            "seq",
            scatter_dimension=1,
            tiled=True,
        ).astype(jnp.float32),
        lax.psum_scatter(
            value_grad_buf.reshape(1, buf_rows, feat_width).astype(jnp.bfloat16),
            "seq",
            scatter_dimension=1,
            tiled=True,
        ).astype(jnp.float32),
    )
    key_full = key_sum[0]
    value_full = value_sum[0]
    query_rows = query_full.reshape(tok_rows, feat_width)
    local_sums = jnp.stack(
        [
            head_squares(query_rows, head_count),
            head_squares(key_full, head_count),
            head_squares(value_full, head_count),
        ],
        axis=-1,
    )
    total_sums = lax.psum(local_sums, "seq")
    grad_features = jnp.log(total_sums / (seq_count * tok_rows * HD) + 1e-06)
    return (
        query_rows.astype(jnp.bfloat16)[None],
        key_full.astype(jnp.bfloat16)[None],
        value_full.astype(jnp.bfloat16)[None],
        grad_features[None],
    )


def per_device(*args):
    parts, sides = lax.axis_size("seq"), lax.axis_size("head")
    head_count = args[0].shape[2] // HD
    if head_count >= parts > 1 and head_count % 2 == 0 and sides == 2:
        return by_heads(*args)
    return by_gather(*args)


def solution(mesh):
    in_specs = (
        P(("grp", "clip"), "seq", "head"),
        P(("grp", "clip"), "seq", "head"),
        P(("grp", "clip"), "seq", "head"),
        P(("grp", "clip"), "seq", "head"),
        P("head", None),
        P(("grp", "clip"), None, None),
        P(("grp", "clip"), None),
    )
    out_specs = (
        P(("grp", "clip"), "seq", "head"),
        P(("grp", "clip"), "seq", "head"),
        P(("grp", "clip"), "seq", "head"),
        P(("grp", "clip"), "head", None),
    )
    return jax.shard_map(
        per_device, mesh=mesh, in_specs=in_specs, out_specs=out_specs, check_vma=False
    )
```

```python
import functools
import math

import jax
import jax.numpy as jnp
from jax import lax
from jax.experimental import pallas as pl
from jax.experimental.pallas import tpu as pltpu
from jax.sharding import PartitionSpec as P

HD = 128
TILE = 256
STAT_ROWS = 16
SMALL_GRANT = 12 << 20
ATTEND_GRANT = 24 << 20
SMEM = pl.BlockSpec(memory_space=pltpu.SMEM)
VMEM = pl.BlockSpec(memory_space=pltpu.VMEM)
ANY = pl.BlockSpec(memory_space=pl.ANY)
HBM = pl.BlockSpec(memory_space=pltpu.HBM)
NT = (((1,), (1,)), ((), ()))
NN = (((1,), (0,)), ((), ()))
TN = (((0,), (0,)), ((), ()))


def mm(lhs, rhs, dims):
    return lax.dot_general(lhs, rhs, dims, preferred_element_type=jnp.float32)


def pack_kernel(slots, heads_ref, *refs):
    tensors = refs[: len(refs) - slots - 1]
    outs = refs[len(refs) - slots - 1 : -1]
    copies = []
    for slot, out in enumerate(outs):
        cols = pl.ds(pl.multiple_of(heads_ref[slot] * HD, HD), HD)
        for j, tensor in enumerate(tensors):
            copies.append(
                pltpu.make_async_copy(tensor.at[:, cols], out.at[j], refs[-1].at[slot, j])
            )
    for copy in copies:
        copy.start()
    for copy in copies:
        copy.wait()


def pack(heads, tensors):
    rows = tensors[0].shape[0]
    slots = heads.shape[0]
    return pl.pallas_call(
        functools.partial(pack_kernel, slots),
        out_shape=[jax.ShapeDtypeStruct((len(tensors), rows, HD), jnp.bfloat16)] * slots,
        in_specs=[SMEM] + [HBM] * len(tensors),
        out_specs=[VMEM] * slots,
        scratch_shapes=[pltpu.SemaphoreType.DMA((slots, len(tensors)))],
        cost_estimate=pl.CostEstimate(
            flops=0, transcendentals=0, bytes_accessed=12 * slots * rows * HD
        ),
        name="pack_heads",
    )(heads, *tensors)


def project_own_kernel(src_ref, grad_ref, w_ref, out):
    out[0] = mm(grad_ref[...], w_ref[...], NT)


def project_own(src, grads, w_out):
    rows, feats = grads.shape
    width = w_out.shape[0]
    steps = width // (2 * HD)
    return pl.pallas_call(
        project_own_kernel,
        out_shape=jax.ShapeDtypeStruct((steps, rows, 2 * HD), jnp.float32),
        grid_spec=pltpu.PrefetchScalarGridSpec(
            num_scalar_prefetch=1,
            grid=(steps,),
            in_specs=[
                pl.BlockSpec((rows, feats), lambda s, src: (0, 0)),
                pl.BlockSpec((2 * HD, feats), lambda s, src: (s, src[0])),
            ],
            out_specs=pl.BlockSpec((1, rows, 2 * HD), lambda s, src: (s, 0, 0)),
        ),
        compiler_params=pltpu.CompilerParams(vmem_limit_bytes=SMALL_GRANT),
        cost_estimate=pl.CostEstimate(
            flops=2 * rows * feats * width,
            transcendentals=0,
            bytes_accessed=2 * (grads.size + width * feats) + 4 * rows * width,
        ),
        name="project_own",
    )(src, grads, w_out)


def project_rest_kernel(heads_ref, src_ref, grad_ref, w_ref, acc_ref, *refs):
    outs, held = refs[:-1], refs[-1]
    total = mm(grad_ref[...], w_ref[...], NT) + acc_ref[0]
    step = pl.program_id(0)
    for half in range(2):
        held[2 * step + half] = total[:, half * HD : (half + 1) * HD].astype(jnp.bfloat16)

    @pl.when(step == pl.num_programs(0) - 1)
    def _():
        for slot, out in enumerate(outs):
            out[...] = held[heads_ref[slot]]


def project_rest(heads, src, grads, w_out, acc, chunk):
    rows, feats = grads.shape
    slots = heads.shape[0]
    width = w_out.shape[0]
    steps = width // (2 * HD)
    return pl.pallas_call(
        project_rest_kernel,
        out_shape=[jax.ShapeDtypeStruct((rows, HD), jnp.bfloat16)] * slots,
        grid_spec=pltpu.PrefetchScalarGridSpec(
            num_scalar_prefetch=2,
            grid=(steps,),
            in_specs=[
                pl.BlockSpec((rows, feats), lambda s, heads, src: (0, 0)),
                pl.BlockSpec((2 * HD, feats), lambda s, heads, src: (s, src[0])),
                pl.BlockSpec((1, rows, 2 * HD), lambda s, heads, src: (s, chunk, 0)),
            ],
            out_specs=[pl.BlockSpec((rows, HD), lambda s, heads, src: (0, 0))] * slots,
            scratch_shapes=[pltpu.VMEM((width // HD, rows, HD), jnp.bfloat16)],
        ),
        compiler_params=pltpu.CompilerParams(vmem_limit_bytes=SMALL_GRANT),
        cost_estimate=pl.CostEstimate(
            flops=2 * rows * feats * width,
            transcendentals=0,
            bytes_accessed=2 * (grads.size + width * feats) + 6 * rows * width,
        ),
        name="project_rest",
    )(heads, src, grads, w_out, acc)


def attend_kernel(parts, tiles_dev, me_ref, mask_ref, *refs):
    @pl.when(me_ref[1] != 0)
    def _():
        attend_body(parts, tiles_dev, me_ref, mask_ref, *refs)


def attend_body(parts, tiles_dev, me_ref, mask_ref, *refs):
    tiles = parts * tiles_dev
    rows = tiles_dev * TILE
    blocks = refs[:parts]
    chunks = refs[parts : len(refs) - parts - 14]
    outs = refs[len(refs) - parts - 14 : len(refs) - 14]
    q_s, k_s, v_s, g_s, dk_s, dv_s, dq_s, e_s, dp_s, ds_s, m_s, l_s, d_s, sems = refs[-14:]
    score_scale = HD ** (-0.5)
    expo = score_scale * math.log2(math.e)
    me = me_ref[0]
    copies = []
    for part in range(parts):
        span = pl.ds(part * rows, rows)
        pairs = [(blocks[part].at[j], held.at[span]) for j, held in enumerate((q_s, k_s, v_s))]
        for sub in range(tiles_dev):
            span = pl.ds(part * rows + sub * TILE, TILE)
            pairs.append((chunks[sub * parts + part], g_s.at[span]))
        for j, (source, held) in enumerate(pairs):
            copies.append(pltpu.make_async_copy(source, held, sems.at[part, j]))
    for copy in copies:
        copy.start()
    for copy in copies:
        copy.wait()
    dk_s[...] = jnp.zeros_like(dk_s)
    dv_s[...] = jnp.zeros_like(dv_s)

    def home(part):
        return lax.rem(me - part + parts, parts) * tiles_dev

    def query_step(part, query_sq):
        own = home(part)
        span = pl.ds(pl.multiple_of(part * rows, rows), rows)
        query = q_s[span, :]
        grad = g_s[span, :]
        for ki in range(tiles):
            place = home(ki // tiles_dev) + ki % tiles_dev
            scores = mm(k_s[ki * TILE : (ki + 1) * TILE, :], query, NT)
            dprob = mm(v_s[ki * TILE : (ki + 1) * TILE, :], grad, NT)
            top = jnp.max(scores, axis=0, keepdims=True)
            weight = jnp.exp2((scores - top) * expo)
            for sub in range(tiles_dev):
                cols = slice(sub * TILE, (sub + 1) * TILE)
                live = mask_ref[own + sub, place] != 0
                m_s[ki : ki + 1, cols] = jnp.where(live, top[:, cols], -jnp.inf)
            l_s[ki : ki + 1, :] = jnp.sum(weight, axis=0, keepdims=True)
            d_s[ki : ki + 1, :] = jnp.sum(weight * dprob, axis=0, keepdims=True)
            e_s[ki] = weight
            dp_s[ki] = dprob

        tops = m_s[...]
        factor = jnp.exp2((tops - jnp.max(tops, axis=0, keepdims=True)) * expo)
        norm = jnp.sum(l_s[...] * factor, axis=0, keepdims=True)
        delta = jnp.sum(d_s[...] * factor, axis=0, keepdims=True) / norm
        m_s[...] = factor / norm
        for ki in range(tiles):
            weight = e_s[ki] * m_s[ki : ki + 1, :]
            dscore = (weight * (dp_s[ki] - delta)).astype(jnp.bfloat16)
            dv_s[ki] += mm(weight.astype(jnp.bfloat16), grad, NN)
            dk_s[ki] += mm(dscore, query, NN)
            ds_s[ki * TILE : (ki + 1) * TILE, :] = dscore

        query_full = mm(ds_s[...], k_s[...], TN) * score_scale
        dq_s[part] = query_full.astype(jnp.bfloat16)
        return query_sq + jnp.sum(query_full * query_full, axis=0, keepdims=True)

    query_sq = lax.fori_loop(0, parts, query_step, jnp.zeros((1, HD), jnp.float32))
    key_sq = jnp.zeros((1, HD), jnp.float32)
    value_sq = jnp.zeros((1, HD), jnp.float32)
    for part in range(parts):
        for sub in range(tiles_dev):
            tile = part * tiles_dev + sub
            key_full = dk_s[tile] * score_scale
            value_full = dv_s[tile]
            key_sq = key_sq + jnp.sum(key_full * key_full, axis=0, keepdims=True)
            value_sq = value_sq + jnp.sum(value_full * value_full, axis=0, keepdims=True)
            low = sub * TILE
            outs[part][low : low + TILE, :] = dq_s[part, low : low + TILE, :]
            outs[part][rows + low : rows + low + TILE, :] = key_full.astype(jnp.bfloat16)
            outs[part][2 * rows + low : 2 * rows + low + TILE, :] = value_full.astype(jnp.bfloat16)
    row = lax.broadcasted_iota(jnp.int32, (STAT_ROWS, HD), 0)
    total = jnp.where(
        row < 3,
        jnp.sum(query_sq, axis=1, keepdims=True),
        jnp.where(
            row < 6,
            jnp.sum(key_sq, axis=1, keepdims=True),
            jnp.sum(value_sq, axis=1, keepdims=True),
        ),
    )
    high = total.astype(jnp.bfloat16).astype(jnp.float32)
    mid = (total - high).astype(jnp.bfloat16).astype(jnp.float32)
    low = total - high - mid
    piece = lax.rem(row, 3)
    stats = jnp.where(piece == 0, high, jnp.where(piece == 1, mid, low)).astype(jnp.bfloat16)
    for part in range(parts):
        outs[part][3 * rows :, :] = stats


def attend(me, mask, blocks, chunks):
    parts = len(blocks)
    rows = blocks[0].shape[1]
    tiles_dev = rows // TILE
    tiles = parts * tiles_dev
    bf16, f32 = jnp.bfloat16, jnp.float32
    pairs = tiles * tiles
    return pl.pallas_call(
        functools.partial(attend_kernel, parts, tiles_dev),
        out_shape=[jax.ShapeDtypeStruct((3 * rows + STAT_ROWS, HD), bf16)] * parts,
        in_specs=[SMEM, SMEM] + [ANY] * (parts + len(chunks)),
        out_specs=[VMEM] * parts,
        scratch_shapes=[
            pltpu.VMEM((parts * rows, HD), bf16),
            pltpu.VMEM((parts * rows, HD), bf16),
            pltpu.VMEM((parts * rows, HD), bf16),
            pltpu.VMEM((parts * rows, HD), bf16),
            pltpu.VMEM((tiles, TILE, HD), f32),
            pltpu.VMEM((tiles, TILE, HD), f32),
            pltpu.VMEM((parts, rows, HD), bf16),
            pltpu.VMEM((tiles, TILE, rows), f32),
            pltpu.VMEM((tiles, TILE, rows), f32),
            pltpu.VMEM((tiles * TILE, rows), bf16),
            pltpu.VMEM((tiles, rows), f32),
            pltpu.VMEM((tiles, rows), f32),
            pltpu.VMEM((tiles, rows), f32),
            pltpu.SemaphoreType.DMA((parts, 3 + tiles_dev)),
        ],
        cost_estimate=pl.CostEstimate(
            flops=pairs * 10 * TILE * TILE * HD,
            transcendentals=pairs * TILE * TILE,
            bytes_accessed=2 * 7 * parts * rows * HD,
        ),
        compiler_params=pltpu.CompilerParams(vmem_limit_bytes=ATTEND_GRANT),
        name="attend_head",
    )(me, mask, *blocks, *chunks)


def unpack_kernel(parts, rows, count, fresh, heads_ref, live_ref, *refs):
    blocks = refs[:parts]
    rest = refs[parts:]
    feats = None
    if not fresh:
        feats = rest[3][...]
        rest = rest[4:]
    outs = rest[:3]
    feat_out = rest[3]
    stat_s, sems = rest[4:]
    if fresh:
        feats = jnp.zeros(feat_out.shape, jnp.float32)

    def copies(slot):
        cols = pl.ds(pl.multiple_of(heads_ref[slot] * HD, HD), HD)
        return [
            pltpu.make_async_copy(
                blocks[slot].at[pl.ds(j * rows, rows), :], outs[j].at[:, cols], sems.at[slot, j]
            )
            for j in range(3)
        ]

    stat_copies = [
        pltpu.make_async_copy(
            blocks[slot].at[pl.ds(3 * rows, STAT_ROWS), :], stat_s.at[slot], sems.at[slot, 3]
        )
        for slot in range(parts)
    ]
    for copy in stat_copies:
        copy.start()
    for slot in range(parts):
        @pl.when(live_ref[slot] != 0)
        def _():
            for copy in copies(slot):
                copy.start()

    for copy in stat_copies:
        copy.wait()

    row = lax.broadcasted_iota(jnp.int32, feat_out.shape, 2)
    col = lax.broadcasted_iota(jnp.int32, feat_out.shape, 0)
    for slot in range(parts):
        stats = stat_s[slot].astype(jnp.float32)
        here = (row == heads_ref[slot]) & (live_ref[slot] != 0)
        for j in range(3):
            total = stats[3 * j : 3 * j + 1, :] + stats[3 * j + 1 : 3 * j + 2, :]
            total = total + stats[3 * j + 2 : 3 * j + 3, :]
            value = jnp.log(total / count + 1e-06)[:, : feat_out.shape[2]]
            feats = jnp.where(here & (col == j), value[None], feats)
    feat_out[...] = feats
    for slot in range(parts):
        @pl.when(live_ref[slot] != 0)
        def _():
            for copy in copies(slot):
                copy.wait()


def unpack(heads, live, blocks, before, head_count, count):
    parts = len(blocks)
    rows = (blocks[0].shape[0] - STAT_ROWS) // 3
    fresh = before is None
    kept = [] if fresh else list(before)
    big = jax.ShapeDtypeStruct((rows, head_count * HD), jnp.bfloat16)
    return pl.pallas_call(
        functools.partial(unpack_kernel, parts, rows, count, fresh),
        out_shape=[big, big, big, jax.ShapeDtypeStruct((3, 1, head_count), jnp.float32)],
        in_specs=[SMEM, SMEM] + [ANY] * parts + ([] if fresh else [ANY, ANY, ANY, VMEM]),
        out_specs=[ANY, ANY, ANY, VMEM],
        scratch_shapes=[
            pltpu.VMEM((parts, STAT_ROWS, HD), jnp.bfloat16),
            pltpu.SemaphoreType.DMA((parts, 4)),
        ],
        input_output_aliases={} if fresh else {2 + parts + j: j for j in range(3)},
        compiler_params=pltpu.CompilerParams(vmem_limit_bytes=SMALL_GRANT),
        cost_estimate=pl.CostEstimate(
            flops=0, transcendentals=0, bytes_accessed=12 * parts * rows * HD
        ),
        name="unpack_heads",
    )(heads, live, *blocks, *kept)


def shift(arr, axis, step, size, targets):
    pairs = [(s, (s + step) % size) for s in range(size) if (s + step) % size in targets]
    return lax.ppermute(arr, axis, pairs)


def shift_back(arr, axis, step, size, sources):
    return lax.ppermute(arr, axis, [(s, (s - step) % size) for s in sources])


def allowed_tiles(key_list, key_count):
    tiles, slots = key_list.shape
    live = jnp.arange(slots)[None, :] < key_count[:, None]
    hit = (key_list[:, :, None] == jnp.arange(tiles)[None, None, :]) & live[:, :, None]
    return jnp.any(hit, axis=1).astype(jnp.int32)


def by_heads(query_states, key_states, value_states, output_grad, w_out, key_list, key_count):
    parts = lax.axis_size("seq")
    me = lax.axis_index("seq")
    side = lax.axis_index("head")
    rows, width = query_states.shape[1:]
    head_count = width // HD
    full, extra = divmod(head_count, parts)
    low = (parts - extra) // 2
    rounds = [(full * parts, low, extra)] if extra else []
    rounds += [(k * parts, 0, parts) for k in range(full)]
    dest = lax.rem(me + jnp.arange(parts, dtype=jnp.int32), parts)
    heads, lives, targets = [], [], []
    for base, first, size in rounds:
        heads.append(base + jnp.clip(dest - first, 0, size - 1).astype(jnp.int32))
        lives.append(((dest >= first) & (dest < first + size)).astype(jnp.int32))
        targets.append(list(range(first, first + size)))
    mask = allowed_tiles(key_list[0], key_count[0])
    all_heads = jnp.concatenate(heads)
    chunk_count = rows // TILE
    tensors = (query_states[0], key_states[0], value_states[0])

    def send(slots, k):
        moved = [shift(slots[i], "seq", i, parts, targets[k]) for i in range(1, parts)]
        return [slots[0]] + moved

    other = []
    source = output_grad[0]
    for chunk in range(chunk_count):
        if other:
            source, _ = lax.optimization_barrier((source, other[-1]))
        own = source[chunk * TILE : (chunk + 1) * TILE]
        other.append(lax.ppermute(own, "head", [(0, 1), (1, 0)]))
    side = side.astype(jnp.int32).reshape(1)
    blocks = [send(pack(heads[k], tensors), k) for k in range(len(rounds))]
    acc = project_own(side, output_grad[0], w_out)
    chunks = [[] for _ in rounds]
    for chunk in range(chunk_count):
        slots = project_rest(all_heads, 1 - side, other[chunk], w_out, acc, chunk)
        for k in range(len(rounds)):
            chunks[k] += send(slots[k * parts : (k + 1) * parts], k)
    before = None
    for k in range(len(rounds)):
        me_live = jnp.stack([me.astype(jnp.int32), lives[k][0]])
        done = attend(me_live, mask, blocks[k], chunks[k])
        back = [done[0]] + [
            shift_back(done[i], "seq", i, parts, targets[k]) for i in range(1, parts)
        ]
        before = unpack(heads[k], lives[k], back, before, head_count, parts * rows * HD)
    query_grad, key_grad, value_grad, feats = before
    return query_grad[None], key_grad[None], value_grad[None], feats.transpose(1, 2, 0)


def attend_gathered(query_tiles, key_buf, value_buf, grad_tiles, buf_slots, counts):
    score_scale = HD ** (-0.5)
    tile_count, tile_rows, feat_width = query_tiles.shape
    slot_count = buf_slots.shape[1]
    key_span = slot_count * tile_rows
    buf_tiles = key_buf.shape[0]
    key_sel = key_buf[buf_slots].reshape(tile_count, key_span, feat_width)
    value_sel = value_buf[buf_slots].reshape(tile_count, key_span, feat_width)
    allowed = jnp.arange(key_span)[None, :] // tile_rows < counts[:, None]

    def head_step(head_idx, carried):
        query_acc, key_acc, value_acc = carried
        col_start = head_idx * HD
        query_head = lax.dynamic_slice_in_dim(query_tiles, col_start, HD, 2)
        key_head = lax.dynamic_slice_in_dim(key_sel, col_start, HD, 2)
        value_head = lax.dynamic_slice_in_dim(value_sel, col_start, HD, 2)
        grad_head = lax.dynamic_slice_in_dim(grad_tiles, col_start, HD, 2)
        scores = (
            jnp.einsum("iqe,ike->iqk", query_head, key_head, preferred_element_type=jnp.float32)
            * score_scale
        )
        scores = jnp.where(allowed[:, None, :], scores, -jnp.inf)
        row_max = jnp.max(scores, axis=-1, keepdims=True)
        log_norm = row_max + jnp.log(jnp.sum(jnp.exp(scores - row_max), axis=-1, keepdims=True))
        weights = jnp.exp(scores - log_norm)
        weights_b = weights.astype(jnp.bfloat16)
        attn_out = jnp.einsum(
            "iqk,ike->iqe", weights_b, value_head, preferred_element_type=jnp.float32
        ).astype(jnp.bfloat16)
        row_delta = jnp.sum(
            grad_head.astype(jnp.float32) * attn_out.astype(jnp.float32), axis=-1, keepdims=True
        )
        dprob = jnp.einsum(
            "iqe,ike->iqk", grad_head, value_head, preferred_element_type=jnp.float32
        )
        dscore = (weights * (dprob - row_delta)).astype(jnp.bfloat16)
        query_head_grad = score_scale * jnp.einsum(
            "iqk,ike->iqe", dscore, key_head, preferred_element_type=jnp.float32
        )
        key_head_grad = score_scale * jnp.einsum(
            "iqk,iqe->ike", dscore, query_head, preferred_element_type=jnp.float32
        )
        value_head_grad = jnp.einsum(
            "iqk,iqe->ike", weights_b, grad_head, preferred_element_type=jnp.float32
        )
        query_acc = lax.dynamic_update_slice_in_dim(query_acc, query_head_grad, col_start, 2)
        key_acc = lax.dynamic_update_slice_in_dim(key_acc, key_head_grad, col_start, 2)
        value_acc = lax.dynamic_update_slice_in_dim(value_acc, value_head_grad, col_start, 2)
        return (query_acc, key_acc, value_acc)

    start_state = (
        jnp.zeros((tile_count, tile_rows, feat_width), jnp.float32),
        jnp.zeros((tile_count, key_span, feat_width), jnp.float32),
        jnp.zeros((tile_count, key_span, feat_width), jnp.float32),
    )
    query_full, key_sel_grad, value_sel_grad = lax.fori_loop(
        0, feat_width // HD, head_step, start_state
    )
    live_slot = jnp.arange(slot_count)[None, :] < counts[:, None]
    routing = (
        (buf_slots[:, :, None] == jnp.arange(buf_tiles)[None, None, :]) & live_slot[:, :, None]
    ).astype(jnp.float32)
    key_grad_buf = jnp.einsum(
        "imb,imr->br",
        routing,
        key_sel_grad.reshape(tile_count, slot_count, tile_rows * feat_width),
        precision=lax.Precision.HIGHEST,
    )
    value_grad_buf = jnp.einsum(
        "imb,imr->br",
        routing,
        value_sel_grad.reshape(tile_count, slot_count, tile_rows * feat_width),
        precision=lax.Precision.HIGHEST,
    )
    return (
        query_full,
        key_grad_buf.reshape(buf_tiles, tile_rows, feat_width),
        value_grad_buf.reshape(buf_tiles, tile_rows, feat_width),
    )


def head_squares(grads_full, head_count):
    rows = grads_full.reshape(-1, head_count, HD)
    return jnp.sum(rows * rows, axis=(0, 2))


def by_gather(query_states, key_states, value_states, output_grad, w_out, key_list, key_count):
    seq_count = lax.axis_size("seq")
    seq_index = lax.axis_index("seq")
    tok_rows = query_states.shape[1]
    feat_width = query_states.shape[2]
    head_count = feat_width // HD
    tile_count = tok_rows // TILE
    first_tile = seq_index * tile_count
    own_lists = lax.dynamic_slice_in_dim(key_list[0], first_tile, tile_count, 0)
    own_counts = lax.dynamic_slice_in_dim(key_count[0], first_tile, tile_count, 0)
    grad_out = lax.dot_general(
        lax.all_gather(output_grad, "head", axis=2, tiled=True)[0],
        w_out,
        (((1,), (1,)), ((), ())),
        preferred_element_type=jnp.float32,
    ).astype(jnp.bfloat16)
    query_tiles = query_states[0].reshape(tile_count, TILE, feat_width)
    grad_tiles = grad_out.reshape(tile_count, TILE, feat_width)
    key_whole, value_whole = (
        lax.all_gather(key_states, "seq", axis=1, tiled=True),
        lax.all_gather(value_states, "seq", axis=1, tiled=True),
    )
    key_buf = key_whole[0].reshape(-1, TILE, feat_width)
    value_buf = value_whole[0].reshape(-1, TILE, feat_width)
    query_full, key_grad_buf, value_grad_buf = attend_gathered(
        query_tiles, key_buf, value_buf, grad_tiles, own_lists, own_counts
    )
    buf_rows = key_grad_buf.shape[0] * TILE
    key_sum, value_sum = (
        lax.psum_scatter(
            key_grad_buf.reshape(1, buf_rows, feat_width).astype(jnp.bfloat16),
            "seq",
            scatter_dimension=1,
            tiled=True,
        ).astype(jnp.float32),
        lax.psum_scatter(
            value_grad_buf.reshape(1, buf_rows, feat_width).astype(jnp.bfloat16),
            "seq",
            scatter_dimension=1,
            tiled=True,
        ).astype(jnp.float32),
    )
    key_full = key_sum[0]
    value_full = value_sum[0]
    query_rows = query_full.reshape(tok_rows, feat_width)
    local_sums = jnp.stack(
        [
            head_squares(query_rows, head_count),
            head_squares(key_full, head_count),
            head_squares(value_full, head_count),
        ],
        axis=-1,
    )
    total_sums = lax.psum(local_sums, "seq")
    grad_features = jnp.log(total_sums / (seq_count * tok_rows * HD) + 1e-06)
    return (
        query_rows.astype(jnp.bfloat16)[None],
        key_full.astype(jnp.bfloat16)[None],
        value_full.astype(jnp.bfloat16)[None],
        grad_features[None],
    )


def per_device(*args):
    parts, sides = lax.axis_size("seq"), lax.axis_size("head")
    head_count = args[0].shape[2] // HD
    if head_count >= parts > 1 and head_count % 2 == 0 and sides == 2:
        return by_heads(*args)
    return by_gather(*args)


def solution(mesh):
    in_specs = (
        P(("grp", "clip"), "seq", "head"),
        P(("grp", "clip"), "seq", "head"),
        P(("grp", "clip"), "seq", "head"),
        P(("grp", "clip"), "seq", "head"),
        P("head", None),
        P(("grp", "clip"), None, None),
        P(("grp", "clip"), None),
    )
    out_specs = (
        P(("grp", "clip"), "seq", "head"),
        P(("grp", "clip"), "seq", "head"),
        P(("grp", "clip"), "seq", "head"),
        P(("grp", "clip"), "head", None),
    )
    return jax.shard_map(
        per_device, mesh=mesh, in_specs=in_specs, out_specs=out_specs, check_vma=False
    )
```

```python
import functools
import math

import jax
import jax.numpy as jnp
from jax import lax
from jax.experimental import pallas as pl
from jax.experimental.pallas import tpu as pltpu
from jax.sharding import PartitionSpec as P

HD = 128
TILE = 256
STAT_ROWS = 16
SMALL_GRANT = 12 << 20
ATTEND_GRANT = 24 << 20
SMEM = pl.BlockSpec(memory_space=pltpu.SMEM)
VMEM = pl.BlockSpec(memory_space=pltpu.VMEM)
ANY = pl.BlockSpec(memory_space=pl.ANY)
HBM = pl.BlockSpec(memory_space=pltpu.HBM)
NT = (((1,), (1,)), ((), ()))
NN = (((1,), (0,)), ((), ()))
TN = (((0,), (0,)), ((), ()))


def mm(lhs, rhs, dims):
    return lax.dot_general(lhs, rhs, dims, preferred_element_type=jnp.float32)


def stage_kernel(slots, kinds, chunks, heads_ref, *refs):
    tensors = refs[:kinds]
    grad_ref = refs[kinds]
    outs = refs[kinds + 1 : kinds + 1 + slots]
    pieces = refs[kinds + 1 + slots : -2]
    piece_sems, sems = refs[-2:]
    copies = []
    for chunk, piece in enumerate(pieces):
        span = pl.ds(chunk * TILE, TILE)
        copies.append(pltpu.make_async_copy(grad_ref.at[span, :], piece, piece_sems.at[chunk]))
    for slot, out in enumerate(outs):
        cols = pl.ds(pl.multiple_of(heads_ref[slot] * HD, HD), HD)
        for j, tensor in enumerate(tensors):
            copies.append(pltpu.make_async_copy(tensor.at[:, cols], out.at[j], sems.at[slot, j]))
    for copy in copies:
        copy.start()
    for copy in copies:
        copy.wait()


def stage(heads, tensors, grad):
    rows = grad.shape[0]
    slots, kinds, chunks = heads.shape[0], len(tensors), rows // TILE
    held = [pltpu.with_memory_space_constraint(arr, pltpu.HBM) for arr in (*tensors, grad)]
    outs = pl.pallas_call(
        functools.partial(stage_kernel, slots, kinds, chunks),
        out_shape=[pltpu.VMEM((kinds, rows, HD), grad.dtype)] * slots
        + [pltpu.VMEM((TILE, grad.shape[1]), grad.dtype)] * chunks,
        in_specs=[SMEM] + [HBM] * (kinds + 1),
        out_specs=[VMEM] * (slots + chunks),
        scratch_shapes=[
            pltpu.SemaphoreType.DMA((chunks,)),
            pltpu.SemaphoreType.DMA((slots, kinds)),
        ],
        compiler_params=pltpu.CompilerParams(vmem_limit_bytes=SMALL_GRANT),
        cost_estimate=pl.CostEstimate(
            flops=0, transcendentals=0, bytes_accessed=4 * (kinds * slots * rows * HD + grad.size)
        ),
        name="stage_inputs",
    )(heads, *held)
    return outs[:slots], outs[slots:]


def pack_kernel(slots, heads_ref, q_ref, k_ref, v_ref, *refs):
    outs = refs[len(refs) - slots :]
    chunks = len(refs) // slots - 1
    for slot, out in enumerate(outs):
        cols = pl.ds(pl.multiple_of(heads_ref[slot] * HD, HD), HD)
        out[0] = q_ref[:, cols]
        out[1] = k_ref[:, cols]
        out[2] = v_ref[:, cols]
        for chunk in range(chunks):
            out[3, chunk * TILE : (chunk + 1) * TILE, :] = refs[chunk * slots + slot][...]


def pack(heads, query, key, value, grads):
    rows = query.shape[0]
    slots = heads.shape[0]
    kinds = 4 if grads else 3
    return pl.pallas_call(
        functools.partial(pack_kernel, slots),
        out_shape=[jax.ShapeDtypeStruct((kinds, rows, HD), query.dtype)] * slots,
        in_specs=[SMEM, VMEM, VMEM, VMEM] + [VMEM] * len(grads),
        out_specs=[VMEM] * slots,
        compiler_params=pltpu.CompilerParams(vmem_limit_bytes=SMALL_GRANT),
        cost_estimate=pl.CostEstimate(
            flops=0, transcendentals=0, bytes_accessed=6 * (query.size + slots * rows * HD)
        ),
        name="pack_heads",
    )(heads, query, key, value, *grads)


def project_own_kernel(src_ref, grad_ref, w_ref, out):
    out[0] = mm(grad_ref[...], w_ref[...], NT)


def project_own(src, grads, w_out):
    rows, feats = grads.shape
    width = w_out.shape[0]
    steps = width // (2 * HD)
    return pl.pallas_call(
        project_own_kernel,
        out_shape=jax.ShapeDtypeStruct((steps, rows, 2 * HD), jnp.float32),
        grid_spec=pltpu.PrefetchScalarGridSpec(
            num_scalar_prefetch=1,
            grid=(steps,),
            in_specs=[
                pl.BlockSpec((rows, feats), lambda s, src: (0, 0)),
                pl.BlockSpec((2 * HD, feats), lambda s, src: (s, src[0])),
            ],
            out_specs=pl.BlockSpec((1, rows, 2 * HD), lambda s, src: (s, 0, 0)),
        ),
        compiler_params=pltpu.CompilerParams(vmem_limit_bytes=SMALL_GRANT),
        cost_estimate=pl.CostEstimate(
            flops=2 * rows * feats * width,
            transcendentals=0,
            bytes_accessed=2 * (grads.size + width * feats) + 4 * rows * width,
        ),
        name="project_own",
    )(src, grads, w_out)


def project_rest_kernel(heads_ref, src_ref, grad_ref, w_ref, acc_ref, *refs):
    outs, held = refs[:-1], refs[-1]
    total = mm(grad_ref[...], w_ref[...], NT) + acc_ref[0]
    step = pl.program_id(0)
    for half in range(2):
        held[2 * step + half] = total[:, half * HD : (half + 1) * HD].astype(jnp.bfloat16)

    @pl.when(step == pl.num_programs(0) - 1)
    def _():
        for slot, out in enumerate(outs):
            out[...] = held[heads_ref[slot]]


def project_rest(heads, src, grads, w_out, acc, chunk):
    rows, feats = grads.shape
    slots = heads.shape[0]
    width = w_out.shape[0]
    steps = width // (2 * HD)
    return pl.pallas_call(
        project_rest_kernel,
        out_shape=[jax.ShapeDtypeStruct((rows, HD), jnp.bfloat16)] * slots,
        grid_spec=pltpu.PrefetchScalarGridSpec(
            num_scalar_prefetch=2,
            grid=(steps,),
            in_specs=[
                pl.BlockSpec((rows, feats), lambda s, heads, src: (0, 0)),
                pl.BlockSpec((2 * HD, feats), lambda s, heads, src: (s, src[0])),
                pl.BlockSpec((1, rows, 2 * HD), lambda s, heads, src: (s, chunk, 0)),
            ],
            out_specs=[pl.BlockSpec((rows, HD), lambda s, heads, src: (0, 0))] * slots,
            scratch_shapes=[pltpu.VMEM((width // HD, rows, HD), jnp.bfloat16)],
        ),
        compiler_params=pltpu.CompilerParams(vmem_limit_bytes=SMALL_GRANT),
        cost_estimate=pl.CostEstimate(
            flops=2 * rows * feats * width,
            transcendentals=0,
            bytes_accessed=2 * (grads.size + width * feats) + 6 * rows * width,
        ),
        name="project_rest",
    )(heads, src, grads, w_out, acc)


def attend_kernel(parts, tiles_dev, me_ref, mask_ref, *refs):
    @pl.when(me_ref[1] != 0)
    def _():
        attend_body(parts, tiles_dev, me_ref, mask_ref, *refs)


def attend_body(parts, tiles_dev, me_ref, mask_ref, *refs):
    tiles = parts * tiles_dev
    rows = tiles_dev * TILE
    blocks = refs[:parts]
    chunks = refs[parts : len(refs) - parts - 14]
    outs = refs[len(refs) - parts - 14 : len(refs) - 14]
    q_s, k_s, v_s, g_s, dk_s, dv_s, dq_s, e_s, dp_s, ds_s, m_s, l_s, d_s, sems = refs[-14:]
    score_scale = HD ** (-0.5)
    expo = score_scale * math.log2(math.e)
    me = me_ref[0]
    copies = []
    for part in range(parts):
        span = pl.ds(part * rows, rows)
        pairs = [(blocks[part].at[j], held.at[span]) for j, held in enumerate((q_s, k_s, v_s))]
        if chunks:
            for sub in range(tiles_dev):
                span = pl.ds(part * rows + sub * TILE, TILE)
                pairs.append((chunks[sub * parts + part], g_s.at[span]))
        else:
            pairs.append((blocks[part].at[3], g_s.at[span]))
        for j, (source, held) in enumerate(pairs):
            copies.append(pltpu.make_async_copy(source, held, sems.at[part, j]))
    for copy in copies:
        copy.start()
    for copy in copies:
        copy.wait()
    dk_s[...] = jnp.zeros_like(dk_s)
    dv_s[...] = jnp.zeros_like(dv_s)

    def home(part):
        return lax.rem(me - part + parts, parts) * tiles_dev

    def query_step(part, query_sq):
        own = home(part)
        span = pl.ds(pl.multiple_of(part * rows, rows), rows)
        query = q_s[span, :]
        grad = g_s[span, :]
        for ki in range(tiles):
            place = home(ki // tiles_dev) + ki % tiles_dev
            scores = mm(k_s[ki * TILE : (ki + 1) * TILE, :], query, NT)
            dprob = mm(v_s[ki * TILE : (ki + 1) * TILE, :], grad, NT)
            top = jnp.max(scores, axis=0, keepdims=True)
            weight = jnp.exp2((scores - top) * expo)
            for sub in range(tiles_dev):
                cols = slice(sub * TILE, (sub + 1) * TILE)
                live = mask_ref[own + sub, place] != 0
                m_s[ki : ki + 1, cols] = jnp.where(live, top[:, cols], -jnp.inf)
            l_s[ki : ki + 1, :] = jnp.sum(weight, axis=0, keepdims=True)
            d_s[ki : ki + 1, :] = jnp.sum(weight * dprob, axis=0, keepdims=True)
            e_s[ki] = weight
            dp_s[ki] = dprob

        tops = m_s[...]
        factor = jnp.exp2((tops - jnp.max(tops, axis=0, keepdims=True)) * expo)
        norm = jnp.sum(l_s[...] * factor, axis=0, keepdims=True)
        delta = jnp.sum(d_s[...] * factor, axis=0, keepdims=True) / norm
        m_s[...] = factor / norm
        for ki in range(tiles):
            weight = e_s[ki] * m_s[ki : ki + 1, :]
            dscore = (weight * (dp_s[ki] - delta)).astype(jnp.bfloat16)
            dv_s[ki] += mm(weight.astype(jnp.bfloat16), grad, NN)
            dk_s[ki] += mm(dscore, query, NN)
            ds_s[ki * TILE : (ki + 1) * TILE, :] = dscore

        query_full = mm(ds_s[...], k_s[...], TN) * score_scale
        dq_s[part] = query_full.astype(jnp.bfloat16)
        return query_sq + jnp.sum(query_full * query_full, axis=0, keepdims=True)

    query_sq = lax.fori_loop(0, parts, query_step, jnp.zeros((1, HD), jnp.float32))
    key_sq = jnp.zeros((1, HD), jnp.float32)
    value_sq = jnp.zeros((1, HD), jnp.float32)
    for part in range(parts):
        for sub in range(tiles_dev):
            tile = part * tiles_dev + sub
            key_full = dk_s[tile] * score_scale
            value_full = dv_s[tile]
            key_sq = key_sq + jnp.sum(key_full * key_full, axis=0, keepdims=True)
            value_sq = value_sq + jnp.sum(value_full * value_full, axis=0, keepdims=True)
            low = sub * TILE
            outs[part][low : low + TILE, :] = dq_s[part, low : low + TILE, :]
            outs[part][rows + low : rows + low + TILE, :] = key_full.astype(jnp.bfloat16)
            outs[part][2 * rows + low : 2 * rows + low + TILE, :] = value_full.astype(jnp.bfloat16)
    row = lax.broadcasted_iota(jnp.int32, (STAT_ROWS, HD), 0)
    total = jnp.where(
        row < 3,
        jnp.sum(query_sq, axis=1, keepdims=True),
        jnp.where(
            row < 6,
            jnp.sum(key_sq, axis=1, keepdims=True),
            jnp.sum(value_sq, axis=1, keepdims=True),
        ),
    )
    high = total.astype(jnp.bfloat16).astype(jnp.float32)
    mid = (total - high).astype(jnp.bfloat16).astype(jnp.float32)
    low = total - high - mid
    piece = lax.rem(row, 3)
    stats = jnp.where(piece == 0, high, jnp.where(piece == 1, mid, low)).astype(jnp.bfloat16)
    for part in range(parts):
        outs[part][3 * rows :, :] = stats


def attend(me, mask, blocks, chunks):
    parts = len(blocks)
    rows = blocks[0].shape[1]
    tiles_dev = rows // TILE
    tiles = parts * tiles_dev
    bf16, f32 = jnp.bfloat16, jnp.float32
    pairs = tiles * tiles
    return pl.pallas_call(
        functools.partial(attend_kernel, parts, tiles_dev),
        out_shape=[jax.ShapeDtypeStruct((3 * rows + STAT_ROWS, HD), bf16)] * parts,
        in_specs=[SMEM, SMEM] + [ANY] * (parts + len(chunks)),
        out_specs=[VMEM] * parts,
        scratch_shapes=[
            pltpu.VMEM((parts * rows, HD), bf16),
            pltpu.VMEM((parts * rows, HD), bf16),
            pltpu.VMEM((parts * rows, HD), bf16),
            pltpu.VMEM((parts * rows, HD), bf16),
            pltpu.VMEM((tiles, TILE, HD), f32),
            pltpu.VMEM((tiles, TILE, HD), f32),
            pltpu.VMEM((parts, rows, HD), bf16),
            pltpu.VMEM((tiles, TILE, rows), f32),
            pltpu.VMEM((tiles, TILE, rows), f32),
            pltpu.VMEM((tiles * TILE, rows), bf16),
            pltpu.VMEM((tiles, rows), f32),
            pltpu.VMEM((tiles, rows), f32),
            pltpu.VMEM((tiles, rows), f32),
            pltpu.SemaphoreType.DMA((parts, 3 + tiles_dev)),
        ],
        cost_estimate=pl.CostEstimate(
            flops=pairs * 10 * TILE * TILE * HD,
            transcendentals=pairs * TILE * TILE,
            bytes_accessed=2 * 7 * parts * rows * HD,
        ),
        compiler_params=pltpu.CompilerParams(vmem_limit_bytes=ATTEND_GRANT),
        name="attend_head",
    )(me, mask, *blocks, *chunks)


def unpack_kernel(parts, rows, count, fresh, heads_ref, live_ref, *refs):
    blocks = refs[:parts]
    rest = refs[parts:]
    feats = None
    if not fresh:
        feats = rest[3][...]
        rest = rest[4:]
    outs = rest[:3]
    feat_out = rest[3]
    sems = rest[4]
    if fresh:
        feats = jnp.zeros(feat_out.shape, jnp.float32)

    def copies(slot):
        cols = pl.ds(pl.multiple_of(heads_ref[slot] * HD, HD), HD)
        return [
            pltpu.make_async_copy(
                blocks[slot].at[pl.ds(j * rows, rows), :], outs[j].at[:, cols], sems.at[slot, j]
            )
            for j in range(3)
        ]

    for slot in range(parts):
        @pl.when(live_ref[slot] != 0)
        def _():
            for copy in copies(slot):
                copy.start()

    row = lax.broadcasted_iota(jnp.int32, feat_out.shape, 2)
    col = lax.broadcasted_iota(jnp.int32, feat_out.shape, 0)
    for slot in range(parts):
        stats = blocks[slot][3 * rows :, :].astype(jnp.float32)
        here = (row == heads_ref[slot]) & (live_ref[slot] != 0)
        for j in range(3):
            total = stats[3 * j : 3 * j + 1, :] + stats[3 * j + 1 : 3 * j + 2, :]
            total = total + stats[3 * j + 2 : 3 * j + 3, :]
            value = jnp.log(total / count + 1e-06)[:, : feat_out.shape[2]]
            feats = jnp.where(here & (col == j), value[None], feats)
    feat_out[...] = feats
    for slot in range(parts):
        @pl.when(live_ref[slot] != 0)
        def _():
            for copy in copies(slot):
                copy.wait()


def unpack(heads, live, blocks, before, head_count, count):
    parts = len(blocks)
    rows = (blocks[0].shape[0] - STAT_ROWS) // 3
    fresh = before is None
    kept = [] if fresh else list(before)
    big = jax.ShapeDtypeStruct((rows, head_count * HD), jnp.bfloat16)
    return pl.pallas_call(
        functools.partial(unpack_kernel, parts, rows, count, fresh),
        out_shape=[big, big, big, jax.ShapeDtypeStruct((3, 1, head_count), jnp.float32)],
        in_specs=[SMEM, SMEM] + [VMEM] * parts + ([] if fresh else [ANY, ANY, ANY, VMEM]),
        out_specs=[ANY, ANY, ANY, VMEM],
        scratch_shapes=[pltpu.SemaphoreType.DMA((parts, 3))],
        input_output_aliases={} if fresh else {2 + parts + j: j for j in range(3)},
        compiler_params=pltpu.CompilerParams(vmem_limit_bytes=SMALL_GRANT),
        cost_estimate=pl.CostEstimate(
            flops=0, transcendentals=0, bytes_accessed=12 * parts * rows * HD
        ),
        name="unpack_heads",
    )(heads, live, *blocks, *kept)


def shift(arr, axis, step, size, targets):
    pairs = [(s, (s + step) % size) for s in range(size) if (s + step) % size in targets]
    return lax.ppermute(arr, axis, pairs)


def shift_back(arr, axis, step, size, sources):
    return lax.ppermute(arr, axis, [(s, (s - step) % size) for s in sources])


def allowed_tiles(key_list, key_count):
    tiles, slots = key_list.shape
    live = jnp.arange(slots)[None, :] < key_count[:, None]
    hit = (key_list[:, :, None] == jnp.arange(tiles)[None, None, :]) & live[:, :, None]
    return jnp.any(hit, axis=1).astype(jnp.int32)


def by_heads(query_states, key_states, value_states, output_grad, w_out, key_list, key_count):
    parts = lax.axis_size("seq")
    me = lax.axis_index("seq")
    side = lax.axis_index("head")
    rows, width = query_states.shape[1:]
    head_count = width // HD
    full, extra = divmod(head_count, parts)
    low = (parts - extra) // 2
    rounds = [(k * parts, 0, parts) for k in range(full)]
    if extra:
        rounds.append((full * parts, low, extra))
    dest = lax.rem(me + jnp.arange(parts, dtype=jnp.int32), parts)
    heads, lives, targets = [], [], []
    for base, first, size in rounds:
        heads.append(base + jnp.clip(dest - first, 0, size - 1).astype(jnp.int32))
        lives.append(((dest >= first) & (dest < first + size)).astype(jnp.int32))
        targets.append(list(range(first, first + size)))
    mask = allowed_tiles(key_list[0], key_count[0])
    all_heads = jnp.concatenate(heads)
    chunk_count = rows // TILE
    tensors = (query_states[0], key_states[0], value_states[0])
    slots, pieces = stage(heads[0], tensors, output_grad[0])
    other = []
    for own in pieces:
        if other:
            own, _ = lax.optimization_barrier((own, other[-1]))
        other.append(lax.ppermute(own, "head", [(0, 1), (1, 0)]))
    side = side.astype(jnp.int32).reshape(1)
    blocks = [slots[0]] + [shift(slots[i], "seq", i, parts, targets[0]) for i in range(1, parts)]
    acc = project_own(side, output_grad[0], w_out)
    projected = [
        project_rest(all_heads, 1 - side, other[chunk], w_out, acc, chunk)
        for chunk in range(chunk_count)
    ]
    chunks = []
    for slots in projected:
        chunks += [slots[0]]
        chunks += [shift(slots[i], "seq", i, parts, targets[0]) for i in range(1, parts)]
    before = None
    for k in range(len(rounds)):
        me_live = jnp.stack([me.astype(jnp.int32), lives[k][0]])
        ready = (blocks, chunks[:parts])
        done = attend(me_live, mask, blocks, chunks)
        if k + 1 < len(rounds):
            grads = [slot for slots in projected for slot in slots[(k + 1) * parts : (k + 2) * parts]]
            slots = pack(heads[k + 1], *tensors, grads)
            slots, _ = lax.optimization_barrier((slots, ready))
            blocks = [slots[0]] + [
                shift(slots[i], "seq", i, parts, targets[k + 1]) for i in range(1, parts)
            ]
            chunks = []
        back = [done[0]] + [
            shift_back(done[i], "seq", i, parts, targets[k]) for i in range(1, parts)
        ]
        before = unpack(heads[k], lives[k], back, before, head_count, parts * rows * HD)
    query_grad, key_grad, value_grad, feats = before
    return query_grad[None], key_grad[None], value_grad[None], feats.transpose(1, 2, 0)


def attend_gathered(query_tiles, key_buf, value_buf, grad_tiles, buf_slots, counts):
    score_scale = HD ** (-0.5)
    tile_count, tile_rows, feat_width = query_tiles.shape
    slot_count = buf_slots.shape[1]
    key_span = slot_count * tile_rows
    buf_tiles = key_buf.shape[0]
    key_sel = key_buf[buf_slots].reshape(tile_count, key_span, feat_width)
    value_sel = value_buf[buf_slots].reshape(tile_count, key_span, feat_width)
    allowed = jnp.arange(key_span)[None, :] // tile_rows < counts[:, None]

    def head_step(head_idx, carried):
        query_acc, key_acc, value_acc = carried
        col_start = head_idx * HD
        query_head = lax.dynamic_slice_in_dim(query_tiles, col_start, HD, 2)
        key_head = lax.dynamic_slice_in_dim(key_sel, col_start, HD, 2)
        value_head = lax.dynamic_slice_in_dim(value_sel, col_start, HD, 2)
        grad_head = lax.dynamic_slice_in_dim(grad_tiles, col_start, HD, 2)
        scores = (
            jnp.einsum("iqe,ike->iqk", query_head, key_head, preferred_element_type=jnp.float32)
            * score_scale
        )
        scores = jnp.where(allowed[:, None, :], scores, -jnp.inf)
        row_max = jnp.max(scores, axis=-1, keepdims=True)
        log_norm = row_max + jnp.log(jnp.sum(jnp.exp(scores - row_max), axis=-1, keepdims=True))
        weights = jnp.exp(scores - log_norm)
        weights_b = weights.astype(jnp.bfloat16)
        attn_out = jnp.einsum(
            "iqk,ike->iqe", weights_b, value_head, preferred_element_type=jnp.float32
        ).astype(jnp.bfloat16)
        row_delta = jnp.sum(
            grad_head.astype(jnp.float32) * attn_out.astype(jnp.float32), axis=-1, keepdims=True
        )
        dprob = jnp.einsum(
            "iqe,ike->iqk", grad_head, value_head, preferred_element_type=jnp.float32
        )
        dscore = (weights * (dprob - row_delta)).astype(jnp.bfloat16)
        query_head_grad = score_scale * jnp.einsum(
            "iqk,ike->iqe", dscore, key_head, preferred_element_type=jnp.float32
        )
        key_head_grad = score_scale * jnp.einsum(
            "iqk,iqe->ike", dscore, query_head, preferred_element_type=jnp.float32
        )
        value_head_grad = jnp.einsum(
            "iqk,iqe->ike", weights_b, grad_head, preferred_element_type=jnp.float32
        )
        query_acc = lax.dynamic_update_slice_in_dim(query_acc, query_head_grad, col_start, 2)
        key_acc = lax.dynamic_update_slice_in_dim(key_acc, key_head_grad, col_start, 2)
        value_acc = lax.dynamic_update_slice_in_dim(value_acc, value_head_grad, col_start, 2)
        return (query_acc, key_acc, value_acc)

    start_state = (
        jnp.zeros((tile_count, tile_rows, feat_width), jnp.float32),
        jnp.zeros((tile_count, key_span, feat_width), jnp.float32),
        jnp.zeros((tile_count, key_span, feat_width), jnp.float32),
    )
    query_full, key_sel_grad, value_sel_grad = lax.fori_loop(
        0, feat_width // HD, head_step, start_state
    )
    live_slot = jnp.arange(slot_count)[None, :] < counts[:, None]
    routing = (
        (buf_slots[:, :, None] == jnp.arange(buf_tiles)[None, None, :]) & live_slot[:, :, None]
    ).astype(jnp.float32)
    key_grad_buf = jnp.einsum(
        "imb,imr->br",
        routing,
        key_sel_grad.reshape(tile_count, slot_count, tile_rows * feat_width),
        precision=lax.Precision.HIGHEST,
    )
    value_grad_buf = jnp.einsum(
        "imb,imr->br",
        routing,
        value_sel_grad.reshape(tile_count, slot_count, tile_rows * feat_width),
        precision=lax.Precision.HIGHEST,
    )
    return (
        query_full,
        key_grad_buf.reshape(buf_tiles, tile_rows, feat_width),
        value_grad_buf.reshape(buf_tiles, tile_rows, feat_width),
    )


def head_squares(grads_full, head_count):
    rows = grads_full.reshape(-1, head_count, HD)
    return jnp.sum(rows * rows, axis=(0, 2))


def by_gather(query_states, key_states, value_states, output_grad, w_out, key_list, key_count):
    seq_count = lax.axis_size("seq")
    seq_index = lax.axis_index("seq")
    tok_rows = query_states.shape[1]
    feat_width = query_states.shape[2]
    head_count = feat_width // HD
    tile_count = tok_rows // TILE
    first_tile = seq_index * tile_count
    own_lists = lax.dynamic_slice_in_dim(key_list[0], first_tile, tile_count, 0)
    own_counts = lax.dynamic_slice_in_dim(key_count[0], first_tile, tile_count, 0)
    grad_out = lax.dot_general(
        lax.all_gather(output_grad, "head", axis=2, tiled=True)[0],
        w_out,
        (((1,), (1,)), ((), ())),
        preferred_element_type=jnp.float32,
    ).astype(jnp.bfloat16)
    query_tiles = query_states[0].reshape(tile_count, TILE, feat_width)
    grad_tiles = grad_out.reshape(tile_count, TILE, feat_width)
    key_whole, value_whole = (
        lax.all_gather(key_states, "seq", axis=1, tiled=True),
        lax.all_gather(value_states, "seq", axis=1, tiled=True),
    )
    key_buf = key_whole[0].reshape(-1, TILE, feat_width)
    value_buf = value_whole[0].reshape(-1, TILE, feat_width)
    query_full, key_grad_buf, value_grad_buf = attend_gathered(
        query_tiles, key_buf, value_buf, grad_tiles, own_lists, own_counts
    )
    buf_rows = key_grad_buf.shape[0] * TILE
    key_sum, value_sum = (
        lax.psum_scatter(
            key_grad_buf.reshape(1, buf_rows, feat_width).astype(jnp.bfloat16),
            "seq",
            scatter_dimension=1,
            tiled=True,
        ).astype(jnp.float32),
        lax.psum_scatter(
            value_grad_buf.reshape(1, buf_rows, feat_width).astype(jnp.bfloat16),
            "seq",
            scatter_dimension=1,
            tiled=True,
        ).astype(jnp.float32),
    )
    key_full = key_sum[0]
    value_full = value_sum[0]
    query_rows = query_full.reshape(tok_rows, feat_width)
    local_sums = jnp.stack(
        [
            head_squares(query_rows, head_count),
            head_squares(key_full, head_count),
            head_squares(value_full, head_count),
        ],
        axis=-1,
    )
    total_sums = lax.psum(local_sums, "seq")
    grad_features = jnp.log(total_sums / (seq_count * tok_rows * HD) + 1e-06)
    return (
        query_rows.astype(jnp.bfloat16)[None],
        key_full.astype(jnp.bfloat16)[None],
        value_full.astype(jnp.bfloat16)[None],
        grad_features[None],
    )


def per_device(*args):
    parts, sides = lax.axis_size("seq"), lax.axis_size("head")
    head_count = args[0].shape[2] // HD
    if head_count >= parts > 1 and head_count % 2 == 0 and sides == 2:
        return by_heads(*args)
    return by_gather(*args)


def solution(mesh):
    in_specs = (
        P(("grp", "clip"), "seq", "head"),
        P(("grp", "clip"), "seq", "head"),
        P(("grp", "clip"), "seq", "head"),
        P(("grp", "clip"), "seq", "head"),
        P("head", None),
        P(("grp", "clip"), None, None),
        P(("grp", "clip"), None),
    )
    out_specs = (
        P(("grp", "clip"), "seq", "head"),
        P(("grp", "clip"), "seq", "head"),
        P(("grp", "clip"), "seq", "head"),
        P(("grp", "clip"), "head", None),
    )
    return jax.shard_map(
        per_device, mesh=mesh, in_specs=in_specs, out_specs=out_specs, check_vma=False
    )
```

```python
import functools
import math

import jax
import jax.numpy as jnp
from jax import lax
from jax.experimental import pallas as pl
from jax.experimental.pallas import tpu as pltpu
from jax.sharding import PartitionSpec as P


HD = 128
TILE = 256
STAT_ROWS = 16
SMALL_GRANT = 12 << 20
ATTEND_GRANT = 24 << 20
SMEM = pl.BlockSpec(memory_space=pltpu.SMEM)
VMEM = pl.BlockSpec(memory_space=pltpu.VMEM)
ANY = pl.BlockSpec(memory_space=pl.ANY)
HBM = pl.BlockSpec(memory_space=pltpu.HBM)
NT = (((1,), (1,)), ((), ()))
NN = (((1,), (0,)), ((), ()))
TN = (((0,), (0,)), ((), ()))


def mm(lhs, rhs, dims):
    return lax.dot_general(lhs, rhs, dims, preferred_element_type=jnp.float32)


def stage_kernel(slots, kinds, chunks, heads_ref, *refs):
    tensors = refs[:kinds]
    grad_ref = refs[kinds]
    outs = refs[kinds + 1 : -1]
    sems = refs[-1]
    copies = []
    for piece, chunk in enumerate(chunks):
        span = pl.ds(chunk * TILE, TILE)
        copies.append(
            pltpu.make_async_copy(grad_ref.at[span, :], outs[len(slots) + piece], sems.at[piece, kinds])
        )
    for index, slot in enumerate(slots):
        cols = pl.ds(pl.multiple_of(heads_ref[slot] * HD, HD), HD)
        for j, tensor in enumerate(tensors):
            copies.append(
                pltpu.make_async_copy(tensor.at[:, cols], outs[index].at[j], sems.at[index, j])
            )
    for copy in copies:
        copy.start()
    for copy in copies:
        copy.wait()


def stage(heads, tensors, grad, slots, chunks):
    rows = grad.shape[0]
    kinds = len(tensors)
    held = [pltpu.with_memory_space_constraint(arr, pltpu.HBM) for arr in (*tensors, grad)]
    outs = pl.pallas_call(
        functools.partial(stage_kernel, slots, kinds, chunks),
        out_shape=[pltpu.VMEM((kinds, rows, HD), grad.dtype)] * len(slots)
        + [pltpu.VMEM((TILE, grad.shape[1]), grad.dtype)] * len(chunks),
        in_specs=[SMEM] + [HBM] * (kinds + 1),
        out_specs=[VMEM] * (len(slots) + len(chunks)),
        scratch_shapes=[pltpu.SemaphoreType.DMA((max(len(slots), len(chunks)), kinds + 1))],
        compiler_params=pltpu.CompilerParams(vmem_limit_bytes=SMALL_GRANT),
        cost_estimate=pl.CostEstimate(
            flops=0,
            transcendentals=0,
            bytes_accessed=4 * (len(slots) * kinds * rows * HD + len(chunks) * TILE * grad.shape[1]),
        ),
        name="stage_inputs",
    )(heads, *held)
    return outs[: len(slots)], outs[len(slots) :]


def pack_kernel(slots, heads_ref, q_ref, k_ref, v_ref, *refs):
    outs = refs[len(refs) - slots :]
    chunks = len(refs) // slots - 1
    for slot, out in enumerate(outs):
        cols = pl.ds(pl.multiple_of(heads_ref[slot] * HD, HD), HD)
        out[0] = q_ref[:, cols]
        out[1] = k_ref[:, cols]
        out[2] = v_ref[:, cols]
        for chunk in range(chunks):
            out[3, chunk * TILE : (chunk + 1) * TILE, :] = refs[chunk * slots + slot][...]


def pack(heads, query, key, value, grads):
    rows = query.shape[0]
    slots = heads.shape[0]
    kinds = 4 if grads else 3
    return pl.pallas_call(
        functools.partial(pack_kernel, slots),
        out_shape=[jax.ShapeDtypeStruct((kinds, rows, HD), query.dtype)] * slots,
        in_specs=[SMEM, VMEM, VMEM, VMEM] + [VMEM] * len(grads),
        out_specs=[VMEM] * slots,
        compiler_params=pltpu.CompilerParams(vmem_limit_bytes=SMALL_GRANT),
        cost_estimate=pl.CostEstimate(
            flops=0, transcendentals=0, bytes_accessed=6 * (query.size + slots * rows * HD)
        ),
        name="pack_heads",
    )(heads, query, key, value, *grads)


def project_own_kernel(src_ref, grad_ref, w_ref, out):
    out[0] = mm(grad_ref[...], w_ref[...], NT)


def project_own(src, grads, w_out):
    rows, feats = grads.shape
    width = w_out.shape[0]
    steps = width // (2 * HD)
    return pl.pallas_call(
        project_own_kernel,
        out_shape=jax.ShapeDtypeStruct((steps, rows, 2 * HD), jnp.float32),
        grid_spec=pltpu.PrefetchScalarGridSpec(
            num_scalar_prefetch=1,
            grid=(steps,),
            in_specs=[
                pl.BlockSpec((rows, feats), lambda s, src: (0, 0)),
                pl.BlockSpec((2 * HD, feats), lambda s, src: (s, src[0])),
            ],
            out_specs=pl.BlockSpec((1, rows, 2 * HD), lambda s, src: (s, 0, 0)),
        ),
        compiler_params=pltpu.CompilerParams(vmem_limit_bytes=SMALL_GRANT),
        cost_estimate=pl.CostEstimate(
            flops=2 * rows * feats * width,
            transcendentals=0,
            bytes_accessed=2 * (grads.size + width * feats) + 4 * rows * width,
        ),
        name="project_own",
    )(src, grads, w_out)


def project_rest_kernel(heads_ref, src_ref, grad_ref, w_ref, acc_ref, *refs):
    outs, held = refs[:-1], refs[-1]
    total = mm(grad_ref[...], w_ref[...], NT) + acc_ref[0]
    step = pl.program_id(0)
    for half in range(2):
        held[2 * step + half] = total[:, half * HD : (half + 1) * HD].astype(jnp.bfloat16)

    @pl.when(step == pl.num_programs(0) - 1)
    def _():
        for slot, out in enumerate(outs):
            out[...] = held[heads_ref[slot]]


def project_rest(heads, src, grads, w_out, acc, chunk):
    rows, feats = grads.shape
    slots = heads.shape[0]
    width = w_out.shape[0]
    steps = width // (2 * HD)
    return pl.pallas_call(
        project_rest_kernel,
        out_shape=[jax.ShapeDtypeStruct((rows, HD), jnp.bfloat16)] * slots,
        grid_spec=pltpu.PrefetchScalarGridSpec(
            num_scalar_prefetch=2,
            grid=(steps,),
            in_specs=[
                pl.BlockSpec((rows, feats), lambda s, heads, src: (0, 0)),
                pl.BlockSpec((2 * HD, feats), lambda s, heads, src: (s, src[0])),
                pl.BlockSpec((1, rows, 2 * HD), lambda s, heads, src: (s, chunk, 0)),
            ],
            out_specs=[pl.BlockSpec((rows, HD), lambda s, heads, src: (0, 0))] * slots,
            scratch_shapes=[pltpu.VMEM((width // HD, rows, HD), jnp.bfloat16)],
        ),
        compiler_params=pltpu.CompilerParams(vmem_limit_bytes=SMALL_GRANT),
        cost_estimate=pl.CostEstimate(
            flops=2 * rows * feats * width,
            transcendentals=0,
            bytes_accessed=2 * (grads.size + width * feats) + 6 * rows * width,
        ),
        name="project_rest",
    )(heads, src, grads, w_out, acc)


def attend_kernel(parts, tiles_dev, me_ref, mask_ref, *refs):
    @pl.when(me_ref[1] != 0)
    def _():
        attend_body(parts, tiles_dev, me_ref, mask_ref, *refs)


def attend_body(parts, tiles_dev, me_ref, mask_ref, *refs):
    tiles = parts * tiles_dev
    rows = tiles_dev * TILE
    blocks = refs[:parts]
    chunks = refs[parts : len(refs) - parts - 14]
    outs = refs[len(refs) - parts - 14 : len(refs) - 14]
    q_s, k_s, v_s, g_s, dk_s, dv_s, dq_s, e_s, dp_s, ds_s, m_s, l_s, d_s, sems = refs[-14:]
    score_scale = HD ** (-0.5)
    expo = score_scale * math.log2(math.e)
    me = me_ref[0]
    copies = []
    for part in range(parts):
        span = pl.ds(part * rows, rows)
        pairs = [(blocks[part].at[j], held.at[span]) for j, held in enumerate((q_s, k_s, v_s))]
        if chunks:
            for sub in range(tiles_dev):
                span = pl.ds(part * rows + sub * TILE, TILE)
                pairs.append((chunks[sub * parts + part], g_s.at[span]))
        else:
            pairs.append((blocks[part].at[3], g_s.at[span]))
        for j, (source, held) in enumerate(pairs):
            copies.append(pltpu.make_async_copy(source, held, sems.at[part, j]))
    for copy in copies:
        copy.start()
    for copy in copies:
        copy.wait()
    dk_s[...] = jnp.zeros_like(dk_s)
    dv_s[...] = jnp.zeros_like(dv_s)

    def home(part):
        return lax.rem(me - part + parts, parts) * tiles_dev

    def query_step(part, query_sq):
        own = home(part)
        span = pl.ds(pl.multiple_of(part * rows, rows), rows)
        query = q_s[span, :]
        grad = g_s[span, :]
        for ki in range(tiles):
            place = home(ki // tiles_dev) + ki % tiles_dev
            scores = mm(k_s[ki * TILE : (ki + 1) * TILE, :], query, NT)
            dprob = mm(v_s[ki * TILE : (ki + 1) * TILE, :], grad, NT)
            top = jnp.max(scores, axis=0, keepdims=True)
            weight = jnp.exp2((scores - top) * expo)
            for sub in range(tiles_dev):
                cols = slice(sub * TILE, (sub + 1) * TILE)
                live = mask_ref[own + sub, place] != 0
                m_s[ki : ki + 1, cols] = jnp.where(live, top[:, cols], -jnp.inf)
            l_s[ki : ki + 1, :] = jnp.sum(weight, axis=0, keepdims=True)
            d_s[ki : ki + 1, :] = jnp.sum(weight * dprob, axis=0, keepdims=True)
            e_s[ki] = weight
            dp_s[ki] = dprob

        tops = m_s[...]
        factor = jnp.exp2((tops - jnp.max(tops, axis=0, keepdims=True)) * expo)
        norm = jnp.sum(l_s[...] * factor, axis=0, keepdims=True)
        delta = jnp.sum(d_s[...] * factor, axis=0, keepdims=True) / norm
        m_s[...] = factor / norm
        for ki in range(tiles):
            weight = e_s[ki] * m_s[ki : ki + 1, :]
            dscore = (weight * (dp_s[ki] - delta)).astype(jnp.bfloat16)
            dv_s[ki] += mm(weight.astype(jnp.bfloat16), grad, NN)
            dk_s[ki] += mm(dscore, query, NN)
            ds_s[ki * TILE : (ki + 1) * TILE, :] = dscore

        query_full = mm(ds_s[...], k_s[...], TN) * score_scale
        dq_s[part] = query_full.astype(jnp.bfloat16)
        return query_sq + jnp.sum(query_full * query_full, axis=0, keepdims=True)

    query_sq = lax.fori_loop(0, parts, query_step, jnp.zeros((1, HD), jnp.float32))
    key_sq = jnp.zeros((1, HD), jnp.float32)
    value_sq = jnp.zeros((1, HD), jnp.float32)
    for part in range(parts):
        for sub in range(tiles_dev):
            tile = part * tiles_dev + sub
            key_full = dk_s[tile] * score_scale
            value_full = dv_s[tile]
            key_sq = key_sq + jnp.sum(key_full * key_full, axis=0, keepdims=True)
            value_sq = value_sq + jnp.sum(value_full * value_full, axis=0, keepdims=True)
            low = sub * TILE
            outs[part][low : low + TILE, :] = dq_s[part, low : low + TILE, :]
            outs[part][rows + low : rows + low + TILE, :] = key_full.astype(jnp.bfloat16)
            outs[part][2 * rows + low : 2 * rows + low + TILE, :] = value_full.astype(jnp.bfloat16)
    row = lax.broadcasted_iota(jnp.int32, (STAT_ROWS, HD), 0)
    total = jnp.where(
        row < 3,
        jnp.sum(query_sq, axis=1, keepdims=True),
        jnp.where(
            row < 6,
            jnp.sum(key_sq, axis=1, keepdims=True),
            jnp.sum(value_sq, axis=1, keepdims=True),
        ),
    )
    high = total.astype(jnp.bfloat16).astype(jnp.float32)
    mid = (total - high).astype(jnp.bfloat16).astype(jnp.float32)
    low = total - high - mid
    piece = lax.rem(row, 3)
    stats = jnp.where(piece == 0, high, jnp.where(piece == 1, mid, low)).astype(jnp.bfloat16)
    for part in range(parts):
        outs[part][3 * rows :, :] = stats


def attend(me, mask, blocks, chunks):
    parts = len(blocks)
    rows = blocks[0].shape[1]
    tiles_dev = rows // TILE
    tiles = parts * tiles_dev
    bf16, f32 = jnp.bfloat16, jnp.float32
    pairs = tiles * tiles
    return pl.pallas_call(
        functools.partial(attend_kernel, parts, tiles_dev),
        out_shape=[jax.ShapeDtypeStruct((3 * rows + STAT_ROWS, HD), bf16)] * parts,
        in_specs=[SMEM, SMEM] + [ANY] * (parts + len(chunks)),
        out_specs=[VMEM] * parts,
        scratch_shapes=[
            pltpu.VMEM((parts * rows, HD), bf16),
            pltpu.VMEM((parts * rows, HD), bf16),
            pltpu.VMEM((parts * rows, HD), bf16),
            pltpu.VMEM((parts * rows, HD), bf16),
            pltpu.VMEM((tiles, TILE, HD), f32),
            pltpu.VMEM((tiles, TILE, HD), f32),
            pltpu.VMEM((parts, rows, HD), bf16),
            pltpu.VMEM((tiles, TILE, rows), f32),
            pltpu.VMEM((tiles, TILE, rows), f32),
            pltpu.VMEM((tiles * TILE, rows), bf16),
            pltpu.VMEM((tiles, rows), f32),
            pltpu.VMEM((tiles, rows), f32),
            pltpu.VMEM((tiles, rows), f32),
            pltpu.SemaphoreType.DMA((parts, 3 + tiles_dev)),
        ],
        cost_estimate=pl.CostEstimate(
            flops=pairs * 10 * TILE * TILE * HD,
            transcendentals=pairs * TILE * TILE,
            bytes_accessed=2 * 7 * parts * rows * HD,
        ),
        compiler_params=pltpu.CompilerParams(vmem_limit_bytes=ATTEND_GRANT),
        name="attend_head",
    )(me, mask, *blocks, *chunks)


def unpack_kernel(parts, rows, count, fresh, heads_ref, live_ref, *refs):
    blocks = refs[:parts]
    rest = refs[parts:]
    feats = None
    if not fresh:
        feats = rest[3][...]
        rest = rest[4:]
    outs = rest[:3]
    feat_out = rest[3]
    sems = rest[4]
    if fresh:
        feats = jnp.zeros(feat_out.shape, jnp.float32)

    def copies(slot):
        cols = pl.ds(pl.multiple_of(heads_ref[slot] * HD, HD), HD)
        return [
            pltpu.make_async_copy(
                blocks[slot].at[pl.ds(j * rows, rows), :], outs[j].at[:, cols], sems.at[slot, j]
            )
            for j in range(3)
        ]

    for slot in range(parts):
        @pl.when(live_ref[slot] != 0)
        def _():
            for copy in copies(slot):
                copy.start()

    row = lax.broadcasted_iota(jnp.int32, feat_out.shape, 2)
    col = lax.broadcasted_iota(jnp.int32, feat_out.shape, 0)
    for slot in range(parts):
        stats = blocks[slot][3 * rows :, :].astype(jnp.float32)
        here = (row == heads_ref[slot]) & (live_ref[slot] != 0)
        for j in range(3):
            total = stats[3 * j : 3 * j + 1, :] + stats[3 * j + 1 : 3 * j + 2, :]
            total = total + stats[3 * j + 2 : 3 * j + 3, :]
            value = jnp.log(total / count + 1e-06)[:, : feat_out.shape[2]]
            feats = jnp.where(here & (col == j), value[None], feats)
    feat_out[...] = feats
    for slot in range(parts):
        @pl.when(live_ref[slot] != 0)
        def _():
            for copy in copies(slot):
                copy.wait()


def unpack(heads, live, blocks, before, head_count, count):
    parts = len(blocks)
    rows = (blocks[0].shape[0] - STAT_ROWS) // 3
    fresh = before is None
    kept = [] if fresh else list(before)
    big = jax.ShapeDtypeStruct((rows, head_count * HD), jnp.bfloat16)
    return pl.pallas_call(
        functools.partial(unpack_kernel, parts, rows, count, fresh),
        out_shape=[big, big, big, jax.ShapeDtypeStruct((3, 1, head_count), jnp.float32)],
        in_specs=[SMEM, SMEM] + [VMEM] * parts + ([] if fresh else [ANY, ANY, ANY, VMEM]),
        out_specs=[ANY, ANY, ANY, VMEM],
        scratch_shapes=[pltpu.SemaphoreType.DMA((parts, 3))],
        input_output_aliases={} if fresh else {2 + parts + j: j for j in range(3)},
        compiler_params=pltpu.CompilerParams(vmem_limit_bytes=SMALL_GRANT),
        cost_estimate=pl.CostEstimate(
            flops=0, transcendentals=0, bytes_accessed=12 * parts * rows * HD
        ),
        name="unpack_heads",
    )(heads, live, *blocks, *kept)


def shift(arr, axis, step, size, targets):
    pairs = [(s, (s + step) % size) for s in range(size) if (s + step) % size in targets]
    return lax.ppermute(arr, axis, pairs)


def shift_back(arr, axis, step, size, sources):
    return lax.ppermute(arr, axis, [(s, (s - step) % size) for s in sources])


def allowed_tiles(key_list, key_count):
    tiles, slots = key_list.shape
    live = jnp.arange(slots)[None, :] < key_count[:, None]
    hit = (key_list[:, :, None] == jnp.arange(tiles)[None, None, :]) & live[:, :, None]
    return jnp.any(hit, axis=1).astype(jnp.int32)


def by_heads(query_states, key_states, value_states, output_grad, w_out, key_list, key_count):
    parts = lax.axis_size("seq")
    me = lax.axis_index("seq")
    side = lax.axis_index("head")
    rows, width = query_states.shape[1:]
    head_count = width // HD
    full, extra = divmod(head_count, parts)
    low = (parts - extra) // 2
    rounds = [(k * parts, 0, parts) for k in range(full)]
    if extra:
        rounds.append((full * parts, low, extra))
    dest = lax.rem(me + jnp.arange(parts, dtype=jnp.int32), parts)
    heads, lives, targets = [], [], []
    for base, first, size in rounds:
        heads.append(base + jnp.clip(dest - first, 0, size - 1).astype(jnp.int32))
        lives.append(((dest >= first) & (dest < first + size)).astype(jnp.int32))
        targets.append(list(range(first, first + size)))
    mask = allowed_tiles(key_list[0], key_count[0])
    all_heads = jnp.concatenate(heads)
    chunk_count = rows // TILE
    tensors = (query_states[0], key_states[0], value_states[0])
    first, pieces = stage(heads[0], tensors, output_grad[0], range(1, parts), [0])
    own, rest = stage(heads[0], tensors, output_grad[0], [0], range(1, chunk_count))
    pieces = [*pieces, *rest]
    other = []
    for piece in pieces:
        if other:
            piece, _ = lax.optimization_barrier((piece, other[-1]))
        other.append(lax.ppermute(piece, "head", [(0, 1), (1, 0)]))
    side = side.astype(jnp.int32).reshape(1)
    blocks = [*own] + [shift(first[i - 1], "seq", i, parts, targets[0]) for i in range(1, parts)]
    acc = project_own(side, output_grad[0], w_out)
    projected = [
        project_rest(all_heads, 1 - side, other[chunk], w_out, acc, chunk)
        for chunk in range(chunk_count)
    ]
    chunks = []
    for slots in projected:
        chunks += [slots[0]]
        for i in range(1, parts):
            chunks += [shift(slots[i], "seq", i, parts, targets[0])]
    before = None
    for k in range(len(rounds)):
        me_live = jnp.stack([me.astype(jnp.int32), lives[k][0]])
        done = attend(me_live, mask, blocks, chunks)
        if k + 1 < len(rounds):
            grads = [slot for slots in projected for slot in slots[(k + 1) * parts : (k + 2) * parts]]
            slots = pack(heads[k + 1], *tensors, grads)
            blocks = [slots[0]]
            for i in range(1, parts):
                blocks += [shift(slots[i], "seq", i, parts, targets[k + 1])]
            chunks = []
        back = [done[0]] + [
            shift_back(done[i], "seq", i, parts, targets[k]) for i in range(1, parts)
        ]
        before = unpack(heads[k], lives[k], back, before, head_count, parts * rows * HD)
    query_grad, key_grad, value_grad, feats = before
    return query_grad[None], key_grad[None], value_grad[None], feats.transpose(1, 2, 0)


def attend_gathered(query_tiles, key_buf, value_buf, grad_tiles, buf_slots, counts):
    score_scale = HD ** (-0.5)
    tile_count, tile_rows, feat_width = query_tiles.shape
    slot_count = buf_slots.shape[1]
    key_span = slot_count * tile_rows
    buf_tiles = key_buf.shape[0]
    key_sel = key_buf[buf_slots].reshape(tile_count, key_span, feat_width)
    value_sel = value_buf[buf_slots].reshape(tile_count, key_span, feat_width)
    allowed = jnp.arange(key_span)[None, :] // tile_rows < counts[:, None]

    def head_step(head_idx, carried):
        query_acc, key_acc, value_acc = carried
        col_start = head_idx * HD
        query_head = lax.dynamic_slice_in_dim(query_tiles, col_start, HD, 2)
        key_head = lax.dynamic_slice_in_dim(key_sel, col_start, HD, 2)
        value_head = lax.dynamic_slice_in_dim(value_sel, col_start, HD, 2)
        grad_head = lax.dynamic_slice_in_dim(grad_tiles, col_start, HD, 2)
        scores = (
            jnp.einsum("iqe,ike->iqk", query_head, key_head, preferred_element_type=jnp.float32)
            * score_scale
        )
        scores = jnp.where(allowed[:, None, :], scores, -jnp.inf)
        row_max = jnp.max(scores, axis=-1, keepdims=True)
        log_norm = row_max + jnp.log(jnp.sum(jnp.exp(scores - row_max), axis=-1, keepdims=True))
        weights = jnp.exp(scores - log_norm)
        weights_b = weights.astype(jnp.bfloat16)
        attn_out = jnp.einsum(
            "iqk,ike->iqe", weights_b, value_head, preferred_element_type=jnp.float32
        ).astype(jnp.bfloat16)
        row_delta = jnp.sum(
            grad_head.astype(jnp.float32) * attn_out.astype(jnp.float32), axis=-1, keepdims=True
        )
        dprob = jnp.einsum(
            "iqe,ike->iqk", grad_head, value_head, preferred_element_type=jnp.float32
        )
        dscore = (weights * (dprob - row_delta)).astype(jnp.bfloat16)
        query_head_grad = score_scale * jnp.einsum(
            "iqk,ike->iqe", dscore, key_head, preferred_element_type=jnp.float32
        )
        key_head_grad = score_scale * jnp.einsum(
            "iqk,iqe->ike", dscore, query_head, preferred_element_type=jnp.float32
        )
        value_head_grad = jnp.einsum(
            "iqk,iqe->ike", weights_b, grad_head, preferred_element_type=jnp.float32
        )
        query_acc = lax.dynamic_update_slice_in_dim(query_acc, query_head_grad, col_start, 2)
        key_acc = lax.dynamic_update_slice_in_dim(key_acc, key_head_grad, col_start, 2)
        value_acc = lax.dynamic_update_slice_in_dim(value_acc, value_head_grad, col_start, 2)
        return (query_acc, key_acc, value_acc)

    start_state = (
        jnp.zeros((tile_count, tile_rows, feat_width), jnp.float32),
        jnp.zeros((tile_count, key_span, feat_width), jnp.float32),
        jnp.zeros((tile_count, key_span, feat_width), jnp.float32),
    )
    query_full, key_sel_grad, value_sel_grad = lax.fori_loop(
        0, feat_width // HD, head_step, start_state
    )
    live_slot = jnp.arange(slot_count)[None, :] < counts[:, None]
    routing = (
        (buf_slots[:, :, None] == jnp.arange(buf_tiles)[None, None, :]) & live_slot[:, :, None]
    ).astype(jnp.float32)
    key_grad_buf = jnp.einsum(
        "imb,imr->br",
        routing,
        key_sel_grad.reshape(tile_count, slot_count, tile_rows * feat_width),
        precision=lax.Precision.HIGHEST,
    )
    value_grad_buf = jnp.einsum(
        "imb,imr->br",
        routing,
        value_sel_grad.reshape(tile_count, slot_count, tile_rows * feat_width),
        precision=lax.Precision.HIGHEST,
    )
    return (
        query_full,
        key_grad_buf.reshape(buf_tiles, tile_rows, feat_width),
        value_grad_buf.reshape(buf_tiles, tile_rows, feat_width),
    )


def head_squares(grads_full, head_count):
    rows = grads_full.reshape(-1, head_count, HD)
    return jnp.sum(rows * rows, axis=(0, 2))


def by_gather(query_states, key_states, value_states, output_grad, w_out, key_list, key_count):
    seq_count = lax.axis_size("seq")
    seq_index = lax.axis_index("seq")
    tok_rows = query_states.shape[1]
    feat_width = query_states.shape[2]
    head_count = feat_width // HD
    tile_count = tok_rows // TILE
    first_tile = seq_index * tile_count
    own_lists = lax.dynamic_slice_in_dim(key_list[0], first_tile, tile_count, 0)
    own_counts = lax.dynamic_slice_in_dim(key_count[0], first_tile, tile_count, 0)
    grad_out = lax.dot_general(
        lax.all_gather(output_grad, "head", axis=2, tiled=True)[0],
        w_out,
        (((1,), (1,)), ((), ())),
        preferred_element_type=jnp.float32,
    ).astype(jnp.bfloat16)
    query_tiles = query_states[0].reshape(tile_count, TILE, feat_width)
    grad_tiles = grad_out.reshape(tile_count, TILE, feat_width)
    key_whole, value_whole = (
        lax.all_gather(key_states, "seq", axis=1, tiled=True),
        lax.all_gather(value_states, "seq", axis=1, tiled=True),
    )
    key_buf = key_whole[0].reshape(-1, TILE, feat_width)
    value_buf = value_whole[0].reshape(-1, TILE, feat_width)
    query_full, key_grad_buf, value_grad_buf = attend_gathered(
        query_tiles, key_buf, value_buf, grad_tiles, own_lists, own_counts
    )
    buf_rows = key_grad_buf.shape[0] * TILE
    key_sum, value_sum = (
        lax.psum_scatter(
            key_grad_buf.reshape(1, buf_rows, feat_width).astype(jnp.bfloat16),
            "seq",
            scatter_dimension=1,
            tiled=True,
        ).astype(jnp.float32),
        lax.psum_scatter(
            value_grad_buf.reshape(1, buf_rows, feat_width).astype(jnp.bfloat16),
            "seq",
            scatter_dimension=1,
            tiled=True,
        ).astype(jnp.float32),
    )
    key_full = key_sum[0]
    value_full = value_sum[0]
    query_rows = query_full.reshape(tok_rows, feat_width)
    local_sums = jnp.stack(
        [
            head_squares(query_rows, head_count),
            head_squares(key_full, head_count),
            head_squares(value_full, head_count),
        ],
        axis=-1,
    )
    total_sums = lax.psum(local_sums, "seq")
    grad_features = jnp.log(total_sums / (seq_count * tok_rows * HD) + 1e-06)
    return (
        query_rows.astype(jnp.bfloat16)[None],
        key_full.astype(jnp.bfloat16)[None],
        value_full.astype(jnp.bfloat16)[None],
        grad_features[None],
    )


def per_device(*args):
    parts, sides = lax.axis_size("seq"), lax.axis_size("head")
    head_count = args[0].shape[2] // HD
    if head_count >= parts > 1 and head_count % 2 == 0 and sides == 2:
        return by_heads(*args)
    return by_gather(*args)


def solution(mesh):
    in_specs = (
        P(("grp", "clip"), "seq", "head"),
        P(("grp", "clip"), "seq", "head"),
        P(("grp", "clip"), "seq", "head"),
        P(("grp", "clip"), "seq", "head"),
        P("head", None),
        P(("grp", "clip"), None, None),
        P(("grp", "clip"), None),
    )
    out_specs = (
        P(("grp", "clip"), "seq", "head"),
        P(("grp", "clip"), "seq", "head"),
        P(("grp", "clip"), "seq", "head"),
        P(("grp", "clip"), "head", None),
    )
    return jax.shard_map(
        per_device, mesh=mesh, in_specs=in_specs, out_specs=out_specs, check_vma=False
    )
```

```python
import functools
import math

import jax
import jax.numpy as jnp
from jax import lax
from jax.experimental import pallas as pl
from jax.experimental.pallas import tpu as pltpu
from jax.sharding import PartitionSpec as P


HD = 128
TILE = 256
STAT_ROWS = 16
SMALL_GRANT = 12 << 20
ATTEND_GRANT = 24 << 20
SMEM = pl.BlockSpec(memory_space=pltpu.SMEM)
VMEM = pl.BlockSpec(memory_space=pltpu.VMEM)
ANY = pl.BlockSpec(memory_space=pl.ANY)
HBM = pl.BlockSpec(memory_space=pltpu.HBM)
NT = (((1,), (1,)), ((), ()))
NN = (((1,), (0,)), ((), ()))
TN = (((0,), (0,)), ((), ()))


def mm(lhs, rhs, dims):
    return lax.dot_general(lhs, rhs, dims, preferred_element_type=jnp.float32)


def stage_kernel(slots, kinds, chunks, heads_ref, *refs):
    tensors = refs[:kinds]
    grad_ref = refs[kinds]
    outs = refs[kinds + 1 : -1]
    sems = refs[-1]
    copies = []
    for piece, chunk in enumerate(chunks):
        span = pl.ds(chunk * TILE, TILE)
        copies.append(
            pltpu.make_async_copy(grad_ref.at[span, :], outs[len(slots) + piece], sems.at[piece, kinds])
        )
    for index, slot in enumerate(slots):
        cols = pl.ds(pl.multiple_of(heads_ref[slot] * HD, HD), HD)
        for j, tensor in enumerate(tensors):
            copies.append(
                pltpu.make_async_copy(tensor.at[:, cols], outs[index].at[j], sems.at[index, j])
            )
    for copy in copies:
        copy.start()
    for copy in copies:
        copy.wait()


def stage(heads, tensors, grad, slots, chunks):
    rows = grad.shape[0]
    kinds = len(tensors)
    held = [pltpu.with_memory_space_constraint(arr, pltpu.HBM) for arr in (*tensors, grad)]
    outs = pl.pallas_call(
        functools.partial(stage_kernel, slots, kinds, chunks),
        out_shape=[pltpu.VMEM((kinds, rows, HD), grad.dtype)] * len(slots)
        + [pltpu.VMEM((TILE, grad.shape[1]), grad.dtype)] * len(chunks),
        in_specs=[SMEM] + [HBM] * (kinds + 1),
        out_specs=[VMEM] * (len(slots) + len(chunks)),
        scratch_shapes=[pltpu.SemaphoreType.DMA((max(len(slots), len(chunks)), kinds + 1))],
        compiler_params=pltpu.CompilerParams(vmem_limit_bytes=SMALL_GRANT),
        cost_estimate=pl.CostEstimate(
            flops=0,
            transcendentals=0,
            bytes_accessed=4 * (len(slots) * kinds * rows * HD + len(chunks) * TILE * grad.shape[1]),
        ),
        name="stage_inputs",
    )(heads, *held)
    return outs[: len(slots)], outs[len(slots) :]


def pack_kernel(slots, heads_ref, q_ref, k_ref, v_ref, *refs):
    outs = refs[len(refs) - slots :]
    chunks = len(refs) // slots - 1
    for slot, out in enumerate(outs):
        cols = pl.ds(pl.multiple_of(heads_ref[slot] * HD, HD), HD)
        out[0] = q_ref[:, cols]
        out[1] = k_ref[:, cols]
        out[2] = v_ref[:, cols]
        for chunk in range(chunks):
            out[3, chunk * TILE : (chunk + 1) * TILE, :] = refs[chunk * slots + slot][...]


def pack(heads, query, key, value, grads):
    rows = query.shape[0]
    slots = heads.shape[0]
    kinds = 4 if grads else 3
    return pl.pallas_call(
        functools.partial(pack_kernel, slots),
        out_shape=[jax.ShapeDtypeStruct((kinds, rows, HD), query.dtype)] * slots,
        in_specs=[SMEM, VMEM, VMEM, VMEM] + [VMEM] * len(grads),
        out_specs=[VMEM] * slots,
        compiler_params=pltpu.CompilerParams(vmem_limit_bytes=SMALL_GRANT),
        cost_estimate=pl.CostEstimate(
            flops=0, transcendentals=0, bytes_accessed=6 * (query.size + slots * rows * HD)
        ),
        name="pack_heads",
    )(heads, query, key, value, *grads)


def project_own_kernel(src_ref, grad_ref, w_ref, out):
    out[0] = mm(grad_ref[...], w_ref[...], NT)


def project_own(src, grads, w_out):
    rows, feats = grads.shape
    width = w_out.shape[0]
    steps = width // (2 * HD)
    return pl.pallas_call(
        project_own_kernel,
        out_shape=jax.ShapeDtypeStruct((steps, rows, 2 * HD), jnp.float32),
        grid_spec=pltpu.PrefetchScalarGridSpec(
            num_scalar_prefetch=1,
            grid=(steps,),
            in_specs=[
                pl.BlockSpec((rows, feats), lambda s, src: (0, 0)),
                pl.BlockSpec((2 * HD, feats), lambda s, src: (s, src[0])),
            ],
            out_specs=pl.BlockSpec((1, rows, 2 * HD), lambda s, src: (s, 0, 0)),
        ),
        compiler_params=pltpu.CompilerParams(vmem_limit_bytes=SMALL_GRANT),
        cost_estimate=pl.CostEstimate(
            flops=2 * rows * feats * width,
            transcendentals=0,
            bytes_accessed=2 * (grads.size + width * feats) + 4 * rows * width,
        ),
        name="project_own",
    )(src, grads, w_out)


def project_rest_kernel(heads_ref, src_ref, grad_ref, w_ref, acc_ref, *refs):
    outs, held = refs[:-1], refs[-1]
    total = mm(grad_ref[...], w_ref[...], NT) + acc_ref[0]
    step = pl.program_id(0)
    for half in range(2):
        held[2 * step + half] = total[:, half * HD : (half + 1) * HD].astype(jnp.bfloat16)

    @pl.when(step == pl.num_programs(0) - 1)
    def _():
        for slot, out in enumerate(outs):
            out[...] = held[heads_ref[slot]]


def project_rest(heads, src, grads, w_out, acc, chunk):
    rows, feats = grads.shape
    slots = heads.shape[0]
    width = w_out.shape[0]
    steps = width // (2 * HD)
    return pl.pallas_call(
        project_rest_kernel,
        out_shape=[jax.ShapeDtypeStruct((rows, HD), jnp.bfloat16)] * slots,
        grid_spec=pltpu.PrefetchScalarGridSpec(
            num_scalar_prefetch=2,
            grid=(steps,),
            in_specs=[
                pl.BlockSpec((rows, feats), lambda s, heads, src: (0, 0)),
                pl.BlockSpec((2 * HD, feats), lambda s, heads, src: (s, src[0])),
                pl.BlockSpec((1, rows, 2 * HD), lambda s, heads, src: (s, chunk, 0)),
            ],
            out_specs=[pl.BlockSpec((rows, HD), lambda s, heads, src: (0, 0))] * slots,
            scratch_shapes=[pltpu.VMEM((width // HD, rows, HD), jnp.bfloat16)],
        ),
        compiler_params=pltpu.CompilerParams(vmem_limit_bytes=SMALL_GRANT),
        cost_estimate=pl.CostEstimate(
            flops=2 * rows * feats * width,
            transcendentals=0,
            bytes_accessed=2 * (grads.size + width * feats) + 6 * rows * width,
        ),
        name="project_rest",
    )(heads, src, grads, w_out, acc)


def attend_kernel(parts, tiles_dev, me_ref, mask_ref, *refs):
    @pl.when(me_ref[1] != 0)
    def _():
        attend_body(parts, tiles_dev, me_ref, mask_ref, *refs)


def attend_body(parts, tiles_dev, me_ref, mask_ref, *refs):
    tiles = parts * tiles_dev
    rows = tiles_dev * TILE
    blocks = refs[:parts]
    chunks = refs[parts : len(refs) - parts - 14]
    outs = refs[len(refs) - parts - 14 : len(refs) - 14]
    q_s, k_s, v_s, g_s, dk_s, dv_s, dq_s, e_s, dp_s, ds_s, m_s, l_s, d_s, sems = refs[-14:]
    score_scale = HD ** (-0.5)
    expo = score_scale * math.log2(math.e)
    me = me_ref[0]
    copies = []
    for part in range(parts):
        span = pl.ds(part * rows, rows)
        pairs = [(blocks[part].at[j], held.at[span]) for j, held in enumerate((q_s, k_s, v_s))]
        if chunks:
            for sub in range(tiles_dev):
                span = pl.ds(part * rows + sub * TILE, TILE)
                pairs.append((chunks[sub * parts + part], g_s.at[span]))
        else:
            pairs.append((blocks[part].at[3], g_s.at[span]))
        for j, (source, held) in enumerate(pairs):
            copies.append(pltpu.make_async_copy(source, held, sems.at[part, j]))
    for copy in copies:
        copy.start()
    for copy in copies:
        copy.wait()
    dk_s[...] = jnp.zeros_like(dk_s)
    dv_s[...] = jnp.zeros_like(dv_s)

    def home(part):
        return lax.rem(me - part + parts, parts) * tiles_dev

    def query_step(part, query_sq):
        own = home(part)
        span = pl.ds(pl.multiple_of(part * rows, rows), rows)
        query = q_s[span, :]
        grad = g_s[span, :]
        for ki in range(tiles):
            place = home(ki // tiles_dev) + ki % tiles_dev
            scores = mm(k_s[ki * TILE : (ki + 1) * TILE, :], query, NT)
            dprob = mm(v_s[ki * TILE : (ki + 1) * TILE, :], grad, NT)
            top = jnp.max(scores, axis=0, keepdims=True)
            weight = jnp.exp2((scores - top) * expo)
            for sub in range(tiles_dev):
                cols = slice(sub * TILE, (sub + 1) * TILE)
                live = mask_ref[own + sub, place] != 0
                m_s[ki : ki + 1, cols] = jnp.where(live, top[:, cols], -jnp.inf)
            l_s[ki : ki + 1, :] = jnp.sum(weight, axis=0, keepdims=True)
            d_s[ki : ki + 1, :] = jnp.sum(weight * dprob, axis=0, keepdims=True)
            e_s[ki] = weight
            dp_s[ki] = dprob

        tops = m_s[...]
        factor = jnp.exp2((tops - jnp.max(tops, axis=0, keepdims=True)) * expo)
        norm = jnp.sum(l_s[...] * factor, axis=0, keepdims=True)
        delta = jnp.sum(d_s[...] * factor, axis=0, keepdims=True) / norm
        m_s[...] = factor / norm
        for ki in range(tiles):
            weight = e_s[ki] * m_s[ki : ki + 1, :]
            dscore = (weight * (dp_s[ki] - delta)).astype(jnp.bfloat16)
            dv_s[ki] += mm(weight.astype(jnp.bfloat16), grad, NN)
            dk_s[ki] += mm(dscore, query, NN)
            ds_s[ki * TILE : (ki + 1) * TILE, :] = dscore

        query_full = mm(ds_s[...], k_s[...], TN) * score_scale
        dq_s[part] = query_full.astype(jnp.bfloat16)
        return query_sq + jnp.sum(query_full * query_full, axis=0, keepdims=True)

    query_sq = lax.fori_loop(0, parts, query_step, jnp.zeros((1, HD), jnp.float32))
    key_sq = jnp.zeros((1, HD), jnp.float32)
    value_sq = jnp.zeros((1, HD), jnp.float32)
    for part in range(parts):
        for sub in range(tiles_dev):
            tile = part * tiles_dev + sub
            key_full = dk_s[tile] * score_scale
            value_full = dv_s[tile]
            key_sq = key_sq + jnp.sum(key_full * key_full, axis=0, keepdims=True)
            value_sq = value_sq + jnp.sum(value_full * value_full, axis=0, keepdims=True)
            low = sub * TILE
            outs[part][low : low + TILE, :] = dq_s[part, low : low + TILE, :]
            outs[part][rows + low : rows + low + TILE, :] = key_full.astype(jnp.bfloat16)
            outs[part][2 * rows + low : 2 * rows + low + TILE, :] = value_full.astype(jnp.bfloat16)
    row = lax.broadcasted_iota(jnp.int32, (STAT_ROWS, HD), 0)
    total = jnp.where(
        row < 3,
        jnp.sum(query_sq, axis=1, keepdims=True),
        jnp.where(
            row < 6,
            jnp.sum(key_sq, axis=1, keepdims=True),
            jnp.sum(value_sq, axis=1, keepdims=True),
        ),
    )
    high = total.astype(jnp.bfloat16).astype(jnp.float32)
    mid = (total - high).astype(jnp.bfloat16).astype(jnp.float32)
    low = total - high - mid
    piece = lax.rem(row, 3)
    stats = jnp.where(piece == 0, high, jnp.where(piece == 1, mid, low)).astype(jnp.bfloat16)
    for part in range(parts):
        outs[part][3 * rows :, :] = stats


def attend(me, mask, blocks, chunks):
    parts = len(blocks)
    rows = blocks[0].shape[1]
    tiles_dev = rows // TILE
    tiles = parts * tiles_dev
    bf16, f32 = jnp.bfloat16, jnp.float32
    pairs = tiles * tiles
    return pl.pallas_call(
        functools.partial(attend_kernel, parts, tiles_dev),
        out_shape=[jax.ShapeDtypeStruct((3 * rows + STAT_ROWS, HD), bf16)] * parts,
        in_specs=[SMEM, SMEM] + [ANY] * (parts + len(chunks)),
        out_specs=[VMEM] * parts,
        scratch_shapes=[
            pltpu.VMEM((parts * rows, HD), bf16),
            pltpu.VMEM((parts * rows, HD), bf16),
            pltpu.VMEM((parts * rows, HD), bf16),
            pltpu.VMEM((parts * rows, HD), bf16),
            pltpu.VMEM((tiles, TILE, HD), f32),
            pltpu.VMEM((tiles, TILE, HD), f32),
            pltpu.VMEM((parts, rows, HD), bf16),
            pltpu.VMEM((tiles, TILE, rows), f32),
            pltpu.VMEM((tiles, TILE, rows), f32),
            pltpu.VMEM((tiles * TILE, rows), bf16),
            pltpu.VMEM((tiles, rows), f32),
            pltpu.VMEM((tiles, rows), f32),
            pltpu.VMEM((tiles, rows), f32),
            pltpu.SemaphoreType.DMA((parts, 3 + tiles_dev)),
        ],
        cost_estimate=pl.CostEstimate(
            flops=pairs * 10 * TILE * TILE * HD,
            transcendentals=pairs * TILE * TILE,
            bytes_accessed=2 * 7 * parts * rows * HD,
        ),
        compiler_params=pltpu.CompilerParams(vmem_limit_bytes=ATTEND_GRANT),
        name="attend_head",
    )(me, mask, *blocks, *chunks)


def unpack_kernel(parts, rows, count, fresh, heads_ref, live_ref, *refs):
    blocks = refs[:parts]
    rest = refs[parts:]
    feats = None
    if not fresh:
        feats = rest[3][...]
        rest = rest[4:]
    outs = rest[:3]
    feat_out = rest[3]
    sems = rest[4]
    if fresh:
        feats = jnp.zeros(feat_out.shape, jnp.float32)

    def copies(slot):
        cols = pl.ds(pl.multiple_of(heads_ref[slot] * HD, HD), HD)
        return [
            pltpu.make_async_copy(
                blocks[slot].at[pl.ds(j * rows, rows), :], outs[j].at[:, cols], sems.at[slot, j]
            )
            for j in range(3)
        ]

    for slot in range(parts):
        @pl.when(live_ref[slot] != 0)
        def _():
            for copy in copies(slot):
                copy.start()

    row = lax.broadcasted_iota(jnp.int32, feat_out.shape, 2)
    col = lax.broadcasted_iota(jnp.int32, feat_out.shape, 0)
    for slot in range(parts):
        stats = blocks[slot][3 * rows :, :].astype(jnp.float32)
        here = (row == heads_ref[slot]) & (live_ref[slot] != 0)
        for j in range(3):
            total = stats[3 * j : 3 * j + 1, :] + stats[3 * j + 1 : 3 * j + 2, :]
            total = total + stats[3 * j + 2 : 3 * j + 3, :]
            value = jnp.log(total / count + 1e-06)[:, : feat_out.shape[2]]
            feats = jnp.where(here & (col == j), value[None], feats)
    feat_out[...] = feats
    for slot in range(parts):
        @pl.when(live_ref[slot] != 0)
        def _():
            for copy in copies(slot):
                copy.wait()


def unpack(heads, live, blocks, before, head_count, count):
    parts = len(blocks)
    rows = (blocks[0].shape[0] - STAT_ROWS) // 3
    fresh = before is None
    kept = [] if fresh else list(before)
    big = jax.ShapeDtypeStruct((rows, head_count * HD), jnp.bfloat16)
    return pl.pallas_call(
        functools.partial(unpack_kernel, parts, rows, count, fresh),
        out_shape=[big, big, big, jax.ShapeDtypeStruct((3, 1, head_count), jnp.float32)],
        in_specs=[SMEM, SMEM] + [VMEM] * parts + ([] if fresh else [ANY, ANY, ANY, VMEM]),
        out_specs=[ANY, ANY, ANY, VMEM],
        scratch_shapes=[pltpu.SemaphoreType.DMA((parts, 3))],
        input_output_aliases={} if fresh else {2 + parts + j: j for j in range(3)},
        compiler_params=pltpu.CompilerParams(vmem_limit_bytes=SMALL_GRANT),
        cost_estimate=pl.CostEstimate(
            flops=0, transcendentals=0, bytes_accessed=12 * parts * rows * HD
        ),
        name="unpack_heads",
    )(heads, live, *blocks, *kept)


def shift(arr, axis, step, size, targets):
    pairs = [(s, (s + step) % size) for s in range(size) if (s + step) % size in targets]
    return lax.ppermute(arr, axis, pairs)


def shift_back(arr, axis, step, size, sources):
    return lax.ppermute(arr, axis, [(s, (s - step) % size) for s in sources])


def allowed_tiles(key_list, key_count):
    tiles, slots = key_list.shape
    live = jnp.arange(slots)[None, :] < key_count[:, None]
    hit = (key_list[:, :, None] == jnp.arange(tiles)[None, None, :]) & live[:, :, None]
    return jnp.any(hit, axis=1).astype(jnp.int32)


def by_heads(query_states, key_states, value_states, output_grad, w_out, key_list, key_count):
    parts = lax.axis_size("seq")
    me = lax.axis_index("seq")
    side = lax.axis_index("head")
    rows, width = query_states.shape[1:]
    head_count = width // HD
    full, extra = divmod(head_count, parts)
    low = (parts - extra) // 2
    rounds = [(k * parts, 0, parts) for k in range(full)]
    if extra:
        rounds.append((full * parts, low, extra))
    dest = lax.rem(me + jnp.arange(parts, dtype=jnp.int32), parts)
    heads, lives, targets = [], [], []
    for base, first, size in rounds:
        heads.append(base + jnp.clip(dest - first, 0, size - 1).astype(jnp.int32))
        lives.append(((dest >= first) & (dest < first + size)).astype(jnp.int32))
        targets.append(list(range(first, first + size)))
    mask = allowed_tiles(key_list[0], key_count[0])
    all_heads = jnp.concatenate(heads)
    hops = [1, 3, 2] if parts == 4 else list(range(1, parts))
    chunk_count = rows // TILE
    tensors = (query_states[0], key_states[0], value_states[0])
    other = []
    moved, pieces = stage(heads[0], tensors, output_grad[0], hops[:1], [0])
    blocks = [None] * parts

    def trade(piece):
        other.append(lax.ppermute(piece, "head", [(0, 1), (1, 0)]))

    def send_first(hop, slot):
        blocks[hop] = shift(slot, "seq", hop, parts, targets[0])

    trade(pieces[0])
    send_first(hops[0], moved[0])
    moved, _ = stage(heads[0], tensors, output_grad[0], hops[1:], [])
    for hop, slot in zip(hops[1:], moved):
        send_first(hop, slot)
    moved, pieces = stage(heads[0], tensors, output_grad[0], [0], range(1, chunk_count))
    blocks[0] = moved[0]
    for piece in pieces:
        trade(piece)
    side = side.astype(jnp.int32).reshape(1)
    acc = project_own(side, output_grad[0], w_out)
    projected = [
        project_rest(all_heads, 1 - side, other[chunk], w_out, acc, chunk)
        for chunk in range(chunk_count)
    ]
    chunks = []
    for slots in projected:
        landed = [slots[0]] + [None] * (parts - 1)
        for i in hops:
            landed[i] = shift(slots[i], "seq", i, parts, targets[0])
        chunks += landed
    before = None
    for k in range(len(rounds)):
        me_live = jnp.stack([me.astype(jnp.int32), lives[k][0]])
        done = attend(me_live, mask, blocks, chunks)
        if k + 1 < len(rounds):
            grads = [slot for slots in projected for slot in slots[(k + 1) * parts : (k + 2) * parts]]
            slots = pack(heads[k + 1], *tensors, grads)
            blocks = [slots[0]] + [None] * (parts - 1)
            for i in [1, 3, 2]:
                blocks[i] = shift(slots[i], "seq", i, parts, targets[k + 1])
            chunks = []
        back = [done[0]] + [None] * (parts - 1)
        for i in [2, 1, 3]:
            back[i] = shift_back(done[i], "seq", i, parts, targets[k])
        before = unpack(heads[k], lives[k], back, before, head_count, parts * rows * HD)
    query_grad, key_grad, value_grad, feats = before
    return query_grad[None], key_grad[None], value_grad[None], feats.transpose(1, 2, 0)


def attend_gathered(query_tiles, key_buf, value_buf, grad_tiles, buf_slots, counts):
    score_scale = HD ** (-0.5)
    tile_count, tile_rows, feat_width = query_tiles.shape
    slot_count = buf_slots.shape[1]
    key_span = slot_count * tile_rows
    buf_tiles = key_buf.shape[0]
    key_sel = key_buf[buf_slots].reshape(tile_count, key_span, feat_width)
    value_sel = value_buf[buf_slots].reshape(tile_count, key_span, feat_width)
    allowed = jnp.arange(key_span)[None, :] // tile_rows < counts[:, None]

    def head_step(head_idx, carried):
        query_acc, key_acc, value_acc = carried
        col_start = head_idx * HD
        query_head = lax.dynamic_slice_in_dim(query_tiles, col_start, HD, 2)
        key_head = lax.dynamic_slice_in_dim(key_sel, col_start, HD, 2)
        value_head = lax.dynamic_slice_in_dim(value_sel, col_start, HD, 2)
        grad_head = lax.dynamic_slice_in_dim(grad_tiles, col_start, HD, 2)
        scores = (
            jnp.einsum("iqe,ike->iqk", query_head, key_head, preferred_element_type=jnp.float32)
            * score_scale
        )
        scores = jnp.where(allowed[:, None, :], scores, -jnp.inf)
        row_max = jnp.max(scores, axis=-1, keepdims=True)
        log_norm = row_max + jnp.log(jnp.sum(jnp.exp(scores - row_max), axis=-1, keepdims=True))
        weights = jnp.exp(scores - log_norm)
        weights_b = weights.astype(jnp.bfloat16)
        attn_out = jnp.einsum(
            "iqk,ike->iqe", weights_b, value_head, preferred_element_type=jnp.float32
        ).astype(jnp.bfloat16)
        row_delta = jnp.sum(
            grad_head.astype(jnp.float32) * attn_out.astype(jnp.float32), axis=-1, keepdims=True
        )
        dprob = jnp.einsum(
            "iqe,ike->iqk", grad_head, value_head, preferred_element_type=jnp.float32
        )
        dscore = (weights * (dprob - row_delta)).astype(jnp.bfloat16)
        query_head_grad = score_scale * jnp.einsum(
            "iqk,ike->iqe", dscore, key_head, preferred_element_type=jnp.float32
        )
        key_head_grad = score_scale * jnp.einsum(
            "iqk,iqe->ike", dscore, query_head, preferred_element_type=jnp.float32
        )
        value_head_grad = jnp.einsum(
            "iqk,iqe->ike", weights_b, grad_head, preferred_element_type=jnp.float32
        )
        query_acc = lax.dynamic_update_slice_in_dim(query_acc, query_head_grad, col_start, 2)
        key_acc = lax.dynamic_update_slice_in_dim(key_acc, key_head_grad, col_start, 2)
        value_acc = lax.dynamic_update_slice_in_dim(value_acc, value_head_grad, col_start, 2)
        return (query_acc, key_acc, value_acc)

    start_state = (
        jnp.zeros((tile_count, tile_rows, feat_width), jnp.float32),
        jnp.zeros((tile_count, key_span, feat_width), jnp.float32),
        jnp.zeros((tile_count, key_span, feat_width), jnp.float32),
    )
    query_full, key_sel_grad, value_sel_grad = lax.fori_loop(
        0, feat_width // HD, head_step, start_state
    )
    live_slot = jnp.arange(slot_count)[None, :] < counts[:, None]
    routing = (
        (buf_slots[:, :, None] == jnp.arange(buf_tiles)[None, None, :]) & live_slot[:, :, None]
    ).astype(jnp.float32)
    key_grad_buf = jnp.einsum(
        "imb,imr->br",
        routing,
        key_sel_grad.reshape(tile_count, slot_count, tile_rows * feat_width),
        precision=lax.Precision.HIGHEST,
    )
    value_grad_buf = jnp.einsum(
        "imb,imr->br",
        routing,
        value_sel_grad.reshape(tile_count, slot_count, tile_rows * feat_width),
        precision=lax.Precision.HIGHEST,
    )
    return (
        query_full,
        key_grad_buf.reshape(buf_tiles, tile_rows, feat_width),
        value_grad_buf.reshape(buf_tiles, tile_rows, feat_width),
    )


def head_squares(grads_full, head_count):
    rows = grads_full.reshape(-1, head_count, HD)
    return jnp.sum(rows * rows, axis=(0, 2))


def by_gather(query_states, key_states, value_states, output_grad, w_out, key_list, key_count):
    seq_count = lax.axis_size("seq")
    seq_index = lax.axis_index("seq")
    tok_rows = query_states.shape[1]
    feat_width = query_states.shape[2]
    head_count = feat_width // HD
    tile_count = tok_rows // TILE
    first_tile = seq_index * tile_count
    own_lists = lax.dynamic_slice_in_dim(key_list[0], first_tile, tile_count, 0)
    own_counts = lax.dynamic_slice_in_dim(key_count[0], first_tile, tile_count, 0)
    grad_out = lax.dot_general(
        lax.all_gather(output_grad, "head", axis=2, tiled=True)[0],
        w_out,
        (((1,), (1,)), ((), ())),
        preferred_element_type=jnp.float32,
    ).astype(jnp.bfloat16)
    query_tiles = query_states[0].reshape(tile_count, TILE, feat_width)
    grad_tiles = grad_out.reshape(tile_count, TILE, feat_width)
    key_whole, value_whole = (
        lax.all_gather(key_states, "seq", axis=1, tiled=True),
        lax.all_gather(value_states, "seq", axis=1, tiled=True),
    )
    key_buf = key_whole[0].reshape(-1, TILE, feat_width)
    value_buf = value_whole[0].reshape(-1, TILE, feat_width)
    query_full, key_grad_buf, value_grad_buf = attend_gathered(
        query_tiles, key_buf, value_buf, grad_tiles, own_lists, own_counts
    )
    buf_rows = key_grad_buf.shape[0] * TILE
    key_sum, value_sum = (
        lax.psum_scatter(
            key_grad_buf.reshape(1, buf_rows, feat_width).astype(jnp.bfloat16),
            "seq",
            scatter_dimension=1,
            tiled=True,
        ).astype(jnp.float32),
        lax.psum_scatter(
            value_grad_buf.reshape(1, buf_rows, feat_width).astype(jnp.bfloat16),
            "seq",
            scatter_dimension=1,
            tiled=True,
        ).astype(jnp.float32),
    )
    key_full = key_sum[0]
    value_full = value_sum[0]
    query_rows = query_full.reshape(tok_rows, feat_width)
    local_sums = jnp.stack(
        [
            head_squares(query_rows, head_count),
            head_squares(key_full, head_count),
            head_squares(value_full, head_count),
        ],
        axis=-1,
    )
    total_sums = lax.psum(local_sums, "seq")
    grad_features = jnp.log(total_sums / (seq_count * tok_rows * HD) + 1e-06)
    return (
        query_rows.astype(jnp.bfloat16)[None],
        key_full.astype(jnp.bfloat16)[None],
        value_full.astype(jnp.bfloat16)[None],
        grad_features[None],
    )


def per_device(*args):
    parts, sides = lax.axis_size("seq"), lax.axis_size("head")
    head_count = args[0].shape[2] // HD
    if head_count >= parts > 1 and head_count % 2 == 0 and sides == 2:
        return by_heads(*args)
    return by_gather(*args)


def solution(mesh):
    in_specs = (
        P(("grp", "clip"), "seq", "head"),
        P(("grp", "clip"), "seq", "head"),
        P(("grp", "clip"), "seq", "head"),
        P(("grp", "clip"), "seq", "head"),
        P("head", None),
        P(("grp", "clip"), None, None),
        P(("grp", "clip"), None),
    )
    out_specs = (
        P(("grp", "clip"), "seq", "head"),
        P(("grp", "clip"), "seq", "head"),
        P(("grp", "clip"), "seq", "head"),
        P(("grp", "clip"), "head", None),
    )
    return jax.shard_map(
        per_device, mesh=mesh, in_specs=in_specs, out_specs=out_specs, check_vma=False
    )
```
